256 devices in a mesh: ctx: 32 (over z, y_lo, core), head: 8 (over x, y_hi).
Axes of the slice: x: 4, y: 4 (y_hi: 2, y_lo: 2; y = y_hi * 2 + y_lo), z: 8, core: 2. Of those that a mesh axis runs over, the one named last changes fastest.
Arguments:
- hidden: bfloat16 [4096, 8192], P('ctx', 'head'), may hold values from -6 to 6
- query: bfloat16 [4096, 8192], P('ctx', 'head'), may hold values from -60 to 60
- fresh_key_value: bfloat16 [2, 4096, 1024], P(None, 'ctx', 'head'), may hold values from -6 to 6
- cached_key_value: bfloat16 [2, 8192, 1024], P(None, 'ctx', 'head'), may hold values from -6 to 6
- positions: int32 [3, 4096], P(None, 'ctx'), may hold values from 0 to 4095
- out_weight: bfloat16 [8192, 8192], P('head', 'ctx'), may hold values from -0.0625 to 0.0625
- norm_gain: float32 [8192], P('head'), may hold values from 0.25 to 1.75
- layer3_key_value_weight: bfloat16 [8192, 2048], P(None, 'head'), may hold values from -0.0625 to 0.0625
- layer3_key_value_bias: float32 [2048], P('head'), may hold values from -3 to 3
- keep_index: int32 [4096], P('ctx'), may hold values from 0 to 127, as said below
- keep_count: int32 [32], P('ctx'), may hold values from 64 to 128, as said below
Outputs:
- layer2_out: bfloat16 [4096, 8192], P('ctx', 'head')
- layer3_packed_key_value: bfloat16 [4096, 2048], P('ctx', 'head')
The draws below stay inside these ranges and needn't reach their ends.
Inputs may be any that keep to these rules, and one draw needn't show every extreme that they name: `keep_index`: within each block of 128 entries, the first keep_count entries are the kept rows in rising order (all text rows and every second visual row), the rest the dropped rows in rising order. `keep_count`: some block keeps all 128 rows in every draw.
All inputs are finite; a program needn't handle non-finite values.
Results may differ from the reference program's by a relative error of at most 0.012.
Values may be sent and summed in bfloat16 or wider, within the bound.
No kernel may reach another device: no remote copies, remote signals or barrier semaphores. Data moves between devices by JAX's collectives and lax.ppermute only.
A program may use at most 192 MiB of HBM per device.

```python
import jax
import jax.numpy as jnp
from jax import lax

MODEL_WIDTH = 8192
QUERY_HEADS = 64
KEY_VALUE_HEADS = 8
HEAD_DIMENSION = 128
FRESH_TOKENS = 128
FRESH_TOTAL = 4096
CACHED_TOKENS = 8192


def keep_tables(key):
    block_list = FRESH_TOTAL // FRESH_TOKENS
    first_key, second_key, third_key = jax.random.split(jax.random.fold_in(key, 71), 3)
    visual_share = jax.random.randint(first_key, (block_list, 1), 0, FRESH_TOKENS + 1)
    visual = jax.random.randint(second_key, (block_list, FRESH_TOKENS), 0, FRESH_TOKENS) < visual_share
    chosen_block = jax.random.randint(third_key, (), 0, block_list)
    visual = visual & (jnp.arange(block_list)[:, None] != chosen_block)
    visual_rank = jnp.cumsum(visual.astype(jnp.int32), axis=1) - 1
    dropped = visual & (visual_rank % 2 == 1)
    sort_keys = dropped.astype(jnp.int32) * FRESH_TOKENS + jnp.arange(FRESH_TOKENS, dtype=jnp.int32)[None, :]
    kept_order = jnp.argsort(sort_keys, axis=1, stable=True).astype(jnp.int32)
    kept_count = (FRESH_TOKENS - jnp.sum(dropped.astype(jnp.int32), axis=1)).astype(jnp.int32)
    return (kept_order.reshape(-1), kept_count)


def draw_keep_index(key, part):
    return keep_tables(key)[0]


def draw_keep_count(key, part):
    return keep_tables(key)[1]


def draw_query(key, part):
    first_key = jax.random.fold_in(jax.random.fold_in(key, 13), 0)
    shape = (FRESH_TOTAL, QUERY_HEADS * HEAD_DIMENSION)
    values = jax.random.normal(first_key, shape, jnp.float32)
    return jnp.clip(values, -60.0, 60.0).astype(jnp.bfloat16)


def set_ends(result, key, least, top_value):
    extent = result.shape
    spot = [jax.random.randint(jax.random.fold_in(key, axis), (), 0, extent[axis]) for axis in range(len(extent))]
    result = result.at[tuple(spot)].set(least)
    longest = extent.index(max(extent))
    spot[longest] = (spot[longest] + 1) % extent[longest]
    return result.at[tuple(spot)].set(top_value)


def block_scale(key, shape, pieces, low, high):
    level, own = 1.0, jax.random.fold_in(key, 6)
    for dim, shards_of in pieces:
        steps = jnp.exp(jax.random.uniform(jax.random.fold_in(own, dim), (shards_of,), jnp.float32, low / len(pieces), high / len(pieces)))
        level = level * jnp.repeat(steps, shape[dim] // shards_of).reshape([-1 if axis == dim else 1 for axis in range(len(shape))])
    return level


def normal_values(key, extent, deviation, bound, cuts=(), kind=jnp.bfloat16):
    values = deviation * jax.random.normal(key, extent, jnp.float32)
    if cuts:
        values = values * block_scale(key, extent, cuts, -0.22, 0.18)
    return jnp.clip(values, -bound, bound).astype(kind)


def setup_inputs(seed: int = 0) -> dict:
    streams_of = jax.random.split(jax.random.key(seed), 12)
    return {
        "hidden": normal_values(streams_of[0], (FRESH_TOTAL, MODEL_WIDTH), 1.0, 6.0, ((0, 32), (1, 8))),
        "query": draw_query(jax.random.fold_in(streams_of[11], 71), 0),
        "fresh_key_value": normal_values(streams_of[2], (2, FRESH_TOTAL, KEY_VALUE_HEADS * HEAD_DIMENSION), 1.0, 6.0, ((1, 32), (2, 8))),
        "cached_key_value": normal_values(streams_of[3], (2, CACHED_TOKENS, KEY_VALUE_HEADS * HEAD_DIMENSION), 1.0, 6.0, ((1, 32), (2, 8))),
        "positions": set_ends(jax.random.randint(streams_of[4], (3, FRESH_TOTAL), 0, 4096), jax.random.fold_in(streams_of[4], 1), 0, 4095).astype(jnp.int32),
        "out_weight": normal_values(streams_of[5], (QUERY_HEADS * HEAD_DIMENSION, MODEL_WIDTH), (QUERY_HEADS * HEAD_DIMENSION) ** -0.5, 0.0625, ((0, 8), (1, 32))),
        "norm_gain": jnp.clip(1.0 + 0.15 * jax.random.normal(streams_of[6], (MODEL_WIDTH,), jnp.float32), 0.25, 1.75),
        "layer3_key_value_weight": normal_values(streams_of[7], (MODEL_WIDTH, 2 * KEY_VALUE_HEADS * HEAD_DIMENSION), MODEL_WIDTH ** -0.5, 0.0625, ((1, 8),)),
        "layer3_key_value_bias": normal_values(streams_of[8], (2 * KEY_VALUE_HEADS * HEAD_DIMENSION,), 0.5, 3.0, ((0, 8),), jnp.float32),
        "keep_index": draw_keep_index(jax.random.fold_in(streams_of[11], 71), 0),
        "keep_count": draw_keep_count(jax.random.fold_in(streams_of[11], 71), 0),
    }


def tables(positions, head_size):
    half = head_size // 2
    column = jnp.arange(half)
    frequency = jnp.power(jnp.float32(1000000.0), -(2.0 * column.astype(jnp.float32)) / head_size)
    section = (column >= head_size // 8).astype(jnp.int32) + (column >= head_size // 8 + 3 * head_size // 16).astype(jnp.int32)
    places = positions.astype(jnp.float32)
    chosen = jnp.where(section[None, :] == 0, places[0][:, None], jnp.where(section[None, :] == 1, places[1][:, None], places[2][:, None]))
    angles = chosen * frequency[None, :]
    return (jnp.cos(angles), jnp.sin(angles))

def apply_rotary(x, cosine_table, sine_table):
    half = x.shape[-1] // 2
    first_half = x[..., :half]
    second_half = x[..., half:]
    cosine_table = cosine_table[:, None, :]
    sine_table = sine_table[:, None, :]
    return jnp.concatenate([first_half * cosine_table - second_half * sine_table, second_half * cosine_table + first_half * sine_table], axis=-1)

def reference(hidden, query, fresh_key_value, cached_key_value, positions, out_weight, norm_gain, layer3_key_value_weight, layer3_key_value_bias, keep_index, keep_count):
    fresh_token_count = hidden.shape[0]
    block_list = fresh_token_count // FRESH_TOKENS
    query_group_width = QUERY_HEADS // KEY_VALUE_HEADS
    cosine_table, sine_table = tables(positions, HEAD_DIMENSION)
    rotary_query_rows = apply_rotary(query.astype(jnp.float32).reshape(fresh_token_count, QUERY_HEADS, HEAD_DIMENSION), cosine_table, sine_table).astype(jnp.bfloat16)
    rotary_key_rows = apply_rotary(fresh_key_value[0].astype(jnp.float32).reshape(fresh_token_count, KEY_VALUE_HEADS, HEAD_DIMENSION), cosine_table, sine_table).astype(jnp.bfloat16)
    key_matrix_rows = jnp.concatenate([cached_key_value[0].reshape(CACHED_TOKENS, KEY_VALUE_HEADS, HEAD_DIMENSION), rotary_key_rows], axis=0).transpose(1, 0, 2)
    value_matrix_rows = jnp.concatenate([cached_key_value[1].reshape(CACHED_TOKENS, KEY_VALUE_HEADS, HEAD_DIMENSION), fresh_key_value[1].reshape(fresh_token_count, KEY_VALUE_HEADS, HEAD_DIMENSION)], axis=0).transpose(1, 0, 2)
    grouped_rows = rotary_query_rows.reshape(block_list, FRESH_TOKENS, KEY_VALUE_HEADS, query_group_width, HEAD_DIMENSION).transpose(0, 2, 1, 3, 4)

    def per_block(inputs):
        query_block, block_number = inputs
        query_pos = block_number * FRESH_TOKENS + jnp.arange(FRESH_TOKENS)
        recent = jnp.arange(fresh_token_count)[None, :] <= query_pos[:, None]
        visible = jnp.concatenate([jnp.ones((FRESH_TOKENS, CACHED_TOKENS), bool), recent], axis=1)

        def per_head(head_inputs):
            query_head, key_head, value_head = head_inputs
            scores = jnp.einsum('ngd,ld->ngl', query_head.astype(jnp.float32), key_head.astype(jnp.float32)) * HEAD_DIMENSION ** (-0.5)
            scores = jnp.where(visible[:, None, :], scores, -jnp.inf)
            maxima = lax.optimization_barrier(jnp.max(scores, axis=-1, keepdims=True))
            expos = jnp.exp(scores - maxima)
            totals = lax.optimization_barrier(jnp.sum(expos, axis=-1))
            weights = expos.astype(jnp.bfloat16)
            summed = jnp.einsum('ngl,ld->ngd', weights.astype(jnp.float32), value_head.astype(jnp.float32))
            return summed / totals[..., None]
        return lax.map(per_head, (query_block, key_matrix_rows, value_matrix_rows))
    outputs = lax.map(per_block, (grouped_rows, jnp.arange(block_list)))
    attn = outputs.transpose(0, 2, 1, 3, 4).reshape(fresh_token_count, QUERY_HEADS * HEAD_DIMENSION).astype(jnp.bfloat16)
    projection = jnp.dot(attn, out_weight, preferred_element_type=jnp.float32)
    layer2_out = (hidden.astype(jnp.float32) + projection).astype(jnp.bfloat16)
    widened = layer2_out.astype(jnp.float32)
    mean_square = lax.optimization_barrier(jnp.mean(widened * widened, axis=1))
    normalized_rows = (widened * lax.rsqrt(mean_square + 1e-06)[:, None] * norm_gain).astype(jnp.bfloat16)
    layer_three_key_value = (jnp.dot(normalized_rows, layer3_key_value_weight, preferred_element_type=jnp.float32) + layer3_key_value_bias).reshape(fresh_token_count, KEY_VALUE_HEADS, 2, HEAD_DIMENSION)
    layer_three_keys = apply_rotary(layer_three_key_value[:, :, 0], cosine_table, sine_table)
    layer_three_key_value = jnp.stack([layer_three_keys, layer_three_key_value[:, :, 1]], axis=2).reshape(fresh_token_count, 2 * KEY_VALUE_HEADS * HEAD_DIMENSION).astype(jnp.bfloat16)
    grouped_by_block = layer_three_key_value.reshape(block_list, FRESH_TOKENS, 2 * KEY_VALUE_HEADS * HEAD_DIMENSION)
    indices = keep_index.reshape(block_list, FRESH_TOKENS).astype(jnp.int32)
    selected_rows = jnp.take_along_axis(grouped_by_block, indices[:, :, None], axis=1)
    block_occupied = jnp.arange(FRESH_TOKENS)[None, :] < keep_count[:, None]
    layer3_packed_key_value = jnp.where(block_occupied[:, :, None], selected_rows, jnp.zeros_like(selected_rows)).reshape(fresh_token_count, 2 * KEY_VALUE_HEADS * HEAD_DIMENSION)
    return (layer2_out, layer3_packed_key_value)
```

```python
import functools

import jax
import jax.numpy as jnp
from jax import lax
from jax.experimental import pallas as pl
from jax.experimental.pallas import tpu as pltpu
from jax.sharding import Mesh
from jax.sharding import PartitionSpec as P

MODEL_WIDTH = 8192
HEAD = 128
ROWS = 128
CACHED = 256
GROUP = 8
Z = 8
LOG2E = 1.4426950408889634
SCALE = HEAD ** (-0.5) * LOG2E
CTX_AXES = ("z", "yl", "c")
HEAD_AXES = ("x", "yh")
VMEM = 56 * 1024 * 1024
CHUNK = 256
KEY_STEP = 1024


def params(**more):
    return pltpu.CompilerParams(vmem_limit_bytes=VMEM, **more)


def tables(positions, head_size):
    half = head_size // 2
    column = jnp.arange(half)
    frequency = jnp.power(jnp.float32(1000000.0), -(2.0 * column.astype(jnp.float32)) / head_size)
    section = (column >= head_size // 8).astype(jnp.int32) + (
        column >= head_size // 8 + 3 * head_size // 16
    ).astype(jnp.int32)
    places = positions.astype(jnp.float32)
    chosen = jnp.where(
        section[None, :] == 0,
        places[0][:, None],
        jnp.where(section[None, :] == 1, places[1][:, None], places[2][:, None]),
    )
    angles = chosen * frequency[None, :]
    cosine, sine = jnp.cos(angles), jnp.sin(angles)
    return (
        jnp.concatenate([cosine, cosine], axis=1),
        jnp.concatenate([-sine, sine], axis=1),
    )


def rotated(x, cosine, sine):
    return x * cosine + pltpu.roll(x, HEAD // 2, 1) * sine


def prepare_kernel(query, fresh, cached, cosine, sine, query_out, kv_out):
    cos, sin = cosine[...], sine[...]
    for g in range(GROUP):
        piece = query[:, g * HEAD : (g + 1) * HEAD].astype(jnp.float32)
        query_out[g] = rotated(piece, cos, sin).astype(jnp.bfloat16)
    kv_out[:, :CACHED, :] = cached[...]
    kv_out[0, CACHED:, :] = rotated(fresh[0].astype(jnp.float32), cos, sin).astype(jnp.bfloat16)
    kv_out[1, CACHED:, :] = fresh[1]


def prepare(query, fresh, cached, cosine, sine):
    return pl.pallas_call(
        prepare_kernel,
        out_shape=(
            jax.ShapeDtypeStruct((GROUP, ROWS, HEAD), jnp.bfloat16),
            jax.ShapeDtypeStruct((2, CACHED + ROWS, HEAD), jnp.bfloat16),
        ),
        compiler_params=params(),
        name="prepare",
        cost_estimate=pl.CostEstimate(flops=2_000_000, bytes_accessed=1_500_000, transcendentals=0),
    )(query, fresh, cached, cosine, sine)


def column_of(row):
    return jnp.transpose(jnp.broadcast_to(row, (ROWS, ROWS)))


def row_of(column):
    return jnp.transpose(column)[0:1, :]


def attend_kernel(place, query, *refs):
    kv = refs[:Z]
    out, lse_out, keys, values, key_token = refs[Z:]
    step = pl.program_id(0)
    z, yl, c, rc = place[0], place[1], place[2], place[3]

    @pl.when(step == 0)
    def _():
        lane = lax.broadcasted_iota(jnp.int32, (8, ROWS), 1)
        for d in range(Z):
            block = kv[d]
            keys[:, d * CACHED : (d + 1) * CACHED] = jnp.transpose(block[0, :CACHED, :])
            at = Z * CACHED + d * ROWS
            keys[:, at : at + ROWS] = jnp.transpose(block[0, CACHED:, :])
            values[d * CACHED : (d + 1) * CACHED, :HEAD] = block[1, :CACHED, :]
            values[at : at + ROWS, :HEAD] = block[1, CACHED:, :]
            source = lax.rem(z - d + Z, Z)
            key_token[:, d * ROWS : (d + 1) * ROWS] = (
                source * 4 + yl * 2 + c
            ) * ROWS + lane
        values[:, HEAD:] = jnp.ones((Z * (CACHED + ROWS), HEAD), jnp.bfloat16)

    per_block = GROUP * ROWS // CHUNK
    ryl = step // per_block
    block = z * 4 + (yl ^ ryl) * 2 + (c ^ rc)
    inside = lax.broadcasted_iota(jnp.int32, (CHUNK, 1), 0) & (ROWS - 1)
    query_token = block * ROWS + inside
    q = query[...]
    m = jnp.full((CHUNK, 1), -1e30, jnp.float32)
    acc = jnp.zeros((CHUNK, 2 * HEAD), jnp.float32)
    for at in range(0, Z * (CACHED + ROWS), KEY_STEP):
        scores = jnp.dot(q, keys[:, at : at + KEY_STEP], preferred_element_type=jnp.float32)
        if at >= Z * CACHED:
            first = at - Z * CACHED
            visible = key_token[0:1, first : first + KEY_STEP] <= query_token
            scores = jnp.where(visible, scores, -1e30)
        raised = jnp.maximum(m, jnp.max(scores, axis=1, keepdims=True))
        weights = jnp.exp2((scores - raised) * SCALE).astype(jnp.bfloat16)
        factor = jnp.exp2((m - raised) * SCALE)
        acc = acc * factor + jnp.dot(
            weights, values[at : at + KEY_STEP, :], preferred_element_type=jnp.float32
        )
        m = raised
    totals = acc[:, HEAD:]
    out[...] = (acc[:, :HEAD] / totals).astype(jnp.bfloat16)
    lse = m * SCALE + jnp.log2(totals)
    for k in range(CHUNK // ROWS):
        lse_out[step * (CHUNK // ROWS) + k] = row_of(lse[k * ROWS : (k + 1) * ROWS, :])


def attend(place, query, kv):
    rows = query.shape[0]
    total = Z * (CACHED + ROWS)
    whole = pl.BlockSpec((2, CACHED + ROWS, HEAD), lambda i, s: (0, 0, 0))
    return pl.pallas_call(
        attend_kernel,
        grid_spec=pltpu.PrefetchScalarGridSpec(
            num_scalar_prefetch=1,
            grid=(rows // CHUNK,),
            in_specs=[pl.BlockSpec((CHUNK, HEAD), lambda i, s: (i, 0))] + [whole] * Z,
            out_specs=[
                pl.BlockSpec((CHUNK, HEAD), lambda i, s: (i, 0)),
                pl.BlockSpec((rows // ROWS, 1, ROWS), lambda i, s: (0, 0, 0)),
            ],
            scratch_shapes=[
                pltpu.VMEM((HEAD, total), jnp.bfloat16),
                pltpu.VMEM((total, 2 * HEAD), jnp.bfloat16),
                pltpu.VMEM((8, Z * ROWS), jnp.int32),
            ],
        ),
        out_shape=(
            jax.ShapeDtypeStruct((rows, HEAD), jnp.bfloat16),
            jax.ShapeDtypeStruct((rows // ROWS, 1, ROWS), jnp.float32),
        ),
        compiler_params=params(),
        name="attend",
        cost_estimate=pl.CostEstimate(
            flops=4 * rows * total * HEAD,
            bytes_accessed=4 * rows * HEAD + 4 * total * HEAD,
            transcendentals=rows * total,
        ),
    )(place, query, *kv)


def merged(first, second, first_lse, second_lse):
    a, b = column_of(first_lse), column_of(second_lse)
    top = jnp.maximum(a, b)
    wa, wb = jnp.exp2(a - top), jnp.exp2(b - top)
    total = wa + wb
    value = (first.astype(jnp.float32) * wa + second.astype(jnp.float32) * wb) / total
    return value.astype(jnp.bfloat16), top + jnp.log2(total)


def merge_kernel(own, own_lse, other, other_lse, out, lse_out):
    for k in range(own.shape[0] // ROWS):
        at = slice(k * ROWS, (k + 1) * ROWS)
        value, lse = merged(own[at, :], other[at, :], own_lse[k], other_lse[k])
        out[at, :] = value
        lse_out[k] = row_of(lse)


def merge_last_kernel(own, own_lse, other, other_lse, out):
    for y in range(2):
        for g in range(GROUP):
            k, j = y * GROUP + g, (1 - y) * GROUP + g
            value, _ = merged(
                own[k * ROWS : (k + 1) * ROWS, :],
                other[j * ROWS : (j + 1) * ROWS, :],
                own_lse[k],
                other_lse[j],
            )
            out[y, :, g * HEAD : (g + 1) * HEAD] = value


def merge(own, own_lse, other, other_lse):
    return pl.pallas_call(
        merge_kernel,
        out_shape=(
            jax.ShapeDtypeStruct(own.shape, own.dtype),
            jax.ShapeDtypeStruct(own_lse.shape, own_lse.dtype),
        ),
        compiler_params=params(),
        name="merge",
    )(own, own_lse, other, other_lse)


def merge_last(own, own_lse, other, other_lse):
    return pl.pallas_call(
        merge_last_kernel,
        out_shape=jax.ShapeDtypeStruct((2, ROWS, GROUP * HEAD), jnp.bfloat16),
        compiler_params=params(),
        name="merge_last",
    )(own, own_lse, other, other_lse)


def project_kernel(place, near, far, weight, out):
    yl, c = place[1], place[2]
    for rc, rows in ((0, near), (1, far)):
        for ryl in range(2):
            q = (yl ^ ryl) * 2 + (c ^ rc)
            out[q, 0] = jnp.dot(
                rows[ryl], weight[0], preferred_element_type=jnp.float32
            ).astype(jnp.bfloat16)


def project(place, near, far, weight):
    width = GROUP * HEAD
    columns = weight.shape[2]
    return pl.pallas_call(
        project_kernel,
        grid_spec=pltpu.PrefetchScalarGridSpec(
            num_scalar_prefetch=1,
            grid=(Z,),
            in_specs=[
                pl.BlockSpec((2, ROWS, width), lambda i, s: (0, 0, 0)),
                pl.BlockSpec((2, ROWS, width), lambda i, s: (0, 0, 0)),
                pl.BlockSpec((1, width, columns), lambda i, s: (i, 0, 0)),
            ],
            out_specs=pl.BlockSpec((4, 1, ROWS, columns), lambda i, s: (0, i, 0, 0)),
        ),
        out_shape=jax.ShapeDtypeStruct((4, Z, ROWS, columns), jnp.bfloat16),
        compiler_params=params(),
        name="project",
    )(place, near, far, weight)


PAD = 16


def third_kernel(place, received, hidden, gain, near, far, out, partial, scaled):
    c = place[2]
    columns = received.shape[3]
    squares = jnp.zeros((ROWS, 1), jnp.float32)
    for q in range(4):
        at = slice(q * columns, (q + 1) * columns)
        total = received[q, 0].astype(jnp.float32)
        for h in range(1, Z):
            total = total + received[q, h].astype(jnp.float32)
        result = (hidden[:, at].astype(jnp.float32) + total).astype(jnp.bfloat16)
        out[:, at] = result
        wide = result.astype(jnp.float32)
        squares = squares + jnp.sum(wide * wide, axis=1, keepdims=True)
        scaled[q // 2, :, (q % 2) * columns : (q % 2 + 1) * columns] = (
            wide * gain[:, at]
        ).astype(jnp.bfloat16)
    row = row_of(jnp.broadcast_to(squares, (ROWS, ROWS)))
    high = row.astype(jnp.bfloat16)
    low = (row - high.astype(jnp.float32)).astype(jnp.bfloat16)
    tail = jnp.broadcast_to(
        jnp.concatenate([high, low], axis=1).astype(jnp.float32), (PAD, 2 * ROWS)
    ).astype(jnp.bfloat16)
    near_rows, far_rows = scaled[c], scaled[1 - c]
    for h in range(Z):
        product = jnp.dot(near_rows, near[h], preferred_element_type=jnp.float32) + jnp.dot(
            far_rows, far[h], preferred_element_type=jnp.float32
        )
        partial[h, :ROWS, :] = product.astype(jnp.bfloat16)
        partial[h, ROWS:, :] = tail


def third_partials(place, received, hidden, gain, near, far):
    vmem = pl.BlockSpec(memory_space=pltpu.VMEM)
    width = hidden.shape[1]
    return pl.pallas_call(
        third_kernel,
        in_specs=[pl.BlockSpec(memory_space=pltpu.SMEM)] + [vmem] * 5,
        out_specs=(vmem, vmem),
        out_shape=(
            jax.ShapeDtypeStruct(hidden.shape, jnp.bfloat16),
            jax.ShapeDtypeStruct((Z, ROWS + PAD, 2 * HEAD), jnp.bfloat16),
        ),
        scratch_shapes=[pltpu.VMEM((2, ROWS, width // 2), jnp.bfloat16)],
        compiler_params=params(),
        name="third",
    )(place, received, hidden, gain, near, far)


def final_kernel(count, partial, bias, cosine, sine, index, out):
    total = partial[0, :ROWS, :].astype(jnp.float32)
    tail = partial[0, ROWS:, :].astype(jnp.float32)
    for h in range(1, Z):
        total = total + partial[h, :ROWS, :].astype(jnp.float32)
        tail = tail + partial[h, ROWS:, :].astype(jnp.float32)
    squares = tail[0:1, :ROWS] + tail[0:1, ROWS:]
    factor = lax.rsqrt(column_of(squares) / MODEL_WIDTH + 1e-06)
    keys = total[:, :HEAD] * factor + bias[:, :HEAD]
    values = total[:, HEAD:] * factor + bias[:, HEAD:]
    keys = rotated(keys, cosine[...], sine[...])
    rows = jnp.concatenate([keys, values], axis=1).astype(jnp.bfloat16)
    slot = lax.broadcasted_iota(jnp.int32, (ROWS, ROWS), 1)
    token = lax.broadcasted_iota(jnp.int32, (ROWS, ROWS), 0)
    chosen = (token == index[...]) & (slot < count[0])
    pick = jnp.where(chosen, 1.0, 0.0).astype(jnp.bfloat16)
    out[...] = lax.dot_general(
        pick, rows, (((0,), (0,)), ((), ())), preferred_element_type=jnp.float32
    ).astype(jnp.bfloat16)


def final(count, partial, bias, cosine, sine, index):
    vmem = pl.BlockSpec(memory_space=pltpu.VMEM)
    return pl.pallas_call(
        final_kernel,
        in_specs=[pl.BlockSpec(memory_space=pltpu.SMEM)] + [vmem] * 5,
        out_specs=vmem,
        out_shape=jax.ShapeDtypeStruct((ROWS, 2 * HEAD), jnp.bfloat16),
        compiler_params=params(),
        name="final",
    )(count, partial, bias, cosine, sine, index)


def swap(x, axis):
    return lax.ppermute(x, axis, [(0, 1), (1, 0)])


def along_z(x, distance):
    return lax.ppermute(x, "z", [(i, (i + distance) % Z) for i in range(Z)])


def local(
    hidden,
    query,
    fresh_key_value,
    cached_key_value,
    positions,
    out_weight,
    norm_gain,
    layer3_key_value_weight,
    layer3_key_value_bias,
    keep_index,
    keep_count,
):
    z, yl, c = lax.axis_index("z"), lax.axis_index("yl"), lax.axis_index("c")
    place = jnp.stack([z, yl, c, jnp.zeros_like(c)]).astype(jnp.int32)
    far_place = jnp.stack([z, yl, c, jnp.ones_like(c)]).astype(jnp.int32)

    cosine, sine = tables(positions, HEAD)
    rotated_query, kv = prepare(query, fresh_key_value, cached_key_value, cosine, sine)
    pieces = [kv] + [along_z(kv, d) for d in range(1, Z)]
    rotated_query = rotated_query.reshape(GROUP * ROWS, HEAD)
    near_query = jnp.concatenate([rotated_query, swap(rotated_query, "yl")], axis=0)
    far_query = swap(near_query, "c")
    weight = lax.all_gather(out_weight, "z")

    third_rows = layer3_key_value_weight.reshape(Z, 2, MODEL_WIDTH // Z // 2, 2 * HEAD)
    third_rows = lax.dynamic_index_in_dim(third_rows, c, axis=1, keepdims=False)
    third_near = lax.all_to_all(third_rows, HEAD_AXES, 0, 0, tiled=True)
    third_far = swap(third_near, "c")

    send, send_lse = attend(far_place, far_query, pieces)
    got, got_lse = swap(send, "c"), swap(send_lse, "c")
    own, own_lse = attend(place, near_query, pieces)
    own, own_lse = merge(own, own_lse, got, got_lse)
    got, got_lse = swap(own, "yl"), swap(own_lse, "yl")
    near = merge_last(own, own_lse, got, got_lse)
    far = swap(near, "c")

    products = project(place, near, far, weight)
    products = products.reshape(4 * Z, *products.shape[2:])
    received = lax.all_to_all(products, ("yl", "c", "x", "yh"), 0, 0, tiled=True)
    received = received.reshape(4, Z, *received.shape[1:])

    layer2_out, partial = third_partials(
        place, received, hidden, norm_gain.reshape(1, -1), third_near, third_far
    )
    partial = lax.all_to_all(partial, HEAD_AXES, 0, 0, tiled=True)
    packed = final(
        keep_count,
        partial,
        layer3_key_value_bias.reshape(1, -1),
        cosine,
        sine,
        keep_index.reshape(1, -1),
    )
    return (layer2_out, packed)


def solution(mesh):
    split = Mesh(mesh.devices.reshape(Z, 2, 2, 4, 2), CTX_AXES + HEAD_AXES)
    placed = (
        P(CTX_AXES, HEAD_AXES),
        P(CTX_AXES, HEAD_AXES),
        P(None, CTX_AXES, HEAD_AXES),
        P(None, CTX_AXES, HEAD_AXES),
        P(None, CTX_AXES),
        P(HEAD_AXES, CTX_AXES),
        P(HEAD_AXES),
        P(None, HEAD_AXES),
        P(HEAD_AXES),
        P(CTX_AXES),
        P(CTX_AXES),
    )
    return jax.shard_map(
        local,
        mesh=split,
        in_specs=placed,
        out_specs=(P(CTX_AXES, HEAD_AXES), P(CTX_AXES, HEAD_AXES)),
        check_vma=False,
    )
```

```python
import functools

import jax
import jax.numpy as jnp
from jax import lax
from jax.experimental import pallas as pl
from jax.experimental.pallas import tpu as pltpu
from jax.sharding import Mesh
from jax.sharding import PartitionSpec as P

MODEL_WIDTH = 8192
HEAD = 128
ROWS = 128
CACHED = 256
GROUP = 8
Z = 8
LOG2E = 1.4426950408889634
SCALE = HEAD ** (-0.5) * LOG2E
CTX_AXES = ("z", "yl", "c")
HEAD_AXES = ("x", "yh")
VMEM = 56 * 1024 * 1024
CHUNK = 512
BLOCKS = 3
DISTANCES = (0, -1, 1, -2, 2, -3, 3, 4)


def params(**more):
    return pltpu.CompilerParams(vmem_limit_bytes=VMEM, **more)


def tables(positions, head_size):
    half = head_size // 2
    column = jnp.arange(half)
    frequency = jnp.power(jnp.float32(1000000.0), -(2.0 * column.astype(jnp.float32)) / head_size)
    section = (column >= head_size // 8).astype(jnp.int32) + (
        column >= head_size // 8 + 3 * head_size // 16
    ).astype(jnp.int32)
    places = positions.astype(jnp.float32)
    chosen = jnp.where(
        section[None, :] == 0,
        places[0][:, None],
        jnp.where(section[None, :] == 1, places[1][:, None], places[2][:, None]),
    )
    angles = chosen * frequency[None, :]
    cosine, sine = jnp.cos(angles), jnp.sin(angles)
    return (
        jnp.concatenate([cosine, cosine], axis=1),
        jnp.concatenate([-sine, sine], axis=1),
    )


def rotated(x, cosine, sine):
    return x * cosine + pltpu.roll(x, HEAD // 2, 1) * sine


def prepare_kernel(query, fresh, cached, cosine, sine, query_out, kv_out):
    cos, sin = cosine[...], sine[...]
    for g in range(GROUP):
        piece = query[:, g * HEAD : (g + 1) * HEAD].astype(jnp.float32)
        query_out[g] = rotated(piece, cos, sin).astype(jnp.bfloat16)
    for k in range(CACHED // ROWS):
        kv_out[k] = jnp.transpose(cached[0, k * ROWS : (k + 1) * ROWS, :])
        kv_out[BLOCKS + k] = cached[1, k * ROWS : (k + 1) * ROWS, :]
    new_key = rotated(fresh[0].astype(jnp.float32), cos, sin).astype(jnp.bfloat16)
    kv_out[BLOCKS - 1] = jnp.transpose(new_key)
    kv_out[2 * BLOCKS - 1] = fresh[1]


def prepare(query, fresh, cached, cosine, sine):
    return pl.pallas_call(
        prepare_kernel,
        out_shape=(
            jax.ShapeDtypeStruct((GROUP, ROWS, HEAD), jnp.bfloat16),
            jax.ShapeDtypeStruct((2 * BLOCKS, ROWS, HEAD), jnp.bfloat16),
        ),
        compiler_params=params(),
        name="prepare",
        cost_estimate=pl.CostEstimate(flops=2_000_000, bytes_accessed=1_500_000, transcendentals=0),
    )(query, fresh, cached, cosine, sine)


def column_of(row):
    return jnp.transpose(jnp.broadcast_to(row, (ROWS, ROWS)))


def row_of(column):
    return jnp.transpose(column)[0:1, :]


def attend_kernel(cached, fresh, first, last, rc, place, query, *refs):
    n_in = 1 + max([max(k, v) for k, v in cached] + [max(p[0], p[1]) for pair in fresh for p in pair])
    pieces, rest = refs[:n_in], list(refs[n_in:])
    if not first:
        acc_in, m_in = rest[:2]
        rest = rest[2:]
    if last:
        out, lse_out = rest[:2]
    else:
        acc_out, m_out = rest[:2]
    keys, values = rest[2:]
    step = pl.program_id(0)
    z, yl, c = place[0], place[1], place[2]
    steps = len(cached) + len(fresh)

    def value_block(ref, k):
        return ref[BLOCKS + k] if ref.shape[0] == 2 * BLOCKS else ref[k]

    @pl.when(step == 0)
    def _():
        at = 0
        for kp, vp in cached:
            for k in range(2):
                keys[:, at : at + ROWS] = pieces[kp][k]
                values[at : at + ROWS, :HEAD] = value_block(pieces[vp], k)
                at += ROWS
        for pair in fresh:
            for kp, vp, _ in pair:
                keys[:, at : at + ROWS] = pieces[kp][BLOCKS - 1]
                values[at : at + ROWS, :HEAD] = value_block(pieces[vp], BLOCKS - 1)
                at += ROWS
        values[:, HEAD:] = jnp.ones((steps * 2 * ROWS, HEAD), jnp.bfloat16)

    per_block = GROUP * ROWS // CHUNK
    ryl = step // per_block
    block = z * 4 + (yl ^ ryl) * 2 + (c ^ rc)
    inside = lax.broadcasted_iota(jnp.int32, (CHUNK, 1), 0) & (ROWS - 1)
    query_token = block * ROWS + inside
    lane = lax.broadcasted_iota(jnp.int32, (1, 2 * ROWS), 1)
    q = query[...]
    if first:
        m = jnp.full((CHUNK, 1), -1e30, jnp.float32)
        acc = jnp.zeros((CHUNK, 2 * HEAD), jnp.float32)
    else:
        m = m_in[:, 0:1]
        acc = acc_in[...]
    for i in range(steps):
        at = slice(i * 2 * ROWS, (i + 1) * 2 * ROWS)
        scores = jnp.dot(q, keys[:, at], preferred_element_type=jnp.float32)
        if i >= len(cached):
            one, two = (
                (lax.rem(z + p[2] + Z, Z) * 4 + yl * 2 + c) * ROWS for p in fresh[i - len(cached)]
            )
            key_token = jnp.where(lane < ROWS, one + lane, two + lane - ROWS)
            scores = jnp.where(key_token <= query_token, scores, -1e30)
        raised = jnp.maximum(m, jnp.max(scores, axis=1, keepdims=True))
        weights = jnp.exp2((scores - raised) * SCALE).astype(jnp.bfloat16)
        factor = jnp.exp2((m - raised) * SCALE)
        acc = acc * factor + jnp.dot(weights, values[at, :], preferred_element_type=jnp.float32)
        m = raised
    if not last:
        acc_out[...] = acc
        m_out[...] = jnp.broadcast_to(m, (CHUNK, HEAD))
        return
    totals = acc[:, HEAD:]
    out[...] = (acc[:, :HEAD] / totals).astype(jnp.bfloat16)
    lse = m * SCALE + jnp.log2(totals)
    for k in range(CHUNK // ROWS):
        lse_out[step * (CHUNK // ROWS) + k] = row_of(lse[k * ROWS : (k + 1) * ROWS, :])


def attend(place, rc, query, pieces, cached, fresh, state=None, last=False):
    rows = query.shape[0]
    total = 2 * ROWS * (len(cached) + len(fresh))
    row_spec = pl.BlockSpec((CHUNK, HEAD), lambda i, s: (i, 0))
    wide_spec = pl.BlockSpec((CHUNK, 2 * HEAD), lambda i, s: (i, 0))
    in_specs = [row_spec] + [pl.BlockSpec(p.shape, lambda i, s: (0, 0, 0)) for p in pieces]
    args = [query, *pieces]
    if state is not None:
        in_specs += [wide_spec, row_spec]
        args += list(state)
    if last:
        out_specs = [row_spec, pl.BlockSpec((rows // ROWS, 1, ROWS), lambda i, s: (0, 0, 0))]
        out_shape = (
            jax.ShapeDtypeStruct((rows, HEAD), jnp.bfloat16),
            jax.ShapeDtypeStruct((rows // ROWS, 1, ROWS), jnp.float32),
        )
    else:
        out_specs = [wide_spec, row_spec]
        out_shape = (
            jax.ShapeDtypeStruct((rows, 2 * HEAD), jnp.float32),
            jax.ShapeDtypeStruct((rows, HEAD), jnp.float32),
        )
    return pl.pallas_call(
        functools.partial(attend_kernel, cached, fresh, state is None, last, rc),
        grid_spec=pltpu.PrefetchScalarGridSpec(
            num_scalar_prefetch=1,
            grid=(rows // CHUNK,),
            in_specs=in_specs,
            out_specs=out_specs,
            scratch_shapes=[
                pltpu.VMEM((HEAD, total), jnp.bfloat16),
                pltpu.VMEM((total, 2 * HEAD), jnp.bfloat16),
            ],
        ),
        out_shape=out_shape,
        compiler_params=params(),
        name="attend",
        cost_estimate=pl.CostEstimate(
            flops=4 * rows * total * HEAD,
            bytes_accessed=8 * rows * HEAD + 4 * total * HEAD,
            transcendentals=rows * total,
        ),
    )(place, *args)


def merge_weight(first_lse, second_lse):
    top = jnp.maximum(first_lse, second_lse)
    a, b = jnp.exp2(first_lse - top), jnp.exp2(second_lse - top)
    return a / (a + b), top + jnp.log2(a + b)


def merged(first, second, weight):
    a, b = first.astype(jnp.float32), second.astype(jnp.float32)
    share = column_of(weight)
    return (a * share + b * (1.0 - share)).astype(jnp.bfloat16)


def merge_kernel(own, own_lse, other, other_lse, out, lse_out):
    for k in range(own.shape[0] // ROWS):
        at = slice(k * ROWS, (k + 1) * ROWS)
        weight, lse = merge_weight(own_lse[k], other_lse[k])
        out[at, :] = merged(own[at, :], other[at, :], weight)
        lse_out[k] = lse


def merge_last_kernel(own, own_lse, other, other_lse, out):
    for y in range(2):
        for g in range(GROUP):
            k, j = y * GROUP + g, (1 - y) * GROUP + g
            weight, _ = merge_weight(own_lse[k], other_lse[j])
            out[y, :, g * HEAD : (g + 1) * HEAD] = merged(
                own[k * ROWS : (k + 1) * ROWS, :], other[j * ROWS : (j + 1) * ROWS, :], weight
            )


MERGE_COST = pl.CostEstimate(flops=2_000_000, bytes_accessed=1_600_000, transcendentals=4096)


def merge(own, own_lse, other, other_lse):
    return pl.pallas_call(
        merge_kernel,
        out_shape=(
            jax.ShapeDtypeStruct(own.shape, own.dtype),
            jax.ShapeDtypeStruct(own_lse.shape, own_lse.dtype),
        ),
        compiler_params=params(),
        name="merge",
        cost_estimate=MERGE_COST,
    )(own, own_lse, other, other_lse)


def merge_last(own, own_lse, other, other_lse):
    return pl.pallas_call(
        merge_last_kernel,
        out_shape=jax.ShapeDtypeStruct((2, ROWS, GROUP * HEAD), jnp.bfloat16),
        compiler_params=params(),
        name="merge_last",
        cost_estimate=MERGE_COST,
    )(own, own_lse, other, other_lse)


def project_kernel(place, near, far, *refs):
    weights, top, bottom, out = refs[:7], refs[7], refs[8], refs[9]
    z, yl, c = place[0], place[1], place[2]
    width = GROUP * HEAD
    for rc, rows in ((0, near), (1, far)):
        lhs = rows[...].reshape(2 * ROWS, width)
        for i, distance in enumerate(DISTANCES):
            if i < 7:
                product = jnp.dot(lhs, weights[i][...], preferred_element_type=jnp.float32)
            else:
                product = jnp.dot(
                    lhs[:, : width // 2], top[...], preferred_element_type=jnp.float32
                ) + jnp.dot(lhs[:, width // 2 :], bottom[...], preferred_element_type=jnp.float32)
            product = product.astype(jnp.bfloat16)
            target = lax.rem(z + distance + Z, Z)
            for ryl in range(2):
                q = (yl ^ ryl) * 2 + (c ^ rc)
                out[q, target] = product[ryl * ROWS : (ryl + 1) * ROWS, :]


def project(place, near, far, pieces):
    vmem = pl.BlockSpec(memory_space=pltpu.VMEM)
    columns = pieces[0].shape[1]
    return pl.pallas_call(
        project_kernel,
        in_specs=[pl.BlockSpec(memory_space=pltpu.SMEM)] + [vmem] * 11,
        out_specs=vmem,
        out_shape=jax.ShapeDtypeStruct((4, Z, ROWS, columns), jnp.bfloat16),
        compiler_params=params(),
        name="project",
        cost_estimate=pl.CostEstimate(
            flops=2 * 4 * ROWS * GROUP * HEAD * Z * columns,
            bytes_accessed=4_000_000,
            transcendentals=0,
        ),
    )(place, near, far, *pieces)


PAD = 16


def third_kernel(place, received, hidden, gain, near, far, out, partial, scaled):
    c = place[2]
    columns = received.shape[3]
    squares = jnp.zeros((ROWS, columns), jnp.float32)
    for q in range(4):
        at = slice(q * columns, (q + 1) * columns)
        total = received[q, 0].astype(jnp.float32)
        for h in range(1, Z):
            total = total + received[q, h].astype(jnp.float32)
        result = (hidden[:, at].astype(jnp.float32) + total).astype(jnp.bfloat16)
        out[:, at] = result
        wide = result.astype(jnp.float32)
        squares = squares + wide * wide
        scaled[q // 2, :, (q % 2) * columns : (q % 2 + 1) * columns] = (
            wide * gain[:, at]
        ).astype(jnp.bfloat16)
    squares = jnp.sum(squares, axis=1, keepdims=True)
    row = row_of(jnp.broadcast_to(squares, (ROWS, ROWS)))
    high = row.astype(jnp.bfloat16)
    low = (row - high.astype(jnp.float32)).astype(jnp.bfloat16)
    tail = jnp.broadcast_to(
        jnp.concatenate([high, low], axis=1).astype(jnp.float32), (PAD, 2 * ROWS)
    ).astype(jnp.bfloat16)
    near_rows, far_rows = scaled[c], scaled[1 - c]
    for h in range(Z):
        product = jnp.dot(near_rows, near[h], preferred_element_type=jnp.float32) + jnp.dot(
            far_rows, far[h], preferred_element_type=jnp.float32
        )
        partial[h, :ROWS, :] = product.astype(jnp.bfloat16)
        partial[h, ROWS:, :] = tail


def third_partials(place, received, hidden, gain, near, far):
    vmem = pl.BlockSpec(memory_space=pltpu.VMEM)
    width = hidden.shape[1]
    return pl.pallas_call(
        third_kernel,
        in_specs=[pl.BlockSpec(memory_space=pltpu.SMEM)] + [vmem] * 5,
        out_specs=(vmem, vmem),
        out_shape=(
            jax.ShapeDtypeStruct(hidden.shape, jnp.bfloat16),
            jax.ShapeDtypeStruct((Z, ROWS + PAD, 2 * HEAD), jnp.bfloat16),
        ),
        scratch_shapes=[pltpu.VMEM((2, ROWS, width // 2), jnp.bfloat16)],
        compiler_params=params(),
        name="third",
    )(place, received, hidden, gain, near, far)


def final_kernel(count, partial, bias, cosine, sine, index, out):
    total = partial[0, :ROWS, :].astype(jnp.float32)
    tail = partial[0, ROWS:, :].astype(jnp.float32)
    for h in range(1, Z):
        total = total + partial[h, :ROWS, :].astype(jnp.float32)
        tail = tail + partial[h, ROWS:, :].astype(jnp.float32)
    squares = tail[0:1, :ROWS] + tail[0:1, ROWS:]
    factor = lax.rsqrt(column_of(squares) / MODEL_WIDTH + 1e-06)
    keys = total[:, :HEAD] * factor + bias[:, :HEAD]
    values = total[:, HEAD:] * factor + bias[:, HEAD:]
    keys = rotated(keys, cosine[...], sine[...])
    rows = jnp.concatenate([keys, values], axis=1).astype(jnp.bfloat16)
    slot = lax.broadcasted_iota(jnp.int32, (ROWS, ROWS), 1)
    token = lax.broadcasted_iota(jnp.int32, (ROWS, ROWS), 0)
    chosen = (token == index[...]) & (slot < count[0])
    pick = jnp.where(chosen, 1.0, 0.0).astype(jnp.bfloat16)
    out[...] = lax.dot_general(
        pick, rows, (((0,), (0,)), ((), ())), preferred_element_type=jnp.float32
    ).astype(jnp.bfloat16)


def final(count, partial, bias, cosine, sine, index):
    vmem = pl.BlockSpec(memory_space=pltpu.VMEM)
    return pl.pallas_call(
        final_kernel,
        in_specs=[pl.BlockSpec(memory_space=pltpu.SMEM)] + [vmem] * 5,
        out_specs=vmem,
        out_shape=jax.ShapeDtypeStruct((ROWS, 2 * HEAD), jnp.bfloat16),
        compiler_params=params(),
        name="final",
    )(count, partial, bias, cosine, sine, index)


def swap(x, axis):
    return lax.ppermute(x, axis, [(0, 1), (1, 0)])


def along_z(x, distance):
    return lax.ppermute(x, "z", [(i, (i + distance) % Z) for i in range(Z)])


def after(x, *others):
    return lax.optimization_barrier((x, others))[0]


def step(pair):
    return [along_z(pair[0], 1), along_z(pair[1], -1)]


def last_step(pair):
    half = pair[0].shape[0] // 2
    return [along_z(pair[0][:half], 1), along_z(pair[1][half:], -1)]


def local(
    hidden,
    query,
    fresh_key_value,
    cached_key_value,
    positions,
    out_weight,
    norm_gain,
    layer3_key_value_weight,
    layer3_key_value_bias,
    keep_index,
    keep_count,
):
    z, yl, c = lax.axis_index("z"), lax.axis_index("yl"), lax.axis_index("c")
    place = jnp.stack([z, yl, c]).astype(jnp.int32)

    cosine, sine = tables(positions, HEAD)
    rotated_query, kv = prepare(query, fresh_key_value, cached_key_value, cosine, sine)
    weights_1 = step([out_weight, out_weight])
    kv_1 = list(after(step([kv, kv]), *weights_1))
    kv_2 = step(kv_1)
    weights_2 = step(weights_1)
    kv_3 = step(kv_2)
    weights_3 = step(weights_2)
    weights_4 = last_step(weights_3)
    weights = [out_weight, *weights_1, *weights_2, *weights_3, *weights_4]
    rotated_query = rotated_query.reshape(GROUP * ROWS, HEAD)
    near_query = jnp.concatenate([rotated_query, swap(rotated_query, "yl")], axis=0)
    far_query = swap(near_query, "c")
    third_rows = layer3_key_value_weight.reshape(Z, 2, MODEL_WIDTH // Z // 2, 2 * HEAD)
    third_rows = lax.dynamic_index_in_dim(third_rows, c, axis=1, keepdims=False)
    third_rows = after(third_rows, *kv_2, near_query)
    third_near = lax.all_to_all(third_rows, HEAD_AXES, 0, 0, tiled=True)
    third_far = swap(third_near, "c")

    early = [kv, *kv_1, *kv_2]
    early_cached = [(i, i) for i in range(5)]
    early_fresh = [[(0, 0, 0), (1, 1, -1)], [(2, 2, 1), (3, 3, -2)]]
    late_cached = [(1, 1), (2, 2), (3, 4)]
    late_fresh = [[(0, 0, 2), (1, 1, -3)], [(2, 2, 3), (3, 4, 4)]]
    near_query = after(near_query, *weights_2)
    near_state = attend(place, 0, near_query, early, early_cached, early_fresh)
    kv_3 = list(after(kv_3, near_state))
    late = [kv_2[1], *kv_3, *last_step(kv_3)]
    far_query = after(far_query, near_state)
    far_state = attend(place, 1, far_query, early, early_cached, early_fresh)
    far_state = after(far_state, *weights_3)
    send, send_lse = attend(place, 1, far_query, late, late_cached, late_fresh, far_state, True)
    got, got_lse = swap(send, "c"), swap(send_lse, "c")
    own, own_lse = attend(place, 0, near_query, late, late_cached, late_fresh, near_state, True)
    got_lse = after(got_lse, *weights_4)
    own, own_lse = merge(own, own_lse, got, got_lse)
    got, got_lse = swap(own, "yl"), swap(own_lse, "yl")
    got_lse = after(got_lse, third_near)
    near = merge_last(own, own_lse, got, got_lse)
    far = swap(near, "c")

    products = project(place, near, far, weights)
    products = products.reshape(4 * Z, *products.shape[2:])
    received = lax.all_to_all(products, ("yl", "c", "x", "yh"), 0, 0, tiled=True)
    received = received.reshape(4, Z, *received.shape[1:])

    layer2_out, partial = third_partials(
        place, received, hidden, norm_gain.reshape(1, -1), third_near, third_far
    )
    partial = lax.all_to_all(partial, HEAD_AXES, 0, 0, tiled=True)
    packed = final(
        keep_count,
        partial,
        layer3_key_value_bias.reshape(1, -1),
        cosine,
        sine,
        keep_index.reshape(1, -1),
    )
    return (layer2_out, packed)


def solution(mesh):
    split = Mesh(mesh.devices.reshape(Z, 2, 2, 4, 2), CTX_AXES + HEAD_AXES)
    placed = (
        P(CTX_AXES, HEAD_AXES),
        P(CTX_AXES, HEAD_AXES),
        P(None, CTX_AXES, HEAD_AXES),
        P(None, CTX_AXES, HEAD_AXES),
        P(None, CTX_AXES),
        P(HEAD_AXES, CTX_AXES),
        P(HEAD_AXES),
        P(None, HEAD_AXES),
        P(HEAD_AXES),
        P(CTX_AXES),
        P(CTX_AXES),
    )
    return jax.shard_map(
        local,
        mesh=split,
        in_specs=placed,
        out_specs=(P(CTX_AXES, HEAD_AXES), P(CTX_AXES, HEAD_AXES)),
        check_vma=False,
    )
```

```python
import functools

import jax
import jax.numpy as jnp
from jax import lax
from jax.experimental import pallas as pl
from jax.experimental.pallas import tpu as pltpu
from jax.sharding import Mesh
from jax.sharding import PartitionSpec as P

MODEL_WIDTH = 8192
HEAD = 128
ROWS = 128
CACHED = 256
GROUP = 8
Z = 8
LOG2E = 1.4426950408889634
SCALE = HEAD ** (-0.5) * LOG2E
CTX_AXES = ("z", "yl", "c")
HEAD_AXES = ("x", "yh")
VMEM = 56 * 1024 * 1024
CHUNK = 512
BLOCKS = 3
DISTANCES = (0, -1, 1, -2, 2, -3, 3, 4)


def params(**more):
    return pltpu.CompilerParams(vmem_limit_bytes=VMEM, **more)


def tables(positions, head_size):
    half = head_size // 2
    column = jnp.arange(half)
    frequency = jnp.power(jnp.float32(1000000.0), -(2.0 * column.astype(jnp.float32)) / head_size)
    section = (column >= head_size // 8).astype(jnp.int32) + (
        column >= head_size // 8 + 3 * head_size // 16
    ).astype(jnp.int32)
    places = positions.astype(jnp.float32)
    chosen = jnp.where(
        section[None, :] == 0,
        places[0][:, None],
        jnp.where(section[None, :] == 1, places[1][:, None], places[2][:, None]),
    )
    angles = chosen * frequency[None, :]
    cosine, sine = jnp.cos(angles), jnp.sin(angles)
    return (
        jnp.concatenate([cosine, cosine], axis=1),
        jnp.concatenate([-sine, sine], axis=1),
    )


def rotated(x, cosine, sine):
    return x * cosine + pltpu.roll(x, HEAD // 2, 1) * sine


def prepare_kernel(
    place, query, fresh, cached, cosine, sine, weight, query_out, kv_out, weight_out, sem
):
    copy = pltpu.make_async_copy(weight.at[:, place[2]], weight_out, sem)
    copy.start()
    cos, sin = cosine[...], sine[...]
    for g in range(GROUP):
        piece = query[:, g * HEAD : (g + 1) * HEAD].astype(jnp.float32)
        query_out[g] = rotated(piece, cos, sin).astype(jnp.bfloat16)
    for k in range(CACHED // ROWS):
        kv_out[k] = jnp.transpose(cached[0, k * ROWS : (k + 1) * ROWS, :])
        kv_out[BLOCKS + k] = cached[1, k * ROWS : (k + 1) * ROWS, :]
    new_key = rotated(fresh[0].astype(jnp.float32), cos, sin).astype(jnp.bfloat16)
    kv_out[BLOCKS - 1] = jnp.transpose(new_key)
    kv_out[2 * BLOCKS - 1] = fresh[1]
    copy.wait()


def prepare(place, query, fresh, cached, cosine, sine, weight):
    vmem = pl.BlockSpec(memory_space=pltpu.VMEM)
    return pl.pallas_call(
        prepare_kernel,
        in_specs=[pl.BlockSpec(memory_space=pltpu.SMEM)]
        + [vmem] * 5
        + [pl.BlockSpec(memory_space=pl.ANY)],
        out_specs=(vmem, vmem, pl.BlockSpec(memory_space=pl.ANY)),
        out_shape=(
            jax.ShapeDtypeStruct((GROUP, ROWS, HEAD), jnp.bfloat16),
            jax.ShapeDtypeStruct((2 * BLOCKS, ROWS, HEAD), jnp.bfloat16),
            jax.ShapeDtypeStruct((Z, *weight.shape[2:]), jnp.bfloat16),
        ),
        scratch_shapes=[pltpu.SemaphoreType.DMA],
        compiler_params=params(),
        name="prepare",
        cost_estimate=pl.CostEstimate(flops=2_000_000, bytes_accessed=5_500_000, transcendentals=0),
    )(place, query, fresh, cached, cosine, sine, weight)


def column_of(row):
    return jnp.transpose(jnp.broadcast_to(row, (ROWS, ROWS)))


def row_of(column):
    return jnp.transpose(column)[0:1, :]


def attend_kernel(cached, fresh, first, last, rc, place, query, *refs):
    n_in = 1 + max([max(k, v) for k, v in cached] + [max(p[0], p[1]) for pair in fresh for p in pair])
    pieces, rest = refs[:n_in], list(refs[n_in:])
    if not first:
        acc_in, m_in = rest[:2]
        rest = rest[2:]
    if last:
        out, lse_out = rest[:2]
    else:
        acc_out, m_out = rest[:2]
    keys, values = rest[2:]
    step = pl.program_id(0)
    z, yl, c = place[0], place[1], place[2]
    steps = len(cached) + len(fresh)

    def value_block(ref, k):
        return ref[BLOCKS + k] if ref.shape[0] == 2 * BLOCKS else ref[k]

    @pl.when(step == 0)
    def _():
        at = 0
        for kp, vp in cached:
            for k in range(2):
                keys[:, at : at + ROWS] = pieces[kp][k]
                values[at : at + ROWS, :HEAD] = value_block(pieces[vp], k)
                at += ROWS
        for pair in fresh:
            for kp, vp, _ in pair:
                keys[:, at : at + ROWS] = pieces[kp][BLOCKS - 1]
                values[at : at + ROWS, :HEAD] = value_block(pieces[vp], BLOCKS - 1)
                at += ROWS
        values[:, HEAD:] = jnp.ones((steps * 2 * ROWS, HEAD), jnp.bfloat16)

    per_block = GROUP * ROWS // CHUNK
    ryl = step // per_block
    block = z * 4 + (yl ^ ryl) * 2 + (c ^ rc)
    inside = lax.broadcasted_iota(jnp.int32, (CHUNK, 1), 0) & (ROWS - 1)
    query_token = block * ROWS + inside
    lane = lax.broadcasted_iota(jnp.int32, (1, 2 * ROWS), 1)
    q = query[...]
    if first:
        m = jnp.full((CHUNK, 1), -1e30, jnp.float32)
        acc = jnp.zeros((CHUNK, 2 * HEAD), jnp.float32)
    else:
        m = jnp.max(m_in[...], axis=1, keepdims=True)
        acc = acc_in[...]
    for i in range(steps):
        at = slice(i * 2 * ROWS, (i + 1) * 2 * ROWS)
        scores = jnp.dot(q, keys[:, at], preferred_element_type=jnp.float32)
        if i >= len(cached):
            one, two = (
                (lax.rem(z + p[2] + Z, Z) * 4 + yl * 2 + c) * ROWS for p in fresh[i - len(cached)]
            )
            key_token = jnp.where(lane < ROWS, one + lane, two + lane - ROWS)
            scores = jnp.where(key_token <= query_token, scores, -1e30)
        raised = jnp.maximum(m, jnp.max(scores, axis=1, keepdims=True))
        weights = jnp.exp2((scores - raised) * SCALE).astype(jnp.bfloat16)
        factor = jnp.exp2((m - raised) * SCALE)
        acc = acc * factor + jnp.dot(weights, values[at, :], preferred_element_type=jnp.float32)
        m = raised
    if not last:
        acc_out[...] = acc
        m_out[...] = jnp.broadcast_to(m, (CHUNK, HEAD))
        return
    totals = acc[:, HEAD:]
    out[...] = (acc[:, :HEAD] / totals).astype(jnp.bfloat16)
    lse = m * SCALE + jnp.log2(totals)
    for k in range(CHUNK // ROWS):
        lse_out[step * (CHUNK // ROWS) + k] = row_of(lse[k * ROWS : (k + 1) * ROWS, :])


def attend(place, rc, query, pieces, cached, fresh, state=None, last=False):
    rows = query.shape[0]
    total = 2 * ROWS * (len(cached) + len(fresh))
    row_spec = pl.BlockSpec((CHUNK, HEAD), lambda i, s: (i, 0))
    wide_spec = pl.BlockSpec((CHUNK, 2 * HEAD), lambda i, s: (i, 0))
    in_specs = [row_spec] + [pl.BlockSpec(p.shape, lambda i, s: (0, 0, 0)) for p in pieces]
    args = [query, *pieces]
    if state is not None:
        in_specs += [wide_spec, row_spec]
        args += list(state)
    if last:
        out_specs = [row_spec, pl.BlockSpec((rows // ROWS, 1, ROWS), lambda i, s: (0, 0, 0))]
        out_shape = (
            jax.ShapeDtypeStruct((rows, HEAD), jnp.bfloat16),
            jax.ShapeDtypeStruct((rows // ROWS, 1, ROWS), jnp.float32),
        )
    else:
        out_specs = [wide_spec, row_spec]
        out_shape = (
            jax.ShapeDtypeStruct((rows, 2 * HEAD), jnp.float32),
            jax.ShapeDtypeStruct((rows, HEAD), jnp.float32),
        )
    return pl.pallas_call(
        functools.partial(attend_kernel, cached, fresh, state is None, last, rc),
        grid_spec=pltpu.PrefetchScalarGridSpec(
            num_scalar_prefetch=1,
            grid=(rows // CHUNK,),
            in_specs=in_specs,
            out_specs=out_specs,
            scratch_shapes=[
                pltpu.VMEM((HEAD, total), jnp.bfloat16),
                pltpu.VMEM((total, 2 * HEAD), jnp.bfloat16),
            ],
        ),
        out_shape=out_shape,
        compiler_params=params(),
        name="attend",
        cost_estimate=pl.CostEstimate(
            flops=4 * rows * total * HEAD,
            bytes_accessed=8 * rows * HEAD + 4 * total * HEAD,
            transcendentals=rows * total,
        ),
    )(place, *args)


def merge_weight(first_lse, second_lse):
    top = jnp.maximum(first_lse, second_lse)
    a, b = jnp.exp2(first_lse - top), jnp.exp2(second_lse - top)
    return a / (a + b), top + jnp.log2(a + b)


def merged(first, second, weight):
    a, b = first.astype(jnp.float32), second.astype(jnp.float32)
    share = column_of(weight)
    return (a * share + b * (1.0 - share)).astype(jnp.bfloat16)


def merge_kernel(own, own_lse, other, other_lse, out, lse_out):
    for k in range(own.shape[0] // ROWS):
        at = slice(k * ROWS, (k + 1) * ROWS)
        weight, lse = merge_weight(own_lse[k], other_lse[k])
        out[at, :] = merged(own[at, :], other[at, :], weight)
        lse_out[k] = lse


def merge_last_kernel(own, own_lse, other, other_lse, out):
    for y in range(2):
        for g in range(GROUP):
            k, j = y * GROUP + g, (1 - y) * GROUP + g
            weight, _ = merge_weight(own_lse[k], other_lse[j])
            out[y, :, g * HEAD : (g + 1) * HEAD] = merged(
                own[k * ROWS : (k + 1) * ROWS, :], other[j * ROWS : (j + 1) * ROWS, :], weight
            )


MERGE_COST = pl.CostEstimate(flops=2_000_000, bytes_accessed=1_600_000, transcendentals=4096)


def merge(own, own_lse, other, other_lse):
    return pl.pallas_call(
        merge_kernel,
        out_shape=(
            jax.ShapeDtypeStruct(own.shape, own.dtype),
            jax.ShapeDtypeStruct(own_lse.shape, own_lse.dtype),
        ),
        compiler_params=params(),
        name="merge",
        cost_estimate=MERGE_COST,
    )(own, own_lse, other, other_lse)


def merge_last(own, own_lse, other, other_lse):
    return pl.pallas_call(
        merge_last_kernel,
        out_shape=jax.ShapeDtypeStruct((2, ROWS, GROUP * HEAD), jnp.bfloat16),
        compiler_params=params(),
        name="merge_last",
        cost_estimate=MERGE_COST,
    )(own, own_lse, other, other_lse)


def project_kernel(place, near, far, *refs):
    weights, top, bottom, out = refs[:7], refs[7], refs[8], refs[9]
    z, yl, c = place[0], place[1], place[2]
    width = GROUP * HEAD
    for rc, rows in ((0, near), (1, far)):
        lhs = rows[...].reshape(2 * ROWS, width)
        for i, distance in enumerate(DISTANCES):
            if i < 7:
                product = jnp.dot(lhs, weights[i][...], preferred_element_type=jnp.float32)
            else:
                product = jnp.dot(
                    lhs[:, : width // 2], top[...], preferred_element_type=jnp.float32
                ) + jnp.dot(lhs[:, width // 2 :], bottom[...], preferred_element_type=jnp.float32)
            product = product.astype(jnp.bfloat16)
            target = lax.rem(z + distance + Z, Z)
            for ryl in range(2):
                q = (yl ^ ryl) * 2 + (c ^ rc)
                out[q, target] = product[ryl * ROWS : (ryl + 1) * ROWS, :]


def project(place, near, far, pieces):
    vmem = pl.BlockSpec(memory_space=pltpu.VMEM)
    columns = pieces[0].shape[1]
    return pl.pallas_call(
        project_kernel,
        in_specs=[pl.BlockSpec(memory_space=pltpu.SMEM)] + [vmem] * 11,
        out_specs=vmem,
        out_shape=jax.ShapeDtypeStruct((4, Z, ROWS, columns), jnp.bfloat16),
        compiler_params=params(),
        name="project",
        cost_estimate=pl.CostEstimate(
            flops=2 * 4 * ROWS * GROUP * HEAD * Z * columns,
            bytes_accessed=4_000_000,
            transcendentals=0,
        ),
    )(place, near, far, *pieces)


PAD = 16


def third_kernel(place, received, hidden, gain, near, far, out, partial, scaled):
    c = place[2]
    columns = received.shape[3]
    squares = jnp.zeros((ROWS, columns), jnp.float32)
    for q in range(4):
        at = slice(q * columns, (q + 1) * columns)
        total = received[q, 0].astype(jnp.float32)
        for h in range(1, Z):
            total = total + received[q, h].astype(jnp.float32)
        result = (hidden[:, at].astype(jnp.float32) + total).astype(jnp.bfloat16)
        out[:, at] = result
        wide = result.astype(jnp.float32)
        squares = squares + wide * wide
        scaled[q // 2, :, (q % 2) * columns : (q % 2 + 1) * columns] = (
            wide * gain[:, at]
        ).astype(jnp.bfloat16)
    squares = jnp.sum(squares, axis=1, keepdims=True)
    row = row_of(jnp.broadcast_to(squares, (ROWS, ROWS)))
    high = row.astype(jnp.bfloat16)
    low = (row - high.astype(jnp.float32)).astype(jnp.bfloat16)
    tail = jnp.broadcast_to(
        jnp.concatenate([high, low], axis=1).astype(jnp.float32), (PAD, 2 * ROWS)
    ).astype(jnp.bfloat16)
    near_rows, far_rows = scaled[c], scaled[1 - c]
    for h in range(Z):
        product = jnp.dot(near_rows, near[h], preferred_element_type=jnp.float32) + jnp.dot(
            far_rows, far[h], preferred_element_type=jnp.float32
        )
        partial[h, :ROWS, :] = product.astype(jnp.bfloat16)
        partial[h, ROWS:, :] = tail


def third_partials(place, received, hidden, gain, near, far):
    vmem = pl.BlockSpec(memory_space=pltpu.VMEM)
    width = hidden.shape[1]
    return pl.pallas_call(
        third_kernel,
        in_specs=[pl.BlockSpec(memory_space=pltpu.SMEM)] + [vmem] * 5,
        out_specs=(vmem, vmem),
        out_shape=(
            jax.ShapeDtypeStruct(hidden.shape, jnp.bfloat16),
            jax.ShapeDtypeStruct((Z, ROWS + PAD, 2 * HEAD), jnp.bfloat16),
        ),
        scratch_shapes=[pltpu.VMEM((2, ROWS, width // 2), jnp.bfloat16)],
        compiler_params=params(),
        name="third",
    )(place, received, hidden, gain, near, far)


def final_kernel(count, partial, bias, cosine, sine, index, out):
    total = partial[0, :ROWS, :].astype(jnp.float32)
    tail = partial[0, ROWS:, :].astype(jnp.float32)
    for h in range(1, Z):
        total = total + partial[h, :ROWS, :].astype(jnp.float32)
        tail = tail + partial[h, ROWS:, :].astype(jnp.float32)
    squares = tail[0:1, :ROWS] + tail[0:1, ROWS:]
    factor = lax.rsqrt(column_of(squares) / MODEL_WIDTH + 1e-06)
    keys = total[:, :HEAD] * factor + bias[:, :HEAD]
    values = total[:, HEAD:] * factor + bias[:, HEAD:]
    keys = rotated(keys, cosine[...], sine[...])
    rows = jnp.concatenate([keys, values], axis=1).astype(jnp.bfloat16)
    slot = lax.broadcasted_iota(jnp.int32, (ROWS, ROWS), 1)
    token = lax.broadcasted_iota(jnp.int32, (ROWS, ROWS), 0)
    chosen = (token == index[...]) & (slot < count[0])
    pick = jnp.where(chosen, 1.0, 0.0).astype(jnp.bfloat16)
    out[...] = lax.dot_general(
        pick, rows, (((0,), (0,)), ((), ())), preferred_element_type=jnp.float32
    ).astype(jnp.bfloat16)


def final(count, partial, bias, cosine, sine, index):
    vmem = pl.BlockSpec(memory_space=pltpu.VMEM)
    return pl.pallas_call(
        final_kernel,
        in_specs=[pl.BlockSpec(memory_space=pltpu.SMEM)] + [vmem] * 5,
        out_specs=vmem,
        out_shape=jax.ShapeDtypeStruct((ROWS, 2 * HEAD), jnp.bfloat16),
        compiler_params=params(),
        name="final",
    )(count, partial, bias, cosine, sine, index)


def swap(x, axis):
    return lax.ppermute(x, axis, [(0, 1), (1, 0)])


def along_z(x, distance):
    return lax.ppermute(x, "z", [(i, (i + distance) % Z) for i in range(Z)])


def after(x, *others):
    return lax.optimization_barrier((x, others))[0]


def step(pair):
    return [along_z(pair[0], 1), along_z(pair[1], -1)]


def last_step(pair):
    half = pair[0].shape[0] // 2
    return [along_z(pair[0][:half], 1), along_z(pair[1][half:], -1)]


def local(
    hidden,
    query,
    fresh_key_value,
    cached_key_value,
    positions,
    out_weight,
    norm_gain,
    layer3_key_value_weight,
    layer3_key_value_bias,
    keep_index,
    keep_count,
):
    z, yl, c = lax.axis_index("z"), lax.axis_index("yl"), lax.axis_index("c")
    place = jnp.stack([z, yl, c]).astype(jnp.int32)

    cosine, sine = tables(positions, HEAD)
    rotated_query, kv, third_rows = prepare(
        place,
        query,
        fresh_key_value,
        cached_key_value,
        cosine,
        sine,
        layer3_key_value_weight.reshape(Z, 2, MODEL_WIDTH // Z // 2, 2 * HEAD),
    )
    weights_1 = step([out_weight, out_weight])
    kv_1 = list(after(step([kv, kv]), *weights_1))
    kv_2 = step(kv_1)
    weights_2 = step(weights_1)
    kv_3 = step(kv_2)
    weights_2 = list(after(weights_2, *kv_3))
    weights_3 = step(weights_2)
    weights_4 = last_step(weights_3)
    weights = [out_weight, *weights_1, *weights_2, *weights_3, *weights_4]
    rotated_query = rotated_query.reshape(GROUP * ROWS, HEAD)
    near_query = jnp.concatenate([rotated_query, swap(rotated_query, "yl")], axis=0)
    far_query = swap(near_query, "c")
    early = [kv, *kv_1, *kv_2]
    early_cached = [(i, i) for i in range(5)]
    early_fresh = [[(0, 0, 0), (1, 1, -1)], [(2, 2, 1), (3, 3, -2)]]
    late_cached = [(1, 1), (2, 2), (3, 4)]
    late_fresh = [[(0, 0, 2), (1, 1, -3)], [(2, 2, 3), (3, 4, 4)]]
    near_state = attend(place, 0, near_query, early, early_cached, early_fresh)
    kv_3 = list(after(kv_3, near_state))
    late = [kv_2[1], *kv_3, *last_step(kv_3)]
    far_query = after(far_query, near_state, *weights_2)
    third_rows = after(third_rows, *kv_3)
    third_near = lax.all_to_all(third_rows, HEAD_AXES, 0, 0, tiled=True)
    third_far = swap(third_near, "c")
    far_state = attend(place, 1, far_query, early, early_cached, early_fresh)
    far_state = after(far_state, *weights_3)
    send, send_lse = attend(place, 1, far_query, late, late_cached, late_fresh, far_state, True)
    got, got_lse = swap(send, "c"), swap(send_lse, "c")
    own, own_lse = attend(place, 0, near_query, late, late_cached, late_fresh, near_state, True)
    got_lse = after(got_lse, *weights_4)
    own, own_lse = merge(own, own_lse, got, got_lse)
    got, got_lse = swap(own, "yl"), swap(own_lse, "yl")
    got_lse = after(got_lse, third_near)
    near = merge_last(own, own_lse, got, got_lse)
    far = swap(near, "c")

    products = project(place, near, far, weights)
    products = products.reshape(4 * Z, *products.shape[2:])
    received = lax.all_to_all(products, ("yl", "c", "x", "yh"), 0, 0, tiled=True)
    received = received.reshape(4, Z, *received.shape[1:])

    layer2_out, partial = third_partials(
        place, received, hidden, norm_gain.reshape(1, -1), third_near, third_far
    )
    partial = lax.all_to_all(partial, HEAD_AXES, 0, 0, tiled=True)
    packed = final(
        keep_count,
        partial,
        layer3_key_value_bias.reshape(1, -1),
        cosine,
        sine,
        keep_index.reshape(1, -1),
    )
    return (layer2_out, packed)


def solution(mesh):
    split = Mesh(mesh.devices.reshape(Z, 2, 2, 4, 2), CTX_AXES + HEAD_AXES)
    placed = (
        P(CTX_AXES, HEAD_AXES),
        P(CTX_AXES, HEAD_AXES),
        P(None, CTX_AXES, HEAD_AXES),
        P(None, CTX_AXES, HEAD_AXES),
        P(None, CTX_AXES),
        P(HEAD_AXES, CTX_AXES),
        P(HEAD_AXES),
        P(None, HEAD_AXES),
        P(HEAD_AXES),
        P(CTX_AXES),
        P(CTX_AXES),
    )
    return jax.shard_map(
        local,
        mesh=split,
        in_specs=placed,
        out_specs=(P(CTX_AXES, HEAD_AXES), P(CTX_AXES, HEAD_AXES)),
        check_vma=False,
    )
```

```python
import functools

import jax
import jax.numpy as jnp
from jax import lax
from jax.experimental import pallas as pl
from jax.experimental.pallas import tpu as pltpu
from jax.sharding import Mesh
from jax.sharding import PartitionSpec as P

MODEL_WIDTH = 8192
HEAD = 128
ROWS = 128
CACHED = 256
GROUP = 8
Z = 8
LOG2E = 1.4426950408889634
SCALE = HEAD ** (-0.5) * LOG2E
CTX_AXES = ("z", "yl", "c")
HEAD_AXES = ("x", "yh")
VMEM = 56 * 1024 * 1024
CHUNK = 512
BLOCKS = 3


def params(**more):
    return pltpu.CompilerParams(vmem_limit_bytes=VMEM, **more)


def tables(positions, head_size):
    half = head_size // 2
    column = jnp.arange(half)
    frequency = jnp.power(jnp.float32(1000000.0), -(2.0 * column.astype(jnp.float32)) / head_size)
    section = (column >= head_size // 8).astype(jnp.int32) + (
        column >= head_size // 8 + 3 * head_size // 16
    ).astype(jnp.int32)
    places = positions.astype(jnp.float32)
    chosen = jnp.where(
        section[None, :] == 0,
        places[0][:, None],
        jnp.where(section[None, :] == 1, places[1][:, None], places[2][:, None]),
    )
    angles = chosen * frequency[None, :]
    cosine, sine = jnp.cos(angles), jnp.sin(angles)
    return (
        jnp.concatenate([cosine, cosine], axis=1),
        jnp.concatenate([-sine, sine], axis=1),
    )


def rotated(x, cosine, sine):
    return x * cosine + pltpu.roll(x, HEAD // 2, 1) * sine


def prepare_kernel(
    place, query, fresh, cached, cosine, sine, weight, query_out, kv_out, weight_out, sem
):
    copy = pltpu.make_async_copy(weight.at[:, place[2]], weight_out, sem)
    copy.start()
    cos, sin = cosine[...], sine[...]
    for g in range(GROUP):
        piece = query[:, g * HEAD : (g + 1) * HEAD].astype(jnp.float32)
        query_out[g] = rotated(piece, cos, sin).astype(jnp.bfloat16)
    for k in range(CACHED // ROWS):
        kv_out[k] = jnp.transpose(cached[0, k * ROWS : (k + 1) * ROWS, :])
        kv_out[BLOCKS + k] = cached[1, k * ROWS : (k + 1) * ROWS, :]
    new_key = rotated(fresh[0].astype(jnp.float32), cos, sin).astype(jnp.bfloat16)
    kv_out[BLOCKS - 1] = jnp.transpose(new_key)
    kv_out[2 * BLOCKS - 1] = fresh[1]
    copy.wait()


def prepare(place, query, fresh, cached, cosine, sine, weight):
    vmem = pl.BlockSpec(memory_space=pltpu.VMEM)
    return pl.pallas_call(
        prepare_kernel,
        in_specs=[pl.BlockSpec(memory_space=pltpu.SMEM)]
        + [vmem] * 5
        + [pl.BlockSpec(memory_space=pl.ANY)],
        out_specs=(vmem, vmem, vmem),
        out_shape=(
            jax.ShapeDtypeStruct((GROUP, ROWS, HEAD), jnp.bfloat16),
            jax.ShapeDtypeStruct((2 * BLOCKS, ROWS, HEAD), jnp.bfloat16),
            jax.ShapeDtypeStruct((Z, *weight.shape[2:]), jnp.bfloat16),
        ),
        scratch_shapes=[pltpu.SemaphoreType.DMA],
        compiler_params=params(),
        name="prepare",
        cost_estimate=pl.CostEstimate(flops=2_000_000, bytes_accessed=5_500_000, transcendentals=0),
    )(place, query, fresh, cached, cosine, sine, weight)


def column_of(row):
    return jnp.transpose(jnp.broadcast_to(row, (ROWS, ROWS)))


def row_of(column):
    return jnp.transpose(column)[0:1, :]


def attend_kernel(cached, fresh, first, last, rc, place, query, *refs):
    n_in = 1 + max([max(k, v) for k, v in cached] + [max(p[0], p[1]) for pair in fresh for p in pair])
    pieces, rest = refs[:n_in], list(refs[n_in:])
    if not first:
        acc_in, m_in = rest[:2]
        rest = rest[2:]
    if last:
        out, lse_out = rest[:2]
    else:
        acc_out, m_out = rest[:2]
    keys, values = rest[2:]
    step = pl.program_id(0)
    z, yl, c = place[0], place[1], place[2]
    steps = len(cached) + len(fresh)

    @pl.when(step == 0)
    def _():
        at = 0
        for kp, vp in cached:
            for k in range(2):
                keys[:, at : at + ROWS] = pieces[kp][k]
                values[at : at + ROWS, :HEAD] = pieces[vp][BLOCKS + k]
                at += ROWS
        for pair in fresh:
            for kp, vp, _ in pair:
                keys[:, at : at + ROWS] = pieces[kp][BLOCKS - 1]
                values[at : at + ROWS, :HEAD] = pieces[vp][2 * BLOCKS - 1]
                at += ROWS
        values[:, HEAD:] = jnp.ones((steps * 2 * ROWS, HEAD), jnp.bfloat16)

    per_block = GROUP * ROWS // CHUNK
    ryl = step // per_block
    block = z * 4 + (yl ^ ryl) * 2 + (c ^ rc)
    inside = lax.broadcasted_iota(jnp.int32, (CHUNK, 1), 0) & (ROWS - 1)
    query_token = block * ROWS + inside
    lane = lax.broadcasted_iota(jnp.int32, (1, 2 * ROWS), 1)
    q = query[...]
    if first:
        m = jnp.full((CHUNK, 1), -1e30, jnp.float32)
        acc = jnp.zeros((CHUNK, 2 * HEAD), jnp.float32)
    else:
        m = jnp.max(m_in[...], axis=1, keepdims=True)
        acc = acc_in[...]
    for i in range(steps):
        at = slice(i * 2 * ROWS, (i + 1) * 2 * ROWS)
        scores = jnp.dot(q, keys[:, at], preferred_element_type=jnp.float32)
        if i >= len(cached):
            one, two = (
                (lax.rem(z + p[2] + Z, Z) * 4 + yl * 2 + c) * ROWS for p in fresh[i - len(cached)]
            )
            key_token = jnp.where(lane < ROWS, one + lane, two + lane - ROWS)
            scores = jnp.where(key_token <= query_token, scores, -1e30)
        raised = jnp.maximum(m, jnp.max(scores, axis=1, keepdims=True))
        weights = jnp.exp2((scores - raised) * SCALE).astype(jnp.bfloat16)
        factor = jnp.exp2((m - raised) * SCALE)
        acc = acc * factor + jnp.dot(weights, values[at, :], preferred_element_type=jnp.float32)
        m = raised
    if not last:
        acc_out[...] = acc
        m_out[...] = jnp.broadcast_to(m, (CHUNK, HEAD))
        return
    totals = acc[:, HEAD:]
    out[...] = (acc[:, :HEAD] / totals).astype(jnp.bfloat16)
    lse = m * SCALE + jnp.log2(totals)
    for k in range(CHUNK // ROWS):
        lse_out[step * (CHUNK // ROWS) + k] = row_of(lse[k * ROWS : (k + 1) * ROWS, :])


def attend(place, rc, query, pieces, cached, fresh, state=None, last=False):
    rows = query.shape[0]
    total = 2 * ROWS * (len(cached) + len(fresh))
    row_spec = pl.BlockSpec((CHUNK, HEAD), lambda i, s: (i, 0))
    wide_spec = pl.BlockSpec((CHUNK, 2 * HEAD), lambda i, s: (i, 0))
    in_specs = [row_spec] + [pl.BlockSpec(p.shape, lambda i, s: (0, 0, 0)) for p in pieces]
    args = [query, *pieces]
    if state is not None:
        in_specs += [wide_spec, row_spec]
        args += list(state)
    if last:
        out_specs = [row_spec, pl.BlockSpec((rows // ROWS, 1, ROWS), lambda i, s: (0, 0, 0))]
        out_shape = (
            jax.ShapeDtypeStruct((rows, HEAD), jnp.bfloat16),
            jax.ShapeDtypeStruct((rows // ROWS, 1, ROWS), jnp.float32),
        )
    else:
        out_specs = [wide_spec, row_spec]
        out_shape = (
            jax.ShapeDtypeStruct((rows, 2 * HEAD), jnp.float32),
            jax.ShapeDtypeStruct((rows, HEAD), jnp.float32),
        )
    return pl.pallas_call(
        functools.partial(attend_kernel, cached, fresh, state is None, last, rc),
        grid_spec=pltpu.PrefetchScalarGridSpec(
            num_scalar_prefetch=1,
            grid=(rows // CHUNK,),
            in_specs=in_specs,
            out_specs=out_specs,
            scratch_shapes=[
                pltpu.VMEM((HEAD, total), jnp.bfloat16),
                pltpu.VMEM((total, 2 * HEAD), jnp.bfloat16),
            ],
        ),
        out_shape=out_shape,
        compiler_params=params(),
        name="attend",
        cost_estimate=pl.CostEstimate(
            flops=4 * rows * total * HEAD,
            bytes_accessed=8 * rows * HEAD + 4 * total * HEAD,
            transcendentals=rows * total,
        ),
    )(place, *args)


def merge_weight(first_lse, second_lse):
    top = jnp.maximum(first_lse, second_lse)
    a, b = jnp.exp2(first_lse - top), jnp.exp2(second_lse - top)
    return a / (a + b), top + jnp.log2(a + b)


def merged(first, second, weight):
    a, b = first.astype(jnp.float32), second.astype(jnp.float32)
    share = column_of(weight)
    return (a * share + b * (1.0 - share)).astype(jnp.bfloat16)


def merge_kernel(own, own_lse, other, other_lse, out, lse_out):
    for k in range(own.shape[0] // ROWS):
        at = slice(k * ROWS, (k + 1) * ROWS)
        weight, lse = merge_weight(own_lse[k], other_lse[k])
        out[at, :] = merged(own[at, :], other[at, :], weight)
        lse_out[k] = lse


def merge_last_kernel(own, own_lse, other, other_lse, out):
    for y in range(2):
        for g in range(GROUP):
            k, j = y * GROUP + g, (1 - y) * GROUP + g
            weight, _ = merge_weight(own_lse[k], other_lse[j])
            out[y, :, g * HEAD : (g + 1) * HEAD] = merged(
                own[k * ROWS : (k + 1) * ROWS, :], other[j * ROWS : (j + 1) * ROWS, :], weight
            )


MERGE_COST = pl.CostEstimate(flops=2_000_000, bytes_accessed=1_600_000, transcendentals=4096)


def merge(own, own_lse, other, other_lse):
    return pl.pallas_call(
        merge_kernel,
        out_shape=(
            jax.ShapeDtypeStruct(own.shape, own.dtype),
            jax.ShapeDtypeStruct(own_lse.shape, own_lse.dtype),
        ),
        compiler_params=params(),
        name="merge",
        cost_estimate=MERGE_COST,
    )(own, own_lse, other, other_lse)


def merge_last(own, own_lse, other, other_lse):
    return pl.pallas_call(
        merge_last_kernel,
        out_shape=jax.ShapeDtypeStruct((2, ROWS, GROUP * HEAD), jnp.bfloat16),
        compiler_params=params(),
        name="merge_last",
        cost_estimate=MERGE_COST,
    )(own, own_lse, other, other_lse)


def project_kernel(place, near, far, weights, out):
    yl, c = place[1], place[2]
    for rc, rows in ((0, near), (1, far)):
        lhs = rows[...].reshape(2 * ROWS, GROUP * HEAD)
        for target in range(Z):
            product = jnp.dot(lhs, weights[target], preferred_element_type=jnp.float32)
            product = product.astype(jnp.bfloat16)
            for ryl in range(2):
                q = (yl ^ ryl) * 2 + (c ^ rc)
                out[q, target] = product[ryl * ROWS : (ryl + 1) * ROWS, :]


def project(place, near, far, weights):
    vmem = pl.BlockSpec(memory_space=pltpu.VMEM)
    columns = weights.shape[2]
    return pl.pallas_call(
        project_kernel,
        in_specs=[pl.BlockSpec(memory_space=pltpu.SMEM)] + [vmem] * 3,
        out_specs=vmem,
        out_shape=jax.ShapeDtypeStruct((4, Z, ROWS, columns), jnp.bfloat16),
        compiler_params=params(),
        name="project",
        cost_estimate=pl.CostEstimate(
            flops=2 * 4 * ROWS * GROUP * HEAD * Z * columns,
            bytes_accessed=7_000_000,
            transcendentals=0,
        ),
    )(place, near, far, weights)


PAD = 16


def third_kernel(place, received, hidden, gain, near, far, out, partial, scaled):
    c = place[2]
    columns = received.shape[3]
    squares = jnp.zeros((ROWS, columns), jnp.float32)
    for q in range(4):
        at = slice(q * columns, (q + 1) * columns)
        total = received[q, 0].astype(jnp.float32)
        for h in range(1, Z):
            total = total + received[q, h].astype(jnp.float32)
        result = (hidden[:, at].astype(jnp.float32) + total).astype(jnp.bfloat16)
        out[:, at] = result
        wide = result.astype(jnp.float32)
        squares = squares + wide * wide
        scaled[q // 2, :, (q % 2) * columns : (q % 2 + 1) * columns] = (
            wide * gain[:, at]
        ).astype(jnp.bfloat16)
    squares = jnp.sum(squares, axis=1, keepdims=True)
    row = row_of(jnp.broadcast_to(squares, (ROWS, ROWS)))
    high = row.astype(jnp.bfloat16)
    low = (row - high.astype(jnp.float32)).astype(jnp.bfloat16)
    tail = jnp.broadcast_to(
        jnp.concatenate([high, low], axis=1).astype(jnp.float32), (PAD, 2 * ROWS)
    ).astype(jnp.bfloat16)
    near_rows, far_rows = scaled[c], scaled[1 - c]
    for h in range(Z):
        product = jnp.dot(near_rows, near[h], preferred_element_type=jnp.float32) + jnp.dot(
            far_rows, far[h], preferred_element_type=jnp.float32
        )
        partial[h, :ROWS, :] = product.astype(jnp.bfloat16)
        partial[h, ROWS:, :] = tail


def third_partials(place, received, hidden, gain, near, far):
    vmem = pl.BlockSpec(memory_space=pltpu.VMEM)
    width = hidden.shape[1]
    return pl.pallas_call(
        third_kernel,
        in_specs=[pl.BlockSpec(memory_space=pltpu.SMEM)] + [vmem] * 5,
        out_specs=(vmem, vmem),
        out_shape=(
            jax.ShapeDtypeStruct(hidden.shape, jnp.bfloat16),
            jax.ShapeDtypeStruct((Z, ROWS + PAD, 2 * HEAD), jnp.bfloat16),
        ),
        scratch_shapes=[pltpu.VMEM((2, ROWS, width // 2), jnp.bfloat16)],
        compiler_params=params(),
        name="third",
    )(place, received, hidden, gain, near, far)


def final_kernel(count, partial, bias, cosine, sine, index, out):
    total = partial[0, :ROWS, :].astype(jnp.float32)
    tail = partial[0, ROWS:, :].astype(jnp.float32)
    for h in range(1, Z):
        total = total + partial[h, :ROWS, :].astype(jnp.float32)
        tail = tail + partial[h, ROWS:, :].astype(jnp.float32)
    squares = tail[0:1, :ROWS] + tail[0:1, ROWS:]
    factor = lax.rsqrt(column_of(squares) / MODEL_WIDTH + 1e-06)
    keys = total[:, :HEAD] * factor + bias[:, :HEAD]
    values = total[:, HEAD:] * factor + bias[:, HEAD:]
    keys = rotated(keys, cosine[...], sine[...])
    rows = jnp.concatenate([keys, values], axis=1).astype(jnp.bfloat16)
    slot = lax.broadcasted_iota(jnp.int32, (ROWS, ROWS), 1)
    token = lax.broadcasted_iota(jnp.int32, (ROWS, ROWS), 0)
    chosen = (token == index[...]) & (slot < count[0])
    pick = jnp.where(chosen, 1.0, 0.0).astype(jnp.bfloat16)
    out[...] = lax.dot_general(
        pick, rows, (((0,), (0,)), ((), ())), preferred_element_type=jnp.float32
    ).astype(jnp.bfloat16)


def final(count, partial, bias, cosine, sine, index):
    vmem = pl.BlockSpec(memory_space=pltpu.VMEM)
    return pl.pallas_call(
        final_kernel,
        in_specs=[pl.BlockSpec(memory_space=pltpu.SMEM)] + [vmem] * 5,
        out_specs=vmem,
        out_shape=jax.ShapeDtypeStruct((ROWS, 2 * HEAD), jnp.bfloat16),
        compiler_params=params(),
        name="final",
    )(count, partial, bias, cosine, sine, index)


def swap(x, axis):
    return lax.ppermute(x, axis, [(0, 1), (1, 0)])


def along_z(x, distance):
    return lax.ppermute(x, "z", [(i, (i + distance) % Z) for i in range(Z)])


def after(x, *others):
    return lax.optimization_barrier((x, others))[0]


def step(pair):
    return [along_z(pair[0], 1), along_z(pair[1], -1)]


def local(
    hidden,
    query,
    fresh_key_value,
    cached_key_value,
    positions,
    out_weight,
    norm_gain,
    layer3_key_value_weight,
    layer3_key_value_bias,
    keep_index,
    keep_count,
):
    z, yl, c = lax.axis_index("z"), lax.axis_index("yl"), lax.axis_index("c")
    place = jnp.stack([z, yl, c]).astype(jnp.int32)

    cosine, sine = tables(positions, HEAD)
    rotated_query, kv, third_rows = prepare(
        place,
        query,
        fresh_key_value,
        cached_key_value,
        cosine,
        sine,
        layer3_key_value_weight.reshape(Z, 2, MODEL_WIDTH // Z // 2, 2 * HEAD),
    )
    rotated_query = rotated_query.reshape(GROUP * ROWS, HEAD)
    near_query = jnp.concatenate([rotated_query, swap(rotated_query, "yl")], axis=0)
    far_query = swap(near_query, "c")
    weights = lax.all_gather(out_weight, "z")
    kv_1 = list(after(step([kv, kv]), near_query))
    kv_2 = step(kv_1)
    kv_3 = step(kv_2)
    early = [kv, *kv_1, *kv_2]
    early_cached = [(i, i) for i in range(5)]
    early_fresh = [[(0, 0, 0), (1, 1, -1)], [(2, 2, 1), (3, 3, -2)]]
    late_cached = [(1, 1), (2, 2), (3, 3)]
    late_fresh = [[(0, 0, 2), (1, 1, -3)], [(2, 2, 3), (3, 3, 4)]]
    near_state = attend(place, 0, near_query, early, early_cached, early_fresh)
    kv_3 = list(after(kv_3, near_state))
    late = [kv_2[1], *kv_3, along_z(kv_3[0], 1)]
    far_query = after(far_query, near_state)
    third_rows = after(third_rows, *kv_3)
    third_near = lax.all_to_all(third_rows, HEAD_AXES, 0, 0, tiled=True)
    third_far = swap(third_near, "c")
    far_state = attend(place, 1, far_query, early, early_cached, early_fresh)
    send, send_lse = attend(place, 1, far_query, late, late_cached, late_fresh, far_state, True)
    got, got_lse = swap(send, "c"), swap(send_lse, "c")
    own, own_lse = attend(place, 0, near_query, late, late_cached, late_fresh, near_state, True)
    own, own_lse = merge(own, own_lse, got, got_lse)
    got, got_lse = swap(own, "yl"), swap(own_lse, "yl")
    got_lse = after(got_lse, third_near)
    near = merge_last(own, own_lse, got, got_lse)
    far = swap(near, "c")

    products = project(place, near, far, weights)
    products = products.reshape(4 * Z, *products.shape[2:])
    received = lax.all_to_all(products, ("yl", "c", "x", "yh"), 0, 0, tiled=True)
    received = received.reshape(4, Z, *received.shape[1:])

    layer2_out, partial = third_partials(
        place, received, hidden, norm_gain.reshape(1, -1), third_near, third_far
    )
    partial = lax.all_to_all(partial, HEAD_AXES, 0, 0, tiled=True)
    packed = final(
        keep_count,
        partial,
        layer3_key_value_bias.reshape(1, -1),
        cosine,
        sine,
        keep_index.reshape(1, -1),
    )
    return (layer2_out, packed)


def solution(mesh):
    split = Mesh(mesh.devices.reshape(Z, 2, 2, 4, 2), CTX_AXES + HEAD_AXES)
    placed = (
        P(CTX_AXES, HEAD_AXES),
        P(CTX_AXES, HEAD_AXES),
        P(None, CTX_AXES, HEAD_AXES),
        P(None, CTX_AXES, HEAD_AXES),
        P(None, CTX_AXES),
        P(HEAD_AXES, CTX_AXES),
        P(HEAD_AXES),
        P(None, HEAD_AXES),
        P(HEAD_AXES),
        P(CTX_AXES),
        P(CTX_AXES),
    )
    return jax.shard_map(
        local,
        mesh=split,
        in_specs=placed,
        out_specs=(P(CTX_AXES, HEAD_AXES), P(CTX_AXES, HEAD_AXES)),
        check_vma=False,
    )
```

```python
import functools

import jax
import jax.numpy as jnp
from jax import lax
from jax.experimental import pallas as pl
from jax.experimental.pallas import tpu as pltpu
from jax.sharding import Mesh
from jax.sharding import PartitionSpec as P

MODEL_WIDTH = 8192
HEAD = 128
ROWS = 128
CACHED = 256
GROUP = 8
Z = 8
LOG2E = 1.4426950408889634
SCALE = HEAD ** (-0.5) * LOG2E
CTX_AXES = ("z", "yl", "c")
HEAD_AXES = ("x", "yh")
VMEM = 56 * 1024 * 1024
CHUNK = 512
DISTANCES = (0, -1, 1, -2, 2, -3, 3, 4)
BLOCKS = 3


def params(**more):
    return pltpu.CompilerParams(vmem_limit_bytes=VMEM, **more)


def tables(positions, head_size):
    half = head_size // 2
    column = jnp.arange(half)
    frequency = jnp.power(jnp.float32(1000000.0), -(2.0 * column.astype(jnp.float32)) / head_size)
    section = (column >= head_size // 8).astype(jnp.int32) + (
        column >= head_size // 8 + 3 * head_size // 16
    ).astype(jnp.int32)
    places = positions.astype(jnp.float32)
    chosen = jnp.where(
        section[None, :] == 0,
        places[0][:, None],
        jnp.where(section[None, :] == 1, places[1][:, None], places[2][:, None]),
    )
    angles = chosen * frequency[None, :]
    cosine, sine = jnp.cos(angles), jnp.sin(angles)
    return (
        jnp.concatenate([cosine, cosine], axis=1),
        jnp.concatenate([-sine, sine], axis=1),
    )


def rotated(x, cosine, sine):
    return x * cosine + pltpu.roll(x, HEAD // 2, 1) * sine


def prepare_kernel(
    place, query, fresh, cached, cosine, sine, weight, query_out, kv_out, weight_out, sem
):
    copy = pltpu.make_async_copy(weight.at[:, place[2]], weight_out, sem)
    copy.start()
    cos, sin = cosine[...], sine[...]
    for g in range(GROUP):
        piece = query[:, g * HEAD : (g + 1) * HEAD].astype(jnp.float32)
        query_out[g] = rotated(piece, cos, sin).astype(jnp.bfloat16)
    for k in range(CACHED // ROWS):
        kv_out[k] = jnp.transpose(cached[0, k * ROWS : (k + 1) * ROWS, :])
        kv_out[BLOCKS + k] = cached[1, k * ROWS : (k + 1) * ROWS, :]
    new_key = rotated(fresh[0].astype(jnp.float32), cos, sin).astype(jnp.bfloat16)
    kv_out[BLOCKS - 1] = jnp.transpose(new_key)
    kv_out[2 * BLOCKS - 1] = fresh[1]
    copy.wait()


def prepare(place, query, fresh, cached, cosine, sine, weight):
    vmem = pl.BlockSpec(memory_space=pltpu.VMEM)
    return pl.pallas_call(
        prepare_kernel,
        in_specs=[pl.BlockSpec(memory_space=pltpu.SMEM)]
        + [vmem] * 5
        + [pl.BlockSpec(memory_space=pl.ANY)],
        out_specs=(vmem, vmem, vmem),
        out_shape=(
            jax.ShapeDtypeStruct((GROUP, ROWS, HEAD), jnp.bfloat16),
            jax.ShapeDtypeStruct((2 * BLOCKS, ROWS, HEAD), jnp.bfloat16),
            jax.ShapeDtypeStruct((Z, *weight.shape[2:]), jnp.bfloat16),
        ),
        scratch_shapes=[pltpu.SemaphoreType.DMA],
        compiler_params=params(),
        name="prepare",
        cost_estimate=pl.CostEstimate(flops=2_000_000, bytes_accessed=5_500_000, transcendentals=0),
    )(place, query, fresh, cached, cosine, sine, weight)


def column_of(row):
    return jnp.transpose(jnp.broadcast_to(row, (ROWS, ROWS)))


def row_of(column):
    return jnp.transpose(column)[0:1, :]


def attend_kernel(cached, fresh, n_queries, first, last, first_rc, place, *refs):
    n_in = 1 + max([max(k, v) for k, v in cached] + [max(p[0], p[1]) for pair in fresh for p in pair])
    queries, refs = refs[:n_queries], refs[n_queries:]
    pieces, rest = refs[:n_in], list(refs[n_in:])
    if not first:
        acc_in, m_in = rest[:2]
        rest = rest[2:]
    if last:
        out, lse_out = rest[:2]
    else:
        acc_out, m_out = rest[:2]
    keys, values, query = rest[2:]
    step = pl.program_id(0)
    each = pl.num_programs(0) // n_queries
    for k, ref in enumerate(queries):

        @pl.when(step // each == k)
        def _():
            query[...] = ref[...]

    which = step // each
    rc, ryl = first_rc + which // 2, lax.rem(which, 2)
    z, yl, c = place[0], place[1], place[2]
    steps = len(cached) + len(fresh)

    @pl.when(step == 0)
    def _():
        at = 0
        for kp, vp in cached:
            for k in range(2):
                keys[:, at : at + ROWS] = pieces[kp][k]
                values[at : at + ROWS, :HEAD] = pieces[vp][BLOCKS + k]
                at += ROWS
        for pair in fresh:
            for kp, vp, _ in pair:
                keys[:, at : at + ROWS] = pieces[kp][BLOCKS - 1]
                values[at : at + ROWS, :HEAD] = pieces[vp][2 * BLOCKS - 1]
                at += ROWS
        values[:, HEAD:] = jnp.ones((steps * 2 * ROWS, HEAD), jnp.bfloat16)

    block = z * 4 + (yl ^ ryl) * 2 + (c ^ rc)
    inside = lax.broadcasted_iota(jnp.int32, (CHUNK, 1), 0) & (ROWS - 1)
    query_token = block * ROWS + inside
    lane = lax.broadcasted_iota(jnp.int32, (1, 2 * ROWS), 1)
    q = query[...]
    if first:
        m = jnp.full((CHUNK, 1), -1e30, jnp.float32)
        acc = jnp.zeros((CHUNK, 2 * HEAD), jnp.float32)
    else:
        m = jnp.max(m_in[...], axis=1, keepdims=True)
        acc = acc_in[...]
    for i in range(steps):
        at = slice(i * 2 * ROWS, (i + 1) * 2 * ROWS)
        scores = jnp.dot(q, keys[:, at], preferred_element_type=jnp.float32)
        if i >= len(cached):
            one, two = (
                (lax.rem(z + p[2] + Z, Z) * 4 + yl * 2 + c) * ROWS for p in fresh[i - len(cached)]
            )
            key_token = jnp.where(lane < ROWS, one + lane, two + lane - ROWS)
            scores = jnp.where(key_token <= query_token, scores, -1e30)
        raised = jnp.maximum(m, jnp.max(scores, axis=1, keepdims=True))
        weights = jnp.exp2((scores - raised) * SCALE).astype(jnp.bfloat16)
        factor = jnp.exp2((m - raised) * SCALE)
        acc = acc * factor + jnp.dot(weights, values[at, :], preferred_element_type=jnp.float32)
        m = raised
    if not last:
        acc_out[...] = acc
        m_out[...] = jnp.broadcast_to(m, (CHUNK, HEAD))
        return
    totals = acc[:, HEAD:]
    out[...] = (acc[:, :HEAD] / totals).astype(jnp.bfloat16)
    lse = m * SCALE + jnp.log2(totals)
    for k in range(CHUNK // ROWS):
        lse_out[step * (CHUNK // ROWS) + k] = row_of(lse[k * ROWS : (k + 1) * ROWS, :])


def attend(place, queries, first_rc, pieces, cached, fresh, state=None, offset=0, last=False):
    each = queries[0].shape[0] // CHUNK
    rows = each * len(queries) * CHUNK
    total = 2 * ROWS * (len(cached) + len(fresh))
    first_block = offset // CHUNK

    def query_spec(k):
        return pl.BlockSpec(
            (CHUNK, HEAD), lambda i, s: (jnp.clip(i - k * each, 0, each - 1), 0)
        )

    row_spec = pl.BlockSpec((CHUNK, HEAD), lambda i, s: (i, 0))
    in_specs = [query_spec(k) for k in range(len(queries))]
    in_specs += [pl.BlockSpec(p.shape, lambda i, s: (0, 0, 0)) for p in pieces]
    args = [*queries, *pieces]
    if state is not None:
        in_specs += [
            pl.BlockSpec((CHUNK, 2 * HEAD), lambda i, s: (i + first_block, 0)),
            pl.BlockSpec((CHUNK, HEAD), lambda i, s: (i + first_block, 0)),
        ]
        args += list(state)
    if last:
        out_specs = [row_spec, pl.BlockSpec((rows // ROWS, 1, ROWS), lambda i, s: (0, 0, 0))]
        out_shape = (
            jax.ShapeDtypeStruct((rows, HEAD), jnp.bfloat16),
            jax.ShapeDtypeStruct((rows // ROWS, 1, ROWS), jnp.float32),
        )
    else:
        out_specs = [pl.BlockSpec((CHUNK, 2 * HEAD), lambda i, s: (i, 0)), row_spec]
        out_shape = (
            jax.ShapeDtypeStruct((rows, 2 * HEAD), jnp.float32),
            jax.ShapeDtypeStruct((rows, HEAD), jnp.float32),
        )
    return pl.pallas_call(
        functools.partial(
            attend_kernel, cached, fresh, len(queries), state is None, last, first_rc
        ),
        grid_spec=pltpu.PrefetchScalarGridSpec(
            num_scalar_prefetch=1,
            grid=(rows // CHUNK,),
            in_specs=in_specs,
            out_specs=out_specs,
            scratch_shapes=[
                pltpu.VMEM((HEAD, total), jnp.bfloat16),
                pltpu.VMEM((total, 2 * HEAD), jnp.bfloat16),
                pltpu.VMEM((CHUNK, HEAD), jnp.bfloat16),
            ],
        ),
        out_shape=out_shape,
        compiler_params=params(),
        name="attend",
        cost_estimate=pl.CostEstimate(
            flops=4 * rows * total * HEAD,
            bytes_accessed=8 * rows * HEAD + 4 * total * HEAD,
            transcendentals=rows * total,
        ),
    )(place, *args)


def merge_weight(first_lse, second_lse):
    top = jnp.maximum(first_lse, second_lse)
    a, b = jnp.exp2(first_lse - top), jnp.exp2(second_lse - top)
    return a / (a + b), top + jnp.log2(a + b)


def merged(first, second, weight):
    a, b = first.astype(jnp.float32), second.astype(jnp.float32)
    share = column_of(weight)
    return (a * share + b * (1.0 - share)).astype(jnp.bfloat16)


def merge_kernel(own, own_lse, other, other_lse, out, lse_out):
    for k in range(own.shape[0] // ROWS):
        at = slice(k * ROWS, (k + 1) * ROWS)
        weight, lse = merge_weight(own_lse[k], other_lse[k])
        out[at, :] = merged(own[at, :], other[at, :], weight)
        lse_out[k] = lse


def merge_last_kernel(own, own_lse, other, other_lse, out):
    for y in range(2):
        for g in range(GROUP):
            k, j = y * GROUP + g, (1 - y) * GROUP + g
            weight, _ = merge_weight(own_lse[k], other_lse[j])
            out[y, :, g * HEAD : (g + 1) * HEAD] = merged(
                own[k * ROWS : (k + 1) * ROWS, :], other[j * ROWS : (j + 1) * ROWS, :], weight
            )


MERGE_COST = pl.CostEstimate(flops=2_000_000, bytes_accessed=1_600_000, transcendentals=4096)


def merge(own, own_lse, other, other_lse):
    return pl.pallas_call(
        merge_kernel,
        out_shape=(
            jax.ShapeDtypeStruct(own.shape, own.dtype),
            jax.ShapeDtypeStruct(own_lse.shape, own_lse.dtype),
        ),
        compiler_params=params(),
        name="merge",
        cost_estimate=MERGE_COST,
    )(own, own_lse, other, other_lse)


def merge_last(own, own_lse, other, other_lse):
    return pl.pallas_call(
        merge_last_kernel,
        out_shape=jax.ShapeDtypeStruct((2, ROWS, GROUP * HEAD), jnp.bfloat16),
        compiler_params=params(),
        name="merge_last",
        cost_estimate=MERGE_COST,
    )(own, own_lse, other, other_lse)


def project_kernel(place, near, far, *refs):
    weights, out, rows = refs[:Z], refs[Z], refs[Z + 1]
    z, yl, c = place[0], place[1], place[2]
    for ryl in range(2):
        rows[ryl * ROWS : (ryl + 1) * ROWS, :] = near[ryl]
        rows[(2 + ryl) * ROWS : (3 + ryl) * ROWS, :] = far[ryl]
    lhs = rows[...]
    for weight, distance in zip(weights, DISTANCES):
        product = jnp.dot(lhs, weight[...], preferred_element_type=jnp.float32)
        product = product.astype(jnp.bfloat16)
        target = lax.rem(z + distance + Z, Z)
        for k in range(4):
            q = (yl ^ (k % 2)) * 2 + (c ^ (k // 2))
            out[q, target] = product[k * ROWS : (k + 1) * ROWS, :]


def project(place, near, far, weights):
    vmem = pl.BlockSpec(memory_space=pltpu.VMEM)
    columns = weights[0].shape[1]
    return pl.pallas_call(
        project_kernel,
        in_specs=[pl.BlockSpec(memory_space=pltpu.SMEM)] + [vmem] * (2 + Z),
        out_specs=vmem,
        out_shape=jax.ShapeDtypeStruct((4, Z, ROWS, columns), jnp.bfloat16),
        scratch_shapes=[pltpu.VMEM((4 * ROWS, GROUP * HEAD), jnp.bfloat16)],
        compiler_params=params(),
        name="project",
        cost_estimate=pl.CostEstimate(
            flops=2 * 4 * ROWS * GROUP * HEAD * Z * columns,
            bytes_accessed=7_000_000,
            transcendentals=0,
        ),
    )(place, near, far, *weights)


PAD = 16


def third_kernel(place, received, hidden, gain, near, far, out, partial, scaled):
    c = place[2]
    columns = received.shape[3]
    squares = jnp.zeros((ROWS, columns), jnp.float32)
    for q in range(4):
        at = slice(q * columns, (q + 1) * columns)
        total = received[q, 0].astype(jnp.float32)
        for h in range(1, Z):
            total = total + received[q, h].astype(jnp.float32)
        result = (hidden[:, at].astype(jnp.float32) + total).astype(jnp.bfloat16)
        out[:, at] = result
        wide = result.astype(jnp.float32)
        squares = squares + wide * wide
        scaled[q // 2, :, (q % 2) * columns : (q % 2 + 1) * columns] = (
            wide * gain[:, at]
        ).astype(jnp.bfloat16)
    squares = jnp.sum(squares, axis=1, keepdims=True)
    row = row_of(jnp.broadcast_to(squares, (ROWS, ROWS)))
    high = row.astype(jnp.bfloat16)
    low = (row - high.astype(jnp.float32)).astype(jnp.bfloat16)
    tail = jnp.broadcast_to(
        jnp.concatenate([high, low], axis=1).astype(jnp.float32), (PAD, 2 * ROWS)
    ).astype(jnp.bfloat16)
    near_rows, far_rows = scaled[c], scaled[1 - c]
    for h in range(Z):
        product = jnp.dot(near_rows, near[h], preferred_element_type=jnp.float32) + jnp.dot(
            far_rows, far[h], preferred_element_type=jnp.float32
        )
        partial[h, :ROWS, :] = product.astype(jnp.bfloat16)
        partial[h, ROWS:, :] = tail


def third_partials(place, received, hidden, gain, near, far):
    vmem = pl.BlockSpec(memory_space=pltpu.VMEM)
    width = hidden.shape[1]
    return pl.pallas_call(
        third_kernel,
        in_specs=[pl.BlockSpec(memory_space=pltpu.SMEM)] + [vmem] * 5,
        out_specs=(vmem, vmem),
        out_shape=(
            jax.ShapeDtypeStruct(hidden.shape, jnp.bfloat16),
            jax.ShapeDtypeStruct((Z, ROWS + PAD, 2 * HEAD), jnp.bfloat16),
        ),
        scratch_shapes=[pltpu.VMEM((2, ROWS, width // 2), jnp.bfloat16)],
        compiler_params=params(),
        name="third",
    )(place, received, hidden, gain, near, far)


def final_kernel(count, partial, bias, cosine, sine, index, out):
    total = partial[0, :ROWS, :].astype(jnp.float32)
    tail = partial[0, ROWS:, :].astype(jnp.float32)
    for h in range(1, Z):
        total = total + partial[h, :ROWS, :].astype(jnp.float32)
        tail = tail + partial[h, ROWS:, :].astype(jnp.float32)
    squares = tail[0:1, :ROWS] + tail[0:1, ROWS:]
    factor = lax.rsqrt(column_of(squares) / MODEL_WIDTH + 1e-06)
    keys = total[:, :HEAD] * factor + bias[:, :HEAD]
    values = total[:, HEAD:] * factor + bias[:, HEAD:]
    keys = rotated(keys, cosine[...], sine[...])
    rows = jnp.concatenate([keys, values], axis=1).astype(jnp.bfloat16)
    slot = lax.broadcasted_iota(jnp.int32, (ROWS, ROWS), 1)
    token = lax.broadcasted_iota(jnp.int32, (ROWS, ROWS), 0)
    chosen = (token == index[...]) & (slot < count[0])
    pick = jnp.where(chosen, 1.0, 0.0).astype(jnp.bfloat16)
    out[...] = lax.dot_general(
        pick, rows, (((0,), (0,)), ((), ())), preferred_element_type=jnp.float32
    ).astype(jnp.bfloat16)


def final(count, partial, bias, cosine, sine, index):
    vmem = pl.BlockSpec(memory_space=pltpu.VMEM)
    return pl.pallas_call(
        final_kernel,
        in_specs=[pl.BlockSpec(memory_space=pltpu.SMEM)] + [vmem] * 5,
        out_specs=vmem,
        out_shape=jax.ShapeDtypeStruct((ROWS, 2 * HEAD), jnp.bfloat16),
        compiler_params=params(),
        name="final",
    )(count, partial, bias, cosine, sine, index)


def swap(x, axis):
    return lax.ppermute(x, axis, [(0, 1), (1, 0)])


def along_z(x, distance):
    return lax.ppermute(x, "z", [(i, (i + distance) % Z) for i in range(Z)])


def after(x, *others):
    return lax.optimization_barrier((x, others))[0]


def step(pair):
    return [along_z(pair[0], 1), along_z(pair[1], -1)]


def local(
    hidden,
    query,
    fresh_key_value,
    cached_key_value,
    positions,
    out_weight,
    norm_gain,
    layer3_key_value_weight,
    layer3_key_value_bias,
    keep_index,
    keep_count,
):
    z, yl, c = lax.axis_index("z"), lax.axis_index("yl"), lax.axis_index("c")
    place = jnp.stack([z, yl, c]).astype(jnp.int32)

    cosine, sine = tables(positions, HEAD)
    rotated_query, kv, third_rows = prepare(
        place,
        query,
        fresh_key_value,
        cached_key_value,
        cosine,
        sine,
        layer3_key_value_weight.reshape(Z, 2, MODEL_WIDTH // Z // 2, 2 * HEAD),
    )
    rotated_query = rotated_query.reshape(GROUP * ROWS, HEAD)
    across = swap(rotated_query, "yl")
    other_core = swap(rotated_query, "c")
    kv_1, across = lax.optimization_barrier((step([kv, kv]), across))
    near_query, far_query = [rotated_query, across], [other_core, swap(across, "c")]
    own_weight = after(out_weight, *kv_1)
    weights_1 = step([own_weight, own_weight])
    state = attend(
        place,
        near_query + far_query,
        0,
        [kv, *kv_1],
        [(0, 0), (1, 1), (2, 2)],
        [[(0, 0, 0), (1, 1, -1)]],
    )
    kv_2 = list(after(step(kv_1), state))
    kv_3 = step(kv_2)
    near_query, far_query, kv_3, state, weights_1 = lax.optimization_barrier(
        (near_query, far_query, kv_3, state, weights_1)
    )
    weights_2 = step(weights_1)
    third_rows = after(third_rows, *kv_2)
    third_near = lax.all_to_all(third_rows, HEAD_AXES, 0, 0, tiled=True)
    third_far = swap(third_near, "c")
    kv_4 = along_z(kv_3[0], 1)
    state = attend(
        place,
        near_query + far_query,
        0,
        [kv_1[1], *kv_2],
        [(1, 1), (2, 2)],
        [[(0, 0, 1), (1, 1, -2)]],
        state,
    )
    kv_4, state = lax.optimization_barrier((kv_4, state))
    late = [kv_2[1], *kv_3, kv_4]
    late_cached = [(1, 1), (2, 2), (3, 3)]
    late_fresh = [[(0, 0, 2), (1, 1, -3)], [(2, 2, 3), (3, 3, 4)]]
    state = after(state, *weights_2)
    weights_3 = step(weights_2)
    send, send_lse = attend(
        place, far_query, 1, late, late_cached, late_fresh, state, 2 * GROUP * ROWS, True
    )
    got, got_lse = swap(send, "c"), swap(send_lse, "c")
    own, own_lse = attend(
        place, near_query, 0, late, late_cached, late_fresh, state, 0, True
    )
    got_lse = after(got_lse, *weights_3)
    own, own_lse = merge(own, own_lse, got, got_lse)
    got, got_lse = swap(own, "yl"), swap(own_lse, "yl")
    weights_4 = along_z(weights_3[0], 1)
    got_lse = after(got_lse, third_near)
    near = merge_last(own, own_lse, got, got_lse)
    far = swap(near, "c")
    weights = [out_weight, *weights_1, *weights_2, *weights_3, weights_4]

    products = project(place, near, far, weights)
    products = products.reshape(4 * Z, *products.shape[2:])
    received = lax.all_to_all(products, ("yl", "c", "x", "yh"), 0, 0, tiled=True)
    received = received.reshape(4, Z, *received.shape[1:])

    layer2_out, partial = third_partials(
        place, received, hidden, norm_gain.reshape(1, -1), third_near, third_far
    )
    partial = lax.all_to_all(partial, HEAD_AXES, 0, 0, tiled=True)
    packed = final(
        keep_count,
        partial,
        layer3_key_value_bias.reshape(1, -1),
        cosine,
        sine,
        keep_index.reshape(1, -1),
    )
    return (layer2_out, packed)


def solution(mesh):
    split = Mesh(mesh.devices.reshape(Z, 2, 2, 4, 2), CTX_AXES + HEAD_AXES)
    placed = (
        P(CTX_AXES, HEAD_AXES),
        P(CTX_AXES, HEAD_AXES),
        P(None, CTX_AXES, HEAD_AXES),
        P(None, CTX_AXES, HEAD_AXES),
        P(None, CTX_AXES),
        P(HEAD_AXES, CTX_AXES),
        P(HEAD_AXES),
        P(None, HEAD_AXES),
        P(HEAD_AXES),
        P(CTX_AXES),
        P(CTX_AXES),
    )
    return jax.shard_map(
        local,
        mesh=split,
        in_specs=placed,
        out_specs=(P(CTX_AXES, HEAD_AXES), P(CTX_AXES, HEAD_AXES)),
        check_vma=False,
    )
```

```python
import functools

import jax
import jax.numpy as jnp
from jax import lax
from jax.experimental import pallas as pl
from jax.experimental.pallas import tpu as pltpu
from jax.sharding import Mesh
from jax.sharding import PartitionSpec as P

MODEL_WIDTH = 8192
HEAD = 128
ROWS = 128
CACHED = 256
GROUP = 8
Z = 8
LOG2E = 1.4426950408889634
SCALE = HEAD ** (-0.5) * LOG2E
CTX_AXES = ("z", "yl", "c")
HEAD_AXES = ("x", "yh")
VMEM = 56 * 1024 * 1024
DISTANCES = (0, -1, 1, -2, 2, -3, 3, 4)
BLOCKS = 3


def params(**more):
    return pltpu.CompilerParams(vmem_limit_bytes=VMEM, **more)


def tables(positions, head_size):
    half = head_size // 2
    column = jnp.arange(half)
    frequency = jnp.power(jnp.float32(1000000.0), -(2.0 * column.astype(jnp.float32)) / head_size)
    section = (column >= head_size // 8).astype(jnp.int32) + (
        column >= head_size // 8 + 3 * head_size // 16
    ).astype(jnp.int32)
    places = positions.astype(jnp.float32)
    chosen = jnp.where(
        section[None, :] == 0,
        places[0][:, None],
        jnp.where(section[None, :] == 1, places[1][:, None], places[2][:, None]),
    )
    angles = chosen * frequency[None, :]
    cosine, sine = jnp.cos(angles), jnp.sin(angles)
    return (
        jnp.concatenate([cosine, cosine], axis=1),
        jnp.concatenate([-sine, sine], axis=1),
    )


def rotated(x, cosine, sine):
    return x * cosine + pltpu.roll(x, HEAD // 2, 1) * sine


def prepare_kernel(query, fresh, cached, cosine, sine, query_out, kv_out):
    cos, sin = cosine[...], sine[...]
    for g in range(GROUP):
        piece = query[:, g * HEAD : (g + 1) * HEAD].astype(jnp.float32)
        query_out[g] = rotated(piece, cos, sin).astype(jnp.bfloat16)
    for k in range(CACHED // ROWS):
        kv_out[k] = jnp.transpose(cached[0, k * ROWS : (k + 1) * ROWS, :])
        kv_out[BLOCKS + k] = cached[1, k * ROWS : (k + 1) * ROWS, :]
    new_key = rotated(fresh[0].astype(jnp.float32), cos, sin).astype(jnp.bfloat16)
    kv_out[BLOCKS - 1] = jnp.transpose(new_key)
    kv_out[2 * BLOCKS - 1] = fresh[1]


def prepare(query, fresh, cached, cosine, sine):
    return pl.pallas_call(
        prepare_kernel,
        out_shape=(
            jax.ShapeDtypeStruct((GROUP, ROWS, HEAD), jnp.bfloat16),
            jax.ShapeDtypeStruct((2 * BLOCKS, ROWS, HEAD), jnp.bfloat16),
        ),
        compiler_params=params(),
        name="prepare",
        cost_estimate=pl.CostEstimate(flops=2_000_000, bytes_accessed=1_500_000, transcendentals=0),
    )(query, fresh, cached, cosine, sine)


def half_kernel(place, weight, out):
    out[...] = weight[:, 0]


def weight_half(place, weight):
    rows, columns = weight.shape[2:]
    return pl.pallas_call(
        half_kernel,
        grid_spec=pltpu.PrefetchScalarGridSpec(
            num_scalar_prefetch=1,
            grid=(Z // 2,),
            in_specs=[pl.BlockSpec((2, 1, rows, columns), lambda i, s: (i, s[2], 0, 0))],
            out_specs=pl.BlockSpec((2, rows, columns), lambda i, s: (i, 0, 0)),
        ),
        out_shape=jax.ShapeDtypeStruct((Z, rows, columns), jnp.bfloat16),
        compiler_params=params(),
        name="half",
        cost_estimate=pl.CostEstimate(flops=0, bytes_accessed=8_000_000, transcendentals=0),
    )(place, weight)


def column_of(row):
    return jnp.transpose(jnp.broadcast_to(row, (ROWS, ROWS)))


def row_of(column):
    return jnp.transpose(column)[0:1, :]


def attend_kernel(chunk, cached, fresh, n_queries, first, last, first_rc, place, *refs):
    n_in = 1 + max([max(k, v) for k, v in cached] + [max(p[0], p[1]) for pair in fresh for p in pair])
    queries, refs = refs[:n_queries], refs[n_queries:]
    pieces, rest = refs[:n_in], list(refs[n_in:])
    if not first:
        acc_in, m_in = rest[:2]
        rest = rest[2:]
    if last:
        out, lse_out = rest[:2]
    else:
        acc_out, m_out = rest[:2]
    keys, values, query = rest[2:]
    step = pl.program_id(0)
    each = pl.num_programs(0) // n_queries
    for k, ref in enumerate(queries):

        @pl.when(step // each == k)
        def _():
            query[...] = ref[...]

    which = step // each
    rc, ryl = first_rc + which // 2, lax.rem(which, 2)
    z, yl, c = place[0], place[1], place[2]
    steps = len(cached) + len(fresh)

    @pl.when(step == 0)
    def _():
        at = 0
        for kp, vp in cached:
            for k in range(2):
                keys[:, at : at + ROWS] = pieces[kp][k]
                values[at : at + ROWS, :HEAD] = pieces[vp][BLOCKS + k]
                at += ROWS
        for pair in fresh:
            for kp, vp, _ in pair:
                keys[:, at : at + ROWS] = pieces[kp][BLOCKS - 1]
                values[at : at + ROWS, :HEAD] = pieces[vp][2 * BLOCKS - 1]
                at += ROWS
        values[:, HEAD:] = jnp.ones((steps * 2 * ROWS, HEAD), jnp.bfloat16)

    block = z * 4 + (yl ^ ryl) * 2 + (c ^ rc)
    inside = lax.broadcasted_iota(jnp.int32, (chunk, 1), 0) & (ROWS - 1)
    query_token = block * ROWS + inside
    lane = lax.broadcasted_iota(jnp.int32, (1, 2 * ROWS), 1)
    q = query[...]
    if first:
        m = jnp.full((chunk, 1), -1e30, jnp.float32)
        acc = jnp.zeros((chunk, 2 * HEAD), jnp.float32)
    else:
        m = jnp.max(m_in[...], axis=1, keepdims=True)
        acc = acc_in[...]
    for i in range(steps):
        at = slice(i * 2 * ROWS, (i + 1) * 2 * ROWS)
        scores = jnp.dot(q, keys[:, at], preferred_element_type=jnp.float32)
        if i >= len(cached):
            one, two = (
                (lax.rem(z + p[2] + Z, Z) * 4 + yl * 2 + c) * ROWS for p in fresh[i - len(cached)]
            )
            key_token = jnp.where(lane < ROWS, one + lane, two + lane - ROWS)
            scores = jnp.where(key_token <= query_token, scores, -1e30)
        raised = jnp.maximum(m, jnp.max(scores, axis=1, keepdims=True))
        weights = jnp.exp2((scores - raised) * SCALE).astype(jnp.bfloat16)
        factor = jnp.exp2((m - raised) * SCALE)
        acc = acc * factor + jnp.dot(weights, values[at, :], preferred_element_type=jnp.float32)
        m = raised
    if not last:
        acc_out[...] = acc
        m_out[...] = jnp.broadcast_to(m, (chunk, HEAD))
        return
    totals = acc[:, HEAD:]
    out[...] = (acc[:, :HEAD] / totals).astype(jnp.bfloat16)
    lse = m * SCALE + jnp.log2(totals)
    for k in range(chunk // ROWS):
        lse_out[step * (chunk // ROWS) + k] = row_of(lse[k * ROWS : (k + 1) * ROWS, :])


def attend(chunk, place, queries, first_rc, pieces, cached, fresh, state=None, offset=0, last=False):
    each = queries[0].shape[0] // chunk
    rows = each * len(queries) * chunk
    total = 2 * ROWS * (len(cached) + len(fresh))
    first_block = offset // chunk

    def query_spec(k):
        return pl.BlockSpec(
            (chunk, HEAD), lambda i, s: (jnp.clip(i - k * each, 0, each - 1), 0)
        )

    row_spec = pl.BlockSpec((chunk, HEAD), lambda i, s: (i, 0))
    in_specs = [query_spec(k) for k in range(len(queries))]
    in_specs += [pl.BlockSpec(p.shape, lambda i, s: (0, 0, 0)) for p in pieces]
    args = [*queries, *pieces]
    if state is not None:
        in_specs += [
            pl.BlockSpec((chunk, 2 * HEAD), lambda i, s: (i + first_block, 0)),
            pl.BlockSpec((chunk, HEAD), lambda i, s: (i + first_block, 0)),
        ]
        args += list(state)
    if last:
        out_specs = [row_spec, pl.BlockSpec((rows // ROWS, 1, ROWS), lambda i, s: (0, 0, 0))]
        out_shape = (
            jax.ShapeDtypeStruct((rows, HEAD), jnp.bfloat16),
            jax.ShapeDtypeStruct((rows // ROWS, 1, ROWS), jnp.float32),
        )
    else:
        out_specs = [pl.BlockSpec((chunk, 2 * HEAD), lambda i, s: (i, 0)), row_spec]
        out_shape = (
            jax.ShapeDtypeStruct((rows, 2 * HEAD), jnp.float32),
            jax.ShapeDtypeStruct((rows, HEAD), jnp.float32),
        )
    return pl.pallas_call(
        functools.partial(
            attend_kernel, chunk, cached, fresh, len(queries), state is None, last, first_rc
        ),
        grid_spec=pltpu.PrefetchScalarGridSpec(
            num_scalar_prefetch=1,
            grid=(rows // chunk,),
            in_specs=in_specs,
            out_specs=out_specs,
            scratch_shapes=[
                pltpu.VMEM((HEAD, total), jnp.bfloat16),
                pltpu.VMEM((total, 2 * HEAD), jnp.bfloat16),
                pltpu.VMEM((chunk, HEAD), jnp.bfloat16),
            ],
        ),
        out_shape=out_shape,
        compiler_params=params(),
        name="attend",
        cost_estimate=pl.CostEstimate(
            flops=4 * rows * total * HEAD,
            bytes_accessed=8 * rows * HEAD + 4 * total * HEAD,
            transcendentals=rows * total,
        ),
    )(place, *args)


def merge_weight(first_lse, second_lse):
    top = jnp.maximum(first_lse, second_lse)
    a, b = jnp.exp2(first_lse - top), jnp.exp2(second_lse - top)
    return a / (a + b), top + jnp.log2(a + b)


def merged(first, second, weight):
    a, b = first.astype(jnp.float32), second.astype(jnp.float32)
    share = column_of(weight)
    return (a * share + b * (1.0 - share)).astype(jnp.bfloat16)


def merge_kernel(own, own_lse, other, other_lse, out, lse_out):
    for k in range(own.shape[0] // ROWS):
        at = slice(k * ROWS, (k + 1) * ROWS)
        weight, lse = merge_weight(own_lse[k], other_lse[k])
        out[at, :] = merged(own[at, :], other[at, :], weight)
        lse_out[k] = lse


def merge_last_kernel(own, own_lse, other, other_lse, out):
    for y in range(2):
        for g in range(GROUP):
            k, j = y * GROUP + g, (1 - y) * GROUP + g
            weight, _ = merge_weight(own_lse[k], other_lse[j])
            out[y, :, g * HEAD : (g + 1) * HEAD] = merged(
                own[k * ROWS : (k + 1) * ROWS, :], other[j * ROWS : (j + 1) * ROWS, :], weight
            )


MERGE_COST = pl.CostEstimate(flops=2_000_000, bytes_accessed=1_600_000, transcendentals=4096)


def merge(own, own_lse, other, other_lse):
    return pl.pallas_call(
        merge_kernel,
        out_shape=(
            jax.ShapeDtypeStruct(own.shape, own.dtype),
            jax.ShapeDtypeStruct(own_lse.shape, own_lse.dtype),
        ),
        compiler_params=params(),
        name="merge",
        cost_estimate=MERGE_COST,
    )(own, own_lse, other, other_lse)


def merge_last(own, own_lse, other, other_lse):
    return pl.pallas_call(
        merge_last_kernel,
        out_shape=jax.ShapeDtypeStruct((2, ROWS, GROUP * HEAD), jnp.bfloat16),
        compiler_params=params(),
        name="merge_last",
        cost_estimate=MERGE_COST,
    )(own, own_lse, other, other_lse)


def project_kernel(place, near, far, *refs):
    weights, out, rows, held, products, in_sem, out_sem = refs[: Z + 1], *refs[Z + 1 :]
    z, yl, c = place[0], place[1], place[2]
    half = held.shape[1] // 2
    targets = [held.at[i] for i in range(Z - 1)]
    targets += [held.at[Z - 1, pl.ds(0, half)], held.at[Z - 1, pl.ds(half, half)]]
    copies = [
        pltpu.make_async_copy(weights[i], targets[i], in_sem.at[i]) for i in range(Z + 1)
    ]
    for copy in copies:
        copy.start()
    for ryl in range(2):
        rows[ryl * ROWS : (ryl + 1) * ROWS, :] = near[ryl]
        rows[(2 + ryl) * ROWS : (3 + ryl) * ROWS, :] = far[ryl]
    sent = []
    for i, distance in enumerate(DISTANCES):
        for copy in copies[i : i + 1 if i < Z - 1 else Z + 1]:
            copy.wait()
        product = jnp.dot(rows[...], held[i], preferred_element_type=jnp.float32)
        product = product.astype(jnp.bfloat16)
        for k in range(4):
            q = (yl ^ (k % 2)) * 2 + (c ^ (k // 2))
            products[i, q] = product[k * ROWS : (k + 1) * ROWS, :]
        target = lax.rem(z + distance + Z, Z)
        copy = pltpu.make_async_copy(products.at[i], out.at[:, target], out_sem.at[i])
        copy.start()
        sent.append(copy)
    for copy in sent:
        copy.wait()


def project(place, near, far, weights):
    vmem = pl.BlockSpec(memory_space=pltpu.VMEM)
    anywhere = pl.BlockSpec(memory_space=pl.ANY)
    depth, columns = weights[0].shape
    return pl.pallas_call(
        project_kernel,
        in_specs=[pl.BlockSpec(memory_space=pltpu.SMEM), vmem, vmem] + [anywhere] * (Z + 1),
        out_specs=anywhere,
        out_shape=jax.ShapeDtypeStruct((4, Z, ROWS, columns), jnp.bfloat16),
        scratch_shapes=[
            pltpu.VMEM((4 * ROWS, depth), jnp.bfloat16),
            pltpu.VMEM((Z, depth, columns), jnp.bfloat16),
            pltpu.VMEM((Z, 4, ROWS, columns), jnp.bfloat16),
            pltpu.SemaphoreType.DMA((Z + 1,)),
            pltpu.SemaphoreType.DMA((Z,)),
        ],
        compiler_params=params(),
        name="project",
        cost_estimate=pl.CostEstimate(
            flops=2 * 4 * ROWS * depth * Z * columns, bytes_accessed=7_000_000, transcendentals=0
        ),
    )(place, near, far, *weights)


PAD = 16


def third_kernel(place, received, hidden, gain, near, far, out, partial, scaled):
    c = place[2]
    columns = received.shape[3]
    squares = jnp.zeros((ROWS, columns), jnp.float32)
    for q in range(4):
        at = slice(q * columns, (q + 1) * columns)
        total = received[q, 0].astype(jnp.float32)
        for h in range(1, Z):
            total = total + received[q, h].astype(jnp.float32)
        result = (hidden[:, at].astype(jnp.float32) + total).astype(jnp.bfloat16)
        out[:, at] = result
        wide = result.astype(jnp.float32)
        squares = squares + wide * wide
        scaled[q // 2, :, (q % 2) * columns : (q % 2 + 1) * columns] = (
            wide * gain[:, at]
        ).astype(jnp.bfloat16)
    squares = jnp.sum(squares, axis=1, keepdims=True)
    row = row_of(jnp.broadcast_to(squares, (ROWS, ROWS)))
    high = row.astype(jnp.bfloat16)
    low = (row - high.astype(jnp.float32)).astype(jnp.bfloat16)
    tail = jnp.broadcast_to(
        jnp.concatenate([high, low], axis=1).astype(jnp.float32), (PAD, 2 * ROWS)
    ).astype(jnp.bfloat16)
    near_rows, far_rows = scaled[c], scaled[1 - c]
    for h in range(Z):
        product = jnp.dot(near_rows, near[h], preferred_element_type=jnp.float32) + jnp.dot(
            far_rows, far[h], preferred_element_type=jnp.float32
        )
        partial[h, :ROWS, :] = product.astype(jnp.bfloat16)
        partial[h, ROWS:, :] = tail


def third_partials(place, received, hidden, gain, near, far):
    vmem = pl.BlockSpec(memory_space=pltpu.VMEM)
    width = hidden.shape[1]
    return pl.pallas_call(
        third_kernel,
        in_specs=[pl.BlockSpec(memory_space=pltpu.SMEM)] + [vmem] * 5,
        out_specs=(vmem, vmem),
        out_shape=(
            jax.ShapeDtypeStruct(hidden.shape, jnp.bfloat16),
            jax.ShapeDtypeStruct((Z, ROWS + PAD, 2 * HEAD), jnp.bfloat16),
        ),
        scratch_shapes=[pltpu.VMEM((2, ROWS, width // 2), jnp.bfloat16)],
        compiler_params=params(),
        name="third",
    )(place, received, hidden, gain, near, far)


def final_kernel(count, partial, bias, cosine, sine, index, out):
    total = partial[0, :ROWS, :].astype(jnp.float32)
    tail = partial[0, ROWS:, :].astype(jnp.float32)
    for h in range(1, Z):
        total = total + partial[h, :ROWS, :].astype(jnp.float32)
        tail = tail + partial[h, ROWS:, :].astype(jnp.float32)
    squares = tail[0:1, :ROWS] + tail[0:1, ROWS:]
    factor = lax.rsqrt(column_of(squares) / MODEL_WIDTH + 1e-06)
    keys = total[:, :HEAD] * factor + bias[:, :HEAD]
    values = total[:, HEAD:] * factor + bias[:, HEAD:]
    keys = rotated(keys, cosine[...], sine[...])
    rows = jnp.concatenate([keys, values], axis=1).astype(jnp.bfloat16)
    slot = lax.broadcasted_iota(jnp.int32, (ROWS, ROWS), 1)
    token = lax.broadcasted_iota(jnp.int32, (ROWS, ROWS), 0)
    chosen = (token == index[...]) & (slot < count[0])
    pick = jnp.where(chosen, 1.0, 0.0).astype(jnp.bfloat16)
    out[...] = lax.dot_general(
        pick, rows, (((0,), (0,)), ((), ())), preferred_element_type=jnp.float32
    ).astype(jnp.bfloat16)


def final(count, partial, bias, cosine, sine, index):
    vmem = pl.BlockSpec(memory_space=pltpu.VMEM)
    return pl.pallas_call(
        final_kernel,
        in_specs=[pl.BlockSpec(memory_space=pltpu.SMEM)] + [vmem] * 5,
        out_specs=vmem,
        out_shape=jax.ShapeDtypeStruct((ROWS, 2 * HEAD), jnp.bfloat16),
        compiler_params=params(),
        name="final",
    )(count, partial, bias, cosine, sine, index)


def swap(x, axis):
    return lax.ppermute(x, axis, [(0, 1), (1, 0)])


def along_z(x, distance):
    return lax.ppermute(x, "z", [(i, (i + distance) % Z) for i in range(Z)])


def after(x, *others):
    return lax.optimization_barrier((x, others))[0]


def step(pair):
    return [along_z(pair[0], 1), along_z(pair[1], -1)]


def local(
    hidden,
    query,
    fresh_key_value,
    cached_key_value,
    positions,
    out_weight,
    norm_gain,
    layer3_key_value_weight,
    layer3_key_value_bias,
    keep_index,
    keep_count,
):
    z, yl, c = lax.axis_index("z"), lax.axis_index("yl"), lax.axis_index("c")
    place = jnp.stack([z, yl, c]).astype(jnp.int32)

    cosine, sine = tables(positions, HEAD)
    rotated_query, kv = prepare(query, fresh_key_value, cached_key_value, cosine, sine)
    third_rows = weight_half(
        place, layer3_key_value_weight.reshape(Z, 2, MODEL_WIDTH // Z // 2, 2 * HEAD)
    )
    rotated_query = rotated_query.reshape(GROUP * ROWS, HEAD)
    across = swap(rotated_query, "yl")
    other_core = swap(rotated_query, "c")
    kv_1, across, third_rows = lax.optimization_barrier((step([kv, kv]), across, third_rows))
    near_query, far_query = [rotated_query, across], [other_core, swap(across, "c")]
    own_weight = after(out_weight, *kv_1)
    weights_1 = step([own_weight, own_weight])
    state = attend(
        1024,
        place,
        near_query + far_query,
        0,
        [kv, *kv_1],
        [(0, 0), (1, 1), (2, 2)],
        [[(0, 0, 0), (1, 1, -1)]],
    )
    kv_2 = list(after(step(kv_1), state))
    kv_3, weights_1, state = lax.optimization_barrier((step(kv_2), weights_1, state))
    third_near = lax.all_to_all(third_rows, HEAD_AXES, 0, 0, tiled=True)
    third_far = swap(third_near, "c")
    weights_2 = step(weights_1)
    kv_4 = along_z(kv_3[0], 1)
    kv_4, state = lax.optimization_barrier((kv_4, state))
    late = [kv_1[1], *kv_2, *kv_3, kv_4]
    late_cached = [(i, i) for i in range(1, 6)]
    late_fresh = [[(0, 0, 1), (1, 1, -2)], [(2, 2, 2), (3, 3, -3)], [(4, 4, 3), (5, 5, 4)]]
    offset = 2 * GROUP * ROWS
    send, send_lse = attend(
        512, place, far_query, 1, late, late_cached, late_fresh, state, offset, True
    )
    got, got_lse = swap(send, "c"), swap(send_lse, "c")
    near_query, _, weights_2 = lax.optimization_barrier((near_query, send_lse, weights_2))
    weights_3 = step(weights_2)
    own, own_lse = attend(
        512, place, near_query, 0, late, late_cached, late_fresh, state, 0, True
    )
    own, own_lse = merge(own, own_lse, got, got_lse)
    got, got_lse = swap(own, "yl"), swap(own_lse, "yl")
    depth = out_weight.shape[0] // 2
    weights_4 = [along_z(weights_3[0][:depth], 1), along_z(weights_3[1][depth:], -1)]
    got_lse = after(got_lse, third_near, *weights_4)
    near = merge_last(own, own_lse, got, got_lse)
    far = swap(near, "c")
    weights = [out_weight, *weights_1, *weights_2, *weights_3, *weights_4]

    products = project(place, near, far, weights)
    products = products.reshape(4 * Z, *products.shape[2:])
    received = lax.all_to_all(products, ("yl", "c", "x", "yh"), 0, 0, tiled=True)
    received = received.reshape(4, Z, *received.shape[1:])

    layer2_out, partial = third_partials(
        place, received, hidden, norm_gain.reshape(1, -1), third_near, third_far
    )
    partial = lax.all_to_all(partial, HEAD_AXES, 0, 0, tiled=True)
    packed = final(
        keep_count,
        partial,
        layer3_key_value_bias.reshape(1, -1),
        cosine,
        sine,
        keep_index.reshape(1, -1),
    )
    return (layer2_out, packed)


def solution(mesh):
    split = Mesh(mesh.devices.reshape(Z, 2, 2, 4, 2), CTX_AXES + HEAD_AXES)
    placed = (
        P(CTX_AXES, HEAD_AXES),
        P(CTX_AXES, HEAD_AXES),
        P(None, CTX_AXES, HEAD_AXES),
        P(None, CTX_AXES, HEAD_AXES),
        P(None, CTX_AXES),
        P(HEAD_AXES, CTX_AXES),
        P(HEAD_AXES),
        P(None, HEAD_AXES),
        P(HEAD_AXES),
        P(CTX_AXES),
        P(CTX_AXES),
    )
    return jax.shard_map(
        local,
        mesh=split,
        in_specs=placed,
        out_specs=(P(CTX_AXES, HEAD_AXES), P(CTX_AXES, HEAD_AXES)),
        check_vma=False,
    )
```

```python
import functools

import jax
import jax.numpy as jnp
from jax import lax
from jax.experimental import pallas as pl
from jax.experimental.pallas import tpu as pltpu
from jax.sharding import Mesh
from jax.sharding import PartitionSpec as P

MODEL_WIDTH = 8192
HEAD = 128
ROWS = 128
CACHED = 256
GROUP = 8
Z = 8
LOG2E = 1.4426950408889634
SCALE = HEAD ** (-0.5) * LOG2E
CTX_AXES = ("z", "yl", "c")
HEAD_AXES = ("x", "yh")
VMEM = 56 * 1024 * 1024
DISTANCES = (0, -1, 1, -2, 2, -3, 3, 4)
BLOCKS = 3


def params(**more):
    return pltpu.CompilerParams(vmem_limit_bytes=VMEM, **more)


def tables(positions, head_size):
    half = head_size // 2
    column = jnp.arange(half)
    frequency = jnp.power(jnp.float32(1000000.0), -(2.0 * column.astype(jnp.float32)) / head_size)
    section = (column >= head_size // 8).astype(jnp.int32) + (
        column >= head_size // 8 + 3 * head_size // 16
    ).astype(jnp.int32)
    places = positions.astype(jnp.float32)
    chosen = jnp.where(
        section[None, :] == 0,
        places[0][:, None],
        jnp.where(section[None, :] == 1, places[1][:, None], places[2][:, None]),
    )
    angles = chosen * frequency[None, :]
    cosine, sine = jnp.cos(angles), jnp.sin(angles)
    return (
        jnp.concatenate([cosine, cosine], axis=1),
        jnp.concatenate([-sine, sine], axis=1),
    )


def rotated(x, cosine, sine):
    return x * cosine + pltpu.roll(x, HEAD // 2, 1) * sine


def prepare_kernel(query, fresh, cached, cosine, sine, query_out, kv_out):
    cos, sin = cosine[...], sine[...]
    for g in range(GROUP):
        piece = query[:, g * HEAD : (g + 1) * HEAD].astype(jnp.float32)
        query_out[g] = rotated(piece, cos, sin).astype(jnp.bfloat16)
    for k in range(CACHED // ROWS):
        kv_out[k] = jnp.transpose(cached[0, k * ROWS : (k + 1) * ROWS, :])
        kv_out[BLOCKS + k] = cached[1, k * ROWS : (k + 1) * ROWS, :]
    new_key = rotated(fresh[0].astype(jnp.float32), cos, sin).astype(jnp.bfloat16)
    kv_out[BLOCKS - 1] = jnp.transpose(new_key)
    kv_out[2 * BLOCKS - 1] = fresh[1]


def prepare(query, fresh, cached, cosine, sine):
    return pl.pallas_call(
        prepare_kernel,
        out_shape=(
            jax.ShapeDtypeStruct((GROUP, ROWS, HEAD), jnp.bfloat16),
            jax.ShapeDtypeStruct((2 * BLOCKS, ROWS, HEAD), jnp.bfloat16),
        ),
        compiler_params=params(),
        name="prepare",
        cost_estimate=pl.CostEstimate(flops=2_000_000, bytes_accessed=1_500_000, transcendentals=0),
    )(query, fresh, cached, cosine, sine)


def half_kernel(place, weight, out):
    out[...] = weight[:, 0]


def weight_half(place, weight):
    rows, columns = weight.shape[2:]
    return pl.pallas_call(
        half_kernel,
        grid_spec=pltpu.PrefetchScalarGridSpec(
            num_scalar_prefetch=1,
            grid=(Z // 2,),
            in_specs=[pl.BlockSpec((2, 1, rows, columns), lambda i, s: (i, s[2], 0, 0))],
            out_specs=pl.BlockSpec((2, rows, columns), lambda i, s: (i, 0, 0)),
        ),
        out_shape=jax.ShapeDtypeStruct((Z, rows, columns), jnp.bfloat16),
        compiler_params=params(),
        name="half",
        cost_estimate=pl.CostEstimate(flops=0, bytes_accessed=8_000_000, transcendentals=0),
    )(place, weight)


def column_of(row):
    return jnp.transpose(jnp.broadcast_to(row, (ROWS, ROWS)))


def row_of(column):
    return jnp.transpose(column)[0:1, :]


def attend_kernel(chunk, cached, fresh, n_queries, first, last, first_rc, place, *refs):
    n_in = 1 + max([max(k, v) for k, v in cached] + [max(p[0], p[1]) for pair in fresh for p in pair])
    queries, refs = refs[:n_queries], refs[n_queries:]
    pieces, rest = refs[:n_in], list(refs[n_in:])
    if not first:
        acc_in, m_in = rest[:2]
        rest = rest[2:]
    if last:
        out, lse_out = rest[:2]
    else:
        acc_out, m_out = rest[:2]
    keys, values, query = rest[2:]
    step = pl.program_id(0)
    each = pl.num_programs(0) // n_queries
    for k, ref in enumerate(queries):

        @pl.when(step // each == k)
        def _():
            query[...] = ref[...]

    which = step // each
    rc, ryl = first_rc + which // 2, lax.rem(which, 2)
    z, yl, c = place[0], place[1], place[2]
    steps = len(cached) + len(fresh)

    @pl.when(step == 0)
    def _():
        at = 0
        for kp, vp in cached:
            for k in range(2):
                keys[:, at : at + ROWS] = pieces[kp][k]
                values[at : at + ROWS, :HEAD] = pieces[vp][BLOCKS + k]
                at += ROWS
        for pair in fresh:
            for kp, vp, _ in pair:
                keys[:, at : at + ROWS] = pieces[kp][BLOCKS - 1]
                values[at : at + ROWS, :HEAD] = pieces[vp][2 * BLOCKS - 1]
                at += ROWS
        values[:, HEAD:] = jnp.ones((steps * 2 * ROWS, HEAD), jnp.bfloat16)

    block = z * 4 + (yl ^ ryl) * 2 + (c ^ rc)
    inside = lax.broadcasted_iota(jnp.int32, (chunk, 1), 0) & (ROWS - 1)
    query_token = block * ROWS + inside
    lane = lax.broadcasted_iota(jnp.int32, (1, 2 * ROWS), 1)
    q = query[...]
    if first:
        m = jnp.full((chunk, 1), -1e30, jnp.float32)
        acc = jnp.zeros((chunk, 2 * HEAD), jnp.float32)
    else:
        m = jnp.max(m_in[...], axis=1, keepdims=True)
        acc = acc_in[...]
    for i in range(steps):
        at = slice(i * 2 * ROWS, (i + 1) * 2 * ROWS)
        scores = jnp.dot(q, keys[:, at], preferred_element_type=jnp.float32)
        if i >= len(cached):
            one, two = (
                (lax.rem(z + p[2] + Z, Z) * 4 + yl * 2 + c) * ROWS for p in fresh[i - len(cached)]
            )
            key_token = jnp.where(lane < ROWS, one + lane, two + lane - ROWS)
            scores = jnp.where(key_token <= query_token, scores, -1e30)
        raised = jnp.maximum(m, jnp.max(scores, axis=1, keepdims=True))
        weights = jnp.exp2((scores - raised) * SCALE).astype(jnp.bfloat16)
        factor = jnp.exp2((m - raised) * SCALE)
        acc = acc * factor + jnp.dot(weights, values[at, :], preferred_element_type=jnp.float32)
        m = raised
    if not last:
        acc_out[...] = acc
        m_out[...] = jnp.broadcast_to(m, (chunk, HEAD))
        return
    totals = acc[:, HEAD:]
    out[...] = (acc[:, :HEAD] / totals).astype(jnp.bfloat16)
    lse = m * SCALE + jnp.log2(totals)
    for k in range(chunk // ROWS):
        lse_out[step * (chunk // ROWS) + k] = row_of(lse[k * ROWS : (k + 1) * ROWS, :])


def attend(chunk, place, queries, first_rc, pieces, cached, fresh, state=None, offset=0, last=False):
    each = queries[0].shape[0] // chunk
    rows = each * len(queries) * chunk
    total = 2 * ROWS * (len(cached) + len(fresh))
    first_block = offset // chunk

    def query_spec(k):
        return pl.BlockSpec(
            (chunk, HEAD), lambda i, s: (jnp.clip(i - k * each, 0, each - 1), 0)
        )

    row_spec = pl.BlockSpec((chunk, HEAD), lambda i, s: (i, 0))
    in_specs = [query_spec(k) for k in range(len(queries))]
    in_specs += [pl.BlockSpec(p.shape, lambda i, s: (0, 0, 0)) for p in pieces]
    args = [*queries, *pieces]
    if state is not None:
        in_specs += [
            pl.BlockSpec((chunk, 2 * HEAD), lambda i, s: (i + first_block, 0)),
            pl.BlockSpec((chunk, HEAD), lambda i, s: (i + first_block, 0)),
        ]
        args += list(state)
    if last:
        out_specs = [row_spec, pl.BlockSpec((rows // ROWS, 1, ROWS), lambda i, s: (0, 0, 0))]
        out_shape = (
            jax.ShapeDtypeStruct((rows, HEAD), jnp.bfloat16),
            jax.ShapeDtypeStruct((rows // ROWS, 1, ROWS), jnp.float32),
        )
    else:
        out_specs = [pl.BlockSpec((chunk, 2 * HEAD), lambda i, s: (i, 0)), row_spec]
        out_shape = (
            jax.ShapeDtypeStruct((rows, 2 * HEAD), jnp.float32),
            jax.ShapeDtypeStruct((rows, HEAD), jnp.float32),
        )
    return pl.pallas_call(
        functools.partial(
            attend_kernel, chunk, cached, fresh, len(queries), state is None, last, first_rc
        ),
        grid_spec=pltpu.PrefetchScalarGridSpec(
            num_scalar_prefetch=1,
            grid=(rows // chunk,),
            in_specs=in_specs,
            out_specs=out_specs,
            scratch_shapes=[
                pltpu.VMEM((HEAD, total), jnp.bfloat16),
                pltpu.VMEM((total, 2 * HEAD), jnp.bfloat16),
                pltpu.VMEM((chunk, HEAD), jnp.bfloat16),
            ],
        ),
        out_shape=out_shape,
        compiler_params=params(),
        name="attend",
        cost_estimate=pl.CostEstimate(
            flops=4 * rows * total * HEAD,
            bytes_accessed=8 * rows * HEAD + 4 * total * HEAD,
            transcendentals=rows * total,
        ),
    )(place, *args)


def merge_weight(first_lse, second_lse):
    top = jnp.maximum(first_lse, second_lse)
    a, b = jnp.exp2(first_lse - top), jnp.exp2(second_lse - top)
    return a / (a + b), top + jnp.log2(a + b)


def merged(first, second, weight):
    a, b = first.astype(jnp.float32), second.astype(jnp.float32)
    share = column_of(weight)
    return (a * share + b * (1.0 - share)).astype(jnp.bfloat16)


def merge_kernel(own, own_lse, other, other_lse, out, lse_out):
    for k in range(own.shape[0] // ROWS):
        at = slice(k * ROWS, (k + 1) * ROWS)
        weight, lse = merge_weight(own_lse[k], other_lse[k])
        out[at, :] = merged(own[at, :], other[at, :], weight)
        lse_out[k] = lse


def merge_last_kernel(own, own_lse, other, other_lse, out):
    for y in range(2):
        for g in range(GROUP):
            k, j = y * GROUP + g, (1 - y) * GROUP + g
            weight, _ = merge_weight(own_lse[k], other_lse[j])
            out[y, :, g * HEAD : (g + 1) * HEAD] = merged(
                own[k * ROWS : (k + 1) * ROWS, :], other[j * ROWS : (j + 1) * ROWS, :], weight
            )


MERGE_COST = pl.CostEstimate(flops=2_000_000, bytes_accessed=1_600_000, transcendentals=4096)


def merge(own, own_lse, other, other_lse):
    return pl.pallas_call(
        merge_kernel,
        out_shape=(
            jax.ShapeDtypeStruct(own.shape, own.dtype),
            jax.ShapeDtypeStruct(own_lse.shape, own_lse.dtype),
        ),
        compiler_params=params(),
        name="merge",
        cost_estimate=MERGE_COST,
    )(own, own_lse, other, other_lse)


def merge_last(own, own_lse, other, other_lse):
    return pl.pallas_call(
        merge_last_kernel,
        out_shape=jax.ShapeDtypeStruct((2, ROWS, GROUP * HEAD), jnp.bfloat16),
        compiler_params=params(),
        name="merge_last",
        cost_estimate=MERGE_COST,
    )(own, own_lse, other, other_lse)


def project_kernel(place, near, far, *refs):
    weights, top, bottom, out, rows = refs[: Z - 1], *refs[Z - 1 :]
    z, yl, c = place[0], place[1], place[2]
    for ryl in range(2):
        rows[ryl * ROWS : (ryl + 1) * ROWS, :] = near[ryl]
        rows[(2 + ryl) * ROWS : (3 + ryl) * ROWS, :] = far[ryl]
    lhs = rows[...]
    half = GROUP * HEAD // 2
    for i, distance in enumerate(DISTANCES):
        if i < Z - 1:
            product = jnp.dot(lhs, weights[i][...], preferred_element_type=jnp.float32)
        else:
            product = jnp.dot(lhs[:, :half], top[...], preferred_element_type=jnp.float32)
            product += jnp.dot(lhs[:, half:], bottom[...], preferred_element_type=jnp.float32)
        product = product.astype(jnp.bfloat16)
        target = lax.rem(z + distance + Z, Z)
        for k in range(4):
            q = (yl ^ (k % 2)) * 2 + (c ^ (k // 2))
            out[q, target] = product[k * ROWS : (k + 1) * ROWS, :]


def project(place, near, far, weights):
    vmem = pl.BlockSpec(memory_space=pltpu.VMEM)
    depth, columns = weights[0].shape
    return pl.pallas_call(
        project_kernel,
        in_specs=[pl.BlockSpec(memory_space=pltpu.SMEM)] + [vmem] * (3 + Z),
        out_specs=vmem,
        out_shape=jax.ShapeDtypeStruct((4, Z, ROWS, columns), jnp.bfloat16),
        scratch_shapes=[pltpu.VMEM((4 * ROWS, depth), jnp.bfloat16)],
        compiler_params=params(),
        name="project",
        cost_estimate=pl.CostEstimate(
            flops=2 * 4 * ROWS * depth * Z * columns, bytes_accessed=7_000_000, transcendentals=0
        ),
    )(place, near, far, *weights)


PAD = 16


def third_kernel(place, received, hidden, gain, near, far, out, partial, scaled):
    c = place[2]
    columns = received.shape[3]
    squares = jnp.zeros((ROWS, columns), jnp.float32)
    for q in range(4):
        at = slice(q * columns, (q + 1) * columns)
        total = received[q, 0].astype(jnp.float32)
        for h in range(1, Z):
            total = total + received[q, h].astype(jnp.float32)
        result = (hidden[:, at].astype(jnp.float32) + total).astype(jnp.bfloat16)
        out[:, at] = result
        wide = result.astype(jnp.float32)
        squares = squares + wide * wide
        scaled[q // 2, :, (q % 2) * columns : (q % 2 + 1) * columns] = (
            wide * gain[:, at]
        ).astype(jnp.bfloat16)
    squares = jnp.sum(squares, axis=1, keepdims=True)
    row = row_of(jnp.broadcast_to(squares, (ROWS, ROWS)))
    high = row.astype(jnp.bfloat16)
    low = (row - high.astype(jnp.float32)).astype(jnp.bfloat16)
    tail = jnp.broadcast_to(
        jnp.concatenate([high, low], axis=1).astype(jnp.float32), (PAD, 2 * ROWS)
    ).astype(jnp.bfloat16)
    near_rows, far_rows = scaled[c], scaled[1 - c]
    for h in range(Z):
        product = jnp.dot(near_rows, near[h], preferred_element_type=jnp.float32) + jnp.dot(
            far_rows, far[h], preferred_element_type=jnp.float32
        )
        partial[h, :ROWS, :] = product.astype(jnp.bfloat16)
        partial[h, ROWS:, :] = tail


def third_partials(place, received, hidden, gain, near, far):
    vmem = pl.BlockSpec(memory_space=pltpu.VMEM)
    width = hidden.shape[1]
    return pl.pallas_call(
        third_kernel,
        in_specs=[pl.BlockSpec(memory_space=pltpu.SMEM)] + [vmem] * 5,
        out_specs=(vmem, vmem),
        out_shape=(
            jax.ShapeDtypeStruct(hidden.shape, jnp.bfloat16),
            jax.ShapeDtypeStruct((Z, ROWS + PAD, 2 * HEAD), jnp.bfloat16),
        ),
        scratch_shapes=[pltpu.VMEM((2, ROWS, width // 2), jnp.bfloat16)],
        compiler_params=params(),
        name="third",
    )(place, received, hidden, gain, near, far)


def final_kernel(count, partial, bias, cosine, sine, index, out):
    total = partial[0, :ROWS, :].astype(jnp.float32)
    tail = partial[0, ROWS:, :].astype(jnp.float32)
    for h in range(1, Z):
        total = total + partial[h, :ROWS, :].astype(jnp.float32)
        tail = tail + partial[h, ROWS:, :].astype(jnp.float32)
    squares = tail[0:1, :ROWS] + tail[0:1, ROWS:]
    factor = lax.rsqrt(column_of(squares) / MODEL_WIDTH + 1e-06)
    keys = total[:, :HEAD] * factor + bias[:, :HEAD]
    values = total[:, HEAD:] * factor + bias[:, HEAD:]
    keys = rotated(keys, cosine[...], sine[...])
    rows = jnp.concatenate([keys, values], axis=1).astype(jnp.bfloat16)
    slot = lax.broadcasted_iota(jnp.int32, (ROWS, ROWS), 1)
    token = lax.broadcasted_iota(jnp.int32, (ROWS, ROWS), 0)
    chosen = (token == index[...]) & (slot < count[0])
    pick = jnp.where(chosen, 1.0, 0.0).astype(jnp.bfloat16)
    out[...] = lax.dot_general(
        pick, rows, (((0,), (0,)), ((), ())), preferred_element_type=jnp.float32
    ).astype(jnp.bfloat16)


def final(count, partial, bias, cosine, sine, index):
    vmem = pl.BlockSpec(memory_space=pltpu.VMEM)
    return pl.pallas_call(
        final_kernel,
        in_specs=[pl.BlockSpec(memory_space=pltpu.SMEM)] + [vmem] * 5,
        out_specs=vmem,
        out_shape=jax.ShapeDtypeStruct((ROWS, 2 * HEAD), jnp.bfloat16),
        compiler_params=params(),
        name="final",
    )(count, partial, bias, cosine, sine, index)


def swap(x, axis):
    return lax.ppermute(x, axis, [(0, 1), (1, 0)])


def along_z(x, distance):
    return lax.ppermute(x, "z", [(i, (i + distance) % Z) for i in range(Z)])


def after(x, *others):
    return lax.optimization_barrier((x, others))[0]


def step(pair):
    return [along_z(pair[0], 1), along_z(pair[1], -1)]


def local(
    hidden,
    query,
    fresh_key_value,
    cached_key_value,
    positions,
    out_weight,
    norm_gain,
    layer3_key_value_weight,
    layer3_key_value_bias,
    keep_index,
    keep_count,
):
    z, yl, c = lax.axis_index("z"), lax.axis_index("yl"), lax.axis_index("c")
    place = jnp.stack([z, yl, c]).astype(jnp.int32)

    cosine, sine = tables(positions, HEAD)
    rotated_query, kv = prepare(query, fresh_key_value, cached_key_value, cosine, sine)
    third_rows = weight_half(
        place, layer3_key_value_weight.reshape(Z, 2, MODEL_WIDTH // Z // 2, 2 * HEAD)
    )
    rotated_query = rotated_query.reshape(GROUP * ROWS, HEAD)
    across = swap(rotated_query, "yl")
    other_core = swap(rotated_query, "c")
    kv_1, across, third_rows = lax.optimization_barrier((step([kv, kv]), across, third_rows))
    near_query, far_query = [rotated_query, across], [other_core, swap(across, "c")]
    own_weight = after(out_weight, *kv_1)
    weights_1 = step([own_weight, own_weight])
    state = attend(
        1024,
        place,
        near_query + far_query,
        0,
        [kv, *kv_1],
        [(0, 0), (1, 1), (2, 2)],
        [[(0, 0, 0), (1, 1, -1)]],
    )
    kv_2 = list(after(step(kv_1), state))
    kv_3, weights_1, state = lax.optimization_barrier((step(kv_2), weights_1, state))
    third_near = lax.all_to_all(third_rows, HEAD_AXES, 0, 0, tiled=True)
    third_far = swap(third_near, "c")
    weights_2 = step(weights_1)
    kv_4 = along_z(kv_3[0], 1)
    kv_4, state = lax.optimization_barrier((kv_4, state))
    late = [kv_1[1], *kv_2, *kv_3, kv_4]
    late_cached = [(i, i) for i in range(1, 6)]
    late_fresh = [[(0, 0, 1), (1, 1, -2)], [(2, 2, 2), (3, 3, -3)], [(4, 4, 3), (5, 5, 4)]]
    offset = 2 * GROUP * ROWS
    send, send_lse = attend(
        512, place, far_query, 1, late, late_cached, late_fresh, state, offset, True
    )
    got, got_lse = swap(send, "c"), swap(send_lse, "c")
    near_query, _, weights_2 = lax.optimization_barrier((near_query, send_lse, weights_2))
    weights_3 = step(weights_2)
    own, own_lse = attend(
        512, place, near_query, 0, late, late_cached, late_fresh, state, 0, True
    )
    own, own_lse = merge(own, own_lse, got, got_lse)
    got, got_lse = swap(own, "yl"), swap(own_lse, "yl")
    depth = out_weight.shape[0] // 2
    weights_4 = [along_z(weights_3[0][:depth], 1), along_z(weights_3[1][depth:], -1)]
    got_lse = after(got_lse, third_near, *weights_4)
    near = merge_last(own, own_lse, got, got_lse)
    far = swap(near, "c")
    weights = [out_weight, *weights_1, *weights_2, *weights_3, *weights_4]

    products = project(place, near, far, weights)
    products = products.reshape(4 * Z, *products.shape[2:])
    received = lax.all_to_all(products, ("yl", "c", "x", "yh"), 0, 0, tiled=True)
    received = received.reshape(4, Z, *received.shape[1:])

    layer2_out, partial = third_partials(
        place, received, hidden, norm_gain.reshape(1, -1), third_near, third_far
    )
    partial = lax.all_to_all(partial, HEAD_AXES, 0, 0, tiled=True)
    packed = final(
        keep_count,
        partial,
        layer3_key_value_bias.reshape(1, -1),
        cosine,
        sine,
        keep_index.reshape(1, -1),
    )
    return (layer2_out, packed)


def solution(mesh):
    split = Mesh(mesh.devices.reshape(Z, 2, 2, 4, 2), CTX_AXES + HEAD_AXES)
    placed = (
        P(CTX_AXES, HEAD_AXES),
        P(CTX_AXES, HEAD_AXES),
        P(None, CTX_AXES, HEAD_AXES),
        P(None, CTX_AXES, HEAD_AXES),
        P(None, CTX_AXES),
        P(HEAD_AXES, CTX_AXES),
        P(HEAD_AXES),
        P(None, HEAD_AXES),
        P(HEAD_AXES),
        P(CTX_AXES),
        P(CTX_AXES),
    )
    return jax.shard_map(
        local,
        mesh=split,
        in_specs=placed,
        out_specs=(P(CTX_AXES, HEAD_AXES), P(CTX_AXES, HEAD_AXES)),
        check_vma=False,
    )
```

```python
import functools

import jax
import jax.numpy as jnp
from jax import lax
from jax.experimental import pallas as pl
from jax.experimental.pallas import tpu as pltpu
from jax.sharding import Mesh
from jax.sharding import PartitionSpec as P

MODEL_WIDTH = 8192
HEAD = 128
ROWS = 128
CACHED = 256
GROUP = 8
Z = 8
LOG2E = 1.4426950408889634
SCALE = HEAD ** (-0.5) * LOG2E
CTX_AXES = ("z", "yl", "c")
HEAD_AXES = ("x", "yh")
VMEM = 56 * 1024 * 1024
DISTANCES = (0, -1, 1, -2, 2, -3, 3, 4)
BLOCKS = 3


def params(**more):
    return pltpu.CompilerParams(vmem_limit_bytes=VMEM, **more)


def tables(positions, head_size):
    half = head_size // 2
    column = jnp.arange(half)
    frequency = jnp.power(jnp.float32(1000000.0), -(2.0 * column.astype(jnp.float32)) / head_size)
    section = (column >= head_size // 8).astype(jnp.int32) + (
        column >= head_size // 8 + 3 * head_size // 16
    ).astype(jnp.int32)
    places = positions.astype(jnp.float32)
    chosen = jnp.where(
        section[None, :] == 0,
        places[0][:, None],
        jnp.where(section[None, :] == 1, places[1][:, None], places[2][:, None]),
    )
    angles = chosen * frequency[None, :]
    cosine, sine = jnp.cos(angles), jnp.sin(angles)
    return (
        jnp.concatenate([cosine, cosine], axis=1),
        jnp.concatenate([-sine, sine], axis=1),
    )


def rotated(x, cosine, sine):
    return x * cosine + pltpu.roll(x, HEAD // 2, 1) * sine


def prepare_kernel(query, fresh, cached, cosine, sine, query_out, kv_out):
    cos, sin = cosine[...], sine[...]
    for g in range(GROUP):
        piece = query[:, g * HEAD : (g + 1) * HEAD].astype(jnp.float32)
        query_out[g] = rotated(piece, cos, sin).astype(jnp.bfloat16)
    for k in range(CACHED // ROWS):
        kv_out[k] = jnp.transpose(cached[0, k * ROWS : (k + 1) * ROWS, :])
        kv_out[BLOCKS + k] = cached[1, k * ROWS : (k + 1) * ROWS, :]
    new_key = rotated(fresh[0].astype(jnp.float32), cos, sin).astype(jnp.bfloat16)
    kv_out[BLOCKS - 1] = jnp.transpose(new_key)
    kv_out[2 * BLOCKS - 1] = fresh[1]


def prepare(query, fresh, cached, cosine, sine):
    return pl.pallas_call(
        prepare_kernel,
        out_shape=(
            jax.ShapeDtypeStruct((GROUP, ROWS, HEAD), jnp.bfloat16),
            jax.ShapeDtypeStruct((2 * BLOCKS, ROWS, HEAD), jnp.bfloat16),
        ),
        compiler_params=params(),
        name="prepare",
        cost_estimate=pl.CostEstimate(flops=2_000_000, bytes_accessed=1_500_000, transcendentals=0),
    )(query, fresh, cached, cosine, sine)


def half_kernel(place, weight, out):
    out[...] = weight[:, 0]


def weight_half(place, weight):
    rows, columns = weight.shape[2:]
    return pl.pallas_call(
        half_kernel,
        grid_spec=pltpu.PrefetchScalarGridSpec(
            num_scalar_prefetch=1,
            grid=(Z // 2,),
            in_specs=[pl.BlockSpec((2, 1, rows, columns), lambda i, s: (i, s[2], 0, 0))],
            out_specs=pl.BlockSpec((2, rows, columns), lambda i, s: (i, 0, 0)),
        ),
        out_shape=jax.ShapeDtypeStruct((Z, rows, columns), jnp.bfloat16),
        compiler_params=params(),
        name="half",
        cost_estimate=pl.CostEstimate(flops=0, bytes_accessed=8_000_000, transcendentals=0),
    )(place, weight)


def column_of(row):
    return jnp.transpose(jnp.broadcast_to(row, (ROWS, ROWS)))


def row_of(column):
    return jnp.transpose(column)[0:1, :]


def attend_kernel(chunk, cached, fresh, n_queries, first, last, first_rc, place, *refs):
    n_in = 1 + max([max(k, v) for k, v in cached] + [max(p[0], p[1]) for pair in fresh for p in pair])
    queries, refs = refs[:n_queries], refs[n_queries:]
    pieces, rest = refs[:n_in], list(refs[n_in:])
    if not first:
        acc_in, m_in = rest[:2]
        rest = rest[2:]
    if last:
        out, lse_out = rest[:2]
    else:
        acc_out, m_out = rest[:2]
    keys, values, query = rest[2:]
    step = pl.program_id(0)
    each = pl.num_programs(0) // n_queries
    for k, ref in enumerate(queries):

        @pl.when(step // each == k)
        def _():
            query[...] = ref[...]

    which = step // each
    rc, ryl = first_rc + which // 2, lax.rem(which, 2)
    z, yl, c = place[0], place[1], place[2]
    steps = len(cached) + len(fresh)

    @pl.when(step == 0)
    def _():
        at = 0
        for kp, vp in cached:
            for k in range(2):
                keys[:, at : at + ROWS] = pieces[kp][k]
                values[at : at + ROWS, :HEAD] = pieces[vp][BLOCKS + k]
                at += ROWS
        for pair in fresh:
            for kp, vp, _ in pair:
                keys[:, at : at + ROWS] = pieces[kp][BLOCKS - 1]
                values[at : at + ROWS, :HEAD] = pieces[vp][2 * BLOCKS - 1]
                at += ROWS
        values[:, HEAD:] = jnp.ones((steps * 2 * ROWS, HEAD), jnp.bfloat16)

    block = z * 4 + (yl ^ ryl) * 2 + (c ^ rc)
    inside = lax.broadcasted_iota(jnp.int32, (chunk, 1), 0) & (ROWS - 1)
    query_token = block * ROWS + inside
    lane = lax.broadcasted_iota(jnp.int32, (1, 2 * ROWS), 1)
    q = query[...]
    if first:
        m = jnp.full((chunk, 1), -1e30, jnp.float32)
        acc = jnp.zeros((chunk, 2 * HEAD), jnp.float32)
    else:
        m = jnp.max(m_in[...], axis=1, keepdims=True)
        acc = acc_in[...]
    for i in range(steps):
        at = slice(i * 2 * ROWS, (i + 1) * 2 * ROWS)
        scores = jnp.dot(q, keys[:, at], preferred_element_type=jnp.float32)
        if i >= len(cached):
            one, two = (
                (lax.rem(z + p[2] + Z, Z) * 4 + yl * 2 + c) * ROWS for p in fresh[i - len(cached)]
            )
            key_token = jnp.where(lane < ROWS, one + lane, two + lane - ROWS)
            scores = jnp.where(key_token <= query_token, scores, -1e30)
        raised = jnp.maximum(m, jnp.max(scores, axis=1, keepdims=True))
        weights = jnp.exp2((scores - raised) * SCALE).astype(jnp.bfloat16)
        factor = jnp.exp2((m - raised) * SCALE)
        acc = acc * factor + jnp.dot(weights, values[at, :], preferred_element_type=jnp.float32)
        m = raised
    if not last:
        acc_out[...] = acc
        m_out[...] = jnp.broadcast_to(m, (chunk, HEAD))
        return
    totals = acc[:, HEAD:]
    out[...] = (acc[:, :HEAD] / totals).astype(jnp.bfloat16)
    lse = m * SCALE + jnp.log2(totals)
    for k in range(chunk // ROWS):
        lse_out[step * (chunk // ROWS) + k] = row_of(lse[k * ROWS : (k + 1) * ROWS, :])


def attend(chunk, place, queries, first_rc, pieces, cached, fresh, state=None, offset=0, last=False):
    each = queries[0].shape[0] // chunk
    rows = each * len(queries) * chunk
    total = 2 * ROWS * (len(cached) + len(fresh))
    first_block = offset // chunk

    def query_spec(k):
        return pl.BlockSpec(
            (chunk, HEAD), lambda i, s: (jnp.clip(i - k * each, 0, each - 1), 0)
        )

    row_spec = pl.BlockSpec((chunk, HEAD), lambda i, s: (i, 0))
    in_specs = [query_spec(k) for k in range(len(queries))]
    in_specs += [pl.BlockSpec(p.shape, lambda i, s: (0, 0, 0)) for p in pieces]
    args = [*queries, *pieces]
    if state is not None:
        in_specs += [
            pl.BlockSpec((chunk, 2 * HEAD), lambda i, s: (i + first_block, 0)),
            pl.BlockSpec((chunk, HEAD), lambda i, s: (i + first_block, 0)),
        ]
        args += list(state)
    if last:
        out_specs = [row_spec, pl.BlockSpec((rows // ROWS, 1, ROWS), lambda i, s: (0, 0, 0))]
        out_shape = (
            jax.ShapeDtypeStruct((rows, HEAD), jnp.bfloat16),
            jax.ShapeDtypeStruct((rows // ROWS, 1, ROWS), jnp.float32),
        )
    else:
        out_specs = [pl.BlockSpec((chunk, 2 * HEAD), lambda i, s: (i, 0)), row_spec]
        out_shape = (
            jax.ShapeDtypeStruct((rows, 2 * HEAD), jnp.float32),
            jax.ShapeDtypeStruct((rows, HEAD), jnp.float32),
        )
    return pl.pallas_call(
        functools.partial(
            attend_kernel, chunk, cached, fresh, len(queries), state is None, last, first_rc
        ),
        grid_spec=pltpu.PrefetchScalarGridSpec(
            num_scalar_prefetch=1,
            grid=(rows // chunk,),
            in_specs=in_specs,
            out_specs=out_specs,
            scratch_shapes=[
                pltpu.VMEM((HEAD, total), jnp.bfloat16),
                pltpu.VMEM((total, 2 * HEAD), jnp.bfloat16),
                pltpu.VMEM((chunk, HEAD), jnp.bfloat16),
            ],
        ),
        out_shape=out_shape,
        compiler_params=params(),
        name="attend",
        cost_estimate=pl.CostEstimate(
            flops=4 * rows * total * HEAD,
            bytes_accessed=8 * rows * HEAD + 4 * total * HEAD,
            transcendentals=rows * total,
        ),
    )(place, *args)


def merge_weight(first_lse, second_lse):
    top = jnp.maximum(first_lse, second_lse)
    a, b = jnp.exp2(first_lse - top), jnp.exp2(second_lse - top)
    return a / (a + b), top + jnp.log2(a + b)


def merged(first, second, weight):
    a, b = first.astype(jnp.float32), second.astype(jnp.float32)
    share = column_of(weight)
    return (a * share + b * (1.0 - share)).astype(jnp.bfloat16)


def merge_kernel(own, own_lse, other, other_lse, out, lse_out):
    for k in range(own.shape[0] // ROWS):
        at = slice(k * ROWS, (k + 1) * ROWS)
        weight, lse = merge_weight(own_lse[k], other_lse[k])
        out[at, :] = merged(own[at, :], other[at, :], weight)
        lse_out[k] = lse


def merge_last_kernel(own, own_lse, other, other_lse, out):
    for y in range(2):
        for g in range(GROUP):
            k, j = y * GROUP + g, (1 - y) * GROUP + g
            weight, _ = merge_weight(own_lse[k], other_lse[j])
            out[y, :, g * HEAD : (g + 1) * HEAD] = merged(
                own[k * ROWS : (k + 1) * ROWS, :], other[j * ROWS : (j + 1) * ROWS, :], weight
            )


MERGE_COST = pl.CostEstimate(flops=2_000_000, bytes_accessed=1_600_000, transcendentals=4096)


def merge(own, own_lse, other, other_lse):
    return pl.pallas_call(
        merge_kernel,
        out_shape=(
            jax.ShapeDtypeStruct(own.shape, own.dtype),
            jax.ShapeDtypeStruct(own_lse.shape, own_lse.dtype),
        ),
        compiler_params=params(),
        name="merge",
        cost_estimate=MERGE_COST,
    )(own, own_lse, other, other_lse)


def merge_last(own, own_lse, other, other_lse):
    return pl.pallas_call(
        merge_last_kernel,
        out_shape=jax.ShapeDtypeStruct((2, ROWS, GROUP * HEAD), jnp.bfloat16),
        compiler_params=params(),
        name="merge_last",
        cost_estimate=MERGE_COST,
    )(own, own_lse, other, other_lse)


def project_kernel(place, near, far, *refs):
    weights, top, bottom, out, rows = refs[: Z - 1], *refs[Z - 1 :]
    z, yl, c = place[0], place[1], place[2]
    for ryl in range(2):
        rows[ryl * ROWS : (ryl + 1) * ROWS, :] = near[ryl]
        rows[(2 + ryl) * ROWS : (3 + ryl) * ROWS, :] = far[ryl]
    lhs = rows[...]
    half = GROUP * HEAD // 2
    for i, distance in enumerate(DISTANCES):
        if i < Z - 1:
            product = jnp.dot(lhs, weights[i][...], preferred_element_type=jnp.float32)
        else:
            product = jnp.dot(lhs[:, :half], top[...], preferred_element_type=jnp.float32)
            product += jnp.dot(lhs[:, half:], bottom[...], preferred_element_type=jnp.float32)
        product = product.astype(jnp.bfloat16)
        target = lax.rem(z + distance + Z, Z)
        for k in range(4):
            q = (yl ^ (k % 2)) * 2 + (c ^ (k // 2))
            out[q, target] = product[k * ROWS : (k + 1) * ROWS, :]


def project(place, near, far, weights):
    vmem = pl.BlockSpec(memory_space=pltpu.VMEM)
    depth, columns = weights[0].shape
    return pl.pallas_call(
        project_kernel,
        in_specs=[pl.BlockSpec(memory_space=pltpu.SMEM)] + [vmem] * (3 + Z),
        out_specs=vmem,
        out_shape=jax.ShapeDtypeStruct((4, Z, ROWS, columns), jnp.bfloat16),
        scratch_shapes=[pltpu.VMEM((4 * ROWS, depth), jnp.bfloat16)],
        compiler_params=params(),
        name="project",
        cost_estimate=pl.CostEstimate(
            flops=2 * 4 * ROWS * depth * Z * columns, bytes_accessed=7_000_000, transcendentals=0
        ),
    )(place, near, far, *weights)


PAD = 16


def third_kernel(
    place, received, hidden, gain, near, far, out, partial, scaled, squares, held, sem
):
    c, q = place[2], pl.program_id(0)
    copies = [pltpu.make_async_copy(ref, held.at[k], sem.at[k]) for k, ref in ((0, near), (1, far))]

    @pl.when(q == 0)
    def _():
        for copy in copies:
            copy.start()
        squares[...] = jnp.zeros_like(squares)

    total = received[0, 0].astype(jnp.float32)
    for h in range(1, Z):
        total = total + received[0, h].astype(jnp.float32)
    result = (hidden[...].astype(jnp.float32) + total).astype(jnp.bfloat16)
    out[...] = result
    wide = result.astype(jnp.float32)
    squares[...] += wide * wide
    scaled[q] = (wide * gain[...]).astype(jnp.bfloat16)

    @pl.when(q == pl.num_programs(0) - 1)
    def _():
        row = row_of(
            jnp.broadcast_to(jnp.sum(squares[...], axis=1, keepdims=True), (ROWS, ROWS))
        )
        high = row.astype(jnp.bfloat16)
        low = (row - high.astype(jnp.float32)).astype(jnp.bfloat16)
        tail = jnp.broadcast_to(
            jnp.concatenate([high, low], axis=1).astype(jnp.float32), (PAD, 2 * ROWS)
        ).astype(jnp.bfloat16)
        for copy in copies:
            copy.wait()
        near_rows = jnp.concatenate([scaled[2 * c], scaled[2 * c + 1]], axis=1)
        far_rows = jnp.concatenate([scaled[2 - 2 * c], scaled[3 - 2 * c]], axis=1)
        for h in range(Z):
            product = jnp.dot(near_rows, held[0, h], preferred_element_type=jnp.float32)
            product += jnp.dot(far_rows, held[1, h], preferred_element_type=jnp.float32)
            partial[h, :ROWS, :] = product.astype(jnp.bfloat16)
            partial[h, ROWS:, :] = tail


def third_partials(place, received, hidden, gain, near, far):
    columns = received.shape[3]
    anywhere = pl.BlockSpec(memory_space=pl.ANY)
    return pl.pallas_call(
        third_kernel,
        grid_spec=pltpu.PrefetchScalarGridSpec(
            num_scalar_prefetch=1,
            grid=(4,),
            in_specs=[
                pl.BlockSpec((1, Z, ROWS, columns), lambda i, s: (i, 0, 0, 0)),
                pl.BlockSpec((ROWS, columns), lambda i, s: (0, i)),
                pl.BlockSpec((1, columns), lambda i, s: (0, i)),
                anywhere,
                anywhere,
            ],
            out_specs=[
                pl.BlockSpec((ROWS, columns), lambda i, s: (0, i)),
                pl.BlockSpec((Z, ROWS + PAD, 2 * HEAD), lambda i, s: (0, 0, 0)),
            ],
            scratch_shapes=[
                pltpu.VMEM((4, ROWS, columns), jnp.bfloat16),
                pltpu.VMEM((ROWS, columns), jnp.float32),
                pltpu.VMEM((2, *near.shape), jnp.bfloat16),
                pltpu.SemaphoreType.DMA((2,)),
            ],
        ),
        out_shape=(
            jax.ShapeDtypeStruct(hidden.shape, jnp.bfloat16),
            jax.ShapeDtypeStruct((Z, ROWS + PAD, 2 * HEAD), jnp.bfloat16),
        ),
        compiler_params=params(),
        name="third",
    )(place, received, hidden, gain, near, far)


def final_kernel(count, partial, bias, cosine, sine, index, out):
    total = partial[0, :ROWS, :].astype(jnp.float32)
    tail = partial[0, ROWS:, :].astype(jnp.float32)
    for h in range(1, Z):
        total = total + partial[h, :ROWS, :].astype(jnp.float32)
        tail = tail + partial[h, ROWS:, :].astype(jnp.float32)
    squares = tail[0:1, :ROWS] + tail[0:1, ROWS:]
    factor = lax.rsqrt(column_of(squares) / MODEL_WIDTH + 1e-06)
    keys = total[:, :HEAD] * factor + bias[:, :HEAD]
    values = total[:, HEAD:] * factor + bias[:, HEAD:]
    keys = rotated(keys, cosine[...], sine[...])
    rows = jnp.concatenate([keys, values], axis=1).astype(jnp.bfloat16)
    slot = lax.broadcasted_iota(jnp.int32, (ROWS, ROWS), 1)
    token = lax.broadcasted_iota(jnp.int32, (ROWS, ROWS), 0)
    chosen = (token == index[...]) & (slot < count[0])
    pick = jnp.where(chosen, 1.0, 0.0).astype(jnp.bfloat16)
    out[...] = lax.dot_general(
        pick, rows, (((0,), (0,)), ((), ())), preferred_element_type=jnp.float32
    ).astype(jnp.bfloat16)


def final(count, partial, bias, cosine, sine, index):
    vmem = pl.BlockSpec(memory_space=pltpu.VMEM)
    return pl.pallas_call(
        final_kernel,
        in_specs=[pl.BlockSpec(memory_space=pltpu.SMEM)] + [vmem] * 5,
        out_specs=vmem,
        out_shape=jax.ShapeDtypeStruct((ROWS, 2 * HEAD), jnp.bfloat16),
        compiler_params=params(),
        name="final",
    )(count, partial, bias, cosine, sine, index)


def swap(x, axis):
    return lax.ppermute(x, axis, [(0, 1), (1, 0)])


def along_z(x, distance):
    return lax.ppermute(x, "z", [(i, (i + distance) % Z) for i in range(Z)])


def after(x, *others):
    return lax.optimization_barrier((x, others))[0]


def step(pair):
    return [along_z(pair[0], 1), along_z(pair[1], -1)]


def local(
    hidden,
    query,
    fresh_key_value,
    cached_key_value,
    positions,
    out_weight,
    norm_gain,
    layer3_key_value_weight,
    layer3_key_value_bias,
    keep_index,
    keep_count,
):
    z, yl, c = lax.axis_index("z"), lax.axis_index("yl"), lax.axis_index("c")
    place = jnp.stack([z, yl, c]).astype(jnp.int32)

    cosine, sine = tables(positions, HEAD)
    rotated_query, kv = prepare(query, fresh_key_value, cached_key_value, cosine, sine)
    third_rows = weight_half(
        place, layer3_key_value_weight.reshape(Z, 2, MODEL_WIDTH // Z // 2, 2 * HEAD)
    )
    rotated_query = rotated_query.reshape(GROUP * ROWS, HEAD)
    across = swap(rotated_query, "yl")
    other_core = swap(rotated_query, "c")
    kv_1, across, third_rows = lax.optimization_barrier((step([kv, kv]), across, third_rows))
    near_query, far_query = [rotated_query, across], [other_core, swap(across, "c")]
    own_weight = after(out_weight, *kv_1)
    weights_1 = step([own_weight, own_weight])
    state = attend(
        1024,
        place,
        near_query + far_query,
        0,
        [kv, *kv_1],
        [(0, 0), (1, 1), (2, 2)],
        [[(0, 0, 0), (1, 1, -1)]],
    )
    kv_2 = list(after(step(kv_1), state))
    kv_3, weights_1, state = lax.optimization_barrier((step(kv_2), weights_1, state))
    third_near = lax.all_to_all(third_rows, HEAD_AXES, 0, 0, tiled=True)
    third_far = swap(third_near, "c")
    weights_2 = step(weights_1)
    kv_4 = along_z(kv_3[0], 1)
    kv_4, state = lax.optimization_barrier((kv_4, state))
    late = [kv_1[1], *kv_2, *kv_3, kv_4]
    late_cached = [(i, i) for i in range(1, 6)]
    late_fresh = [[(0, 0, 1), (1, 1, -2)], [(2, 2, 2), (3, 3, -3)], [(4, 4, 3), (5, 5, 4)]]
    offset = 2 * GROUP * ROWS
    send, send_lse = attend(
        512, place, far_query, 1, late, late_cached, late_fresh, state, offset, True
    )
    got, got_lse = swap(send, "c"), swap(send_lse, "c")
    near_query, _, weights_2 = lax.optimization_barrier((near_query, send_lse, weights_2))
    weights_3 = step(weights_2)
    own, own_lse = attend(
        512, place, near_query, 0, late, late_cached, late_fresh, state, 0, True
    )
    own, own_lse = merge(own, own_lse, got, got_lse)
    got, got_lse = swap(own, "yl"), swap(own_lse, "yl")
    depth = out_weight.shape[0] // 2
    weights_4 = [along_z(weights_3[0][:depth], 1), along_z(weights_3[1][depth:], -1)]
    got_lse = after(got_lse, third_near, *weights_4)
    near = merge_last(own, own_lse, got, got_lse)
    far = swap(near, "c")
    weights = [out_weight, *weights_1, *weights_2, *weights_3, *weights_4]

    products = project(place, near, far, weights)
    products = products.reshape(4 * Z, *products.shape[2:])
    received = lax.all_to_all(products, ("yl", "c", "x", "yh"), 0, 0, tiled=True)
    received = received.reshape(4, Z, *received.shape[1:])

    layer2_out, partial = third_partials(
        place, received, hidden, norm_gain.reshape(1, -1), third_near, third_far
    )
    partial = lax.all_to_all(partial, HEAD_AXES, 0, 0, tiled=True)
    packed = final(
        keep_count,
        partial,
        layer3_key_value_bias.reshape(1, -1),
        cosine,
        sine,
        keep_index.reshape(1, -1),
    )
    return (layer2_out, packed)


def solution(mesh):
    split = Mesh(mesh.devices.reshape(Z, 2, 2, 4, 2), CTX_AXES + HEAD_AXES)
    placed = (
        P(CTX_AXES, HEAD_AXES),
        P(CTX_AXES, HEAD_AXES),
        P(None, CTX_AXES, HEAD_AXES),
        P(None, CTX_AXES, HEAD_AXES),
        P(None, CTX_AXES),
        P(HEAD_AXES, CTX_AXES),
        P(HEAD_AXES),
        P(None, HEAD_AXES),
        P(HEAD_AXES),
        P(CTX_AXES),
        P(CTX_AXES),
    )
    return jax.shard_map(
        local,
        mesh=split,
        in_specs=placed,
        out_specs=(P(CTX_AXES, HEAD_AXES), P(CTX_AXES, HEAD_AXES)),
        check_vma=False,
    )
```

```python
import functools

import jax
import jax.numpy as jnp
from jax import lax
from jax.experimental import pallas as pl
from jax.experimental.pallas import tpu as pltpu
from jax.sharding import Mesh
from jax.sharding import PartitionSpec as P

MODEL_WIDTH = 8192
HEAD = 128
ROWS = 128
CACHED = 256
GROUP = 8
Z = 8
LOG2E = 1.4426950408889634
SCALE = HEAD ** (-0.5) * LOG2E
CTX_AXES = ("z", "yl", "c")
HEAD_AXES = ("x", "yh")
VMEM = 56 * 1024 * 1024
DISTANCES = (0, -1, 1, -2, 2, -3, 3, 4)
BLOCKS = 3


def params(**more):
    return pltpu.CompilerParams(vmem_limit_bytes=VMEM, **more)


def tables(positions, head_size):
    half = head_size // 2
    column = jnp.arange(half)
    frequency = jnp.power(jnp.float32(1000000.0), -(2.0 * column.astype(jnp.float32)) / head_size)
    section = (column >= head_size // 8).astype(jnp.int32) + (
        column >= head_size // 8 + 3 * head_size // 16
    ).astype(jnp.int32)
    places = positions.astype(jnp.float32)
    chosen = jnp.where(
        section[None, :] == 0,
        places[0][:, None],
        jnp.where(section[None, :] == 1, places[1][:, None], places[2][:, None]),
    )
    angles = chosen * frequency[None, :]
    cosine, sine = jnp.cos(angles), jnp.sin(angles)
    return (
        jnp.concatenate([cosine, cosine], axis=1),
        jnp.concatenate([-sine, sine], axis=1),
    )


def rotated(x, cosine, sine):
    return x * cosine + pltpu.roll(x, HEAD // 2, 1) * sine


def prepare_kernel(query, fresh, cached, cosine, sine, query_out, kv_out):
    cos, sin = cosine[...], sine[...]
    for g in range(GROUP):
        piece = query[:, g * HEAD : (g + 1) * HEAD].astype(jnp.float32)
        query_out[g] = rotated(piece, cos, sin).astype(jnp.bfloat16)
    for k in range(CACHED // ROWS):
        kv_out[k] = jnp.transpose(cached[0, k * ROWS : (k + 1) * ROWS, :])
        kv_out[BLOCKS + k] = cached[1, k * ROWS : (k + 1) * ROWS, :]
    new_key = rotated(fresh[0].astype(jnp.float32), cos, sin).astype(jnp.bfloat16)
    kv_out[BLOCKS - 1] = jnp.transpose(new_key)
    kv_out[2 * BLOCKS - 1] = fresh[1]


def prepare(query, fresh, cached, cosine, sine):
    return pl.pallas_call(
        prepare_kernel,
        out_shape=(
            jax.ShapeDtypeStruct((GROUP, ROWS, HEAD), jnp.bfloat16),
            jax.ShapeDtypeStruct((2 * BLOCKS, ROWS, HEAD), jnp.bfloat16),
        ),
        compiler_params=params(),
        name="prepare",
        cost_estimate=pl.CostEstimate(flops=2_000_000, bytes_accessed=1_500_000, transcendentals=0),
    )(query, fresh, cached, cosine, sine)


def half_kernel(place, weight, out):
    out[...] = weight[:, 0]


def weight_half(place, weight):
    rows, columns = weight.shape[2:]
    return pl.pallas_call(
        half_kernel,
        grid_spec=pltpu.PrefetchScalarGridSpec(
            num_scalar_prefetch=1,
            grid=(Z // 2,),
            in_specs=[pl.BlockSpec((2, 1, rows, columns), lambda i, s: (i, s[2], 0, 0))],
            out_specs=pl.BlockSpec((2, rows, columns), lambda i, s: (i, 0, 0)),
        ),
        out_shape=jax.ShapeDtypeStruct((Z, rows, columns), jnp.bfloat16),
        compiler_params=params(),
        name="half",
        cost_estimate=pl.CostEstimate(flops=0, bytes_accessed=8_000_000, transcendentals=0),
    )(place, weight)


def column_of(row):
    return jnp.transpose(jnp.broadcast_to(row, (ROWS, ROWS)))


def row_of(column):
    return jnp.transpose(column)[0:1, :]


def attend_kernel(chunk, cached, fresh, n_queries, first, last, first_rc, place, *refs):
    n_in = 1 + max([max(k, v) for k, v in cached] + [max(p[0], p[1]) for pair in fresh for p in pair])
    queries, refs = refs[:n_queries], refs[n_queries:]
    pieces, rest = refs[:n_in], list(refs[n_in:])
    if not first:
        acc_in, m_in = rest[:2]
        rest = rest[2:]
    if last:
        out, lse_out = rest[:2]
    else:
        acc_out, m_out = rest[:2]
    keys, values, query = rest[2:]
    step = pl.program_id(0)
    each = pl.num_programs(0) // n_queries
    for k, ref in enumerate(queries):

        @pl.when(step // each == k)
        def _():
            query[...] = ref[...]

    which = step // each
    rc, ryl = first_rc + which // 2, lax.rem(which, 2)
    z, yl, c = place[0], place[1], place[2]
    steps = len(cached) + len(fresh)

    @pl.when(step == 0)
    def _():
        at = 0
        for kp, vp in cached:
            for k in range(2):
                keys[:, at : at + ROWS] = pieces[kp][k]
                values[at : at + ROWS, :HEAD] = pieces[vp][BLOCKS + k]
                at += ROWS
        for pair in fresh:
            for kp, vp, _ in pair:
                keys[:, at : at + ROWS] = pieces[kp][BLOCKS - 1]
                values[at : at + ROWS, :HEAD] = pieces[vp][2 * BLOCKS - 1]
                at += ROWS
        values[:, HEAD:] = jnp.ones((steps * 2 * ROWS, HEAD), jnp.bfloat16)

    block = z * 4 + (yl ^ ryl) * 2 + (c ^ rc)
    inside = lax.broadcasted_iota(jnp.int32, (chunk, 1), 0) & (ROWS - 1)
    query_token = block * ROWS + inside
    lane = lax.broadcasted_iota(jnp.int32, (1, 2 * ROWS), 1)
    q = query[...]
    if first:
        m = jnp.full((chunk, 1), -1e30, jnp.float32)
        acc = jnp.zeros((chunk, 2 * HEAD), jnp.float32)
    else:
        m = jnp.max(m_in[...], axis=1, keepdims=True)
        acc = acc_in[...]
    for i in range(steps):
        at = slice(i * 2 * ROWS, (i + 1) * 2 * ROWS)
        scores = jnp.dot(q, keys[:, at], preferred_element_type=jnp.float32)
        if i >= len(cached):
            one, two = (
                (lax.rem(z + p[2] + Z, Z) * 4 + yl * 2 + c) * ROWS for p in fresh[i - len(cached)]
            )
            key_token = jnp.where(lane < ROWS, one + lane, two + lane - ROWS)
            scores = jnp.where(key_token <= query_token, scores, -1e30)
        raised = jnp.maximum(m, jnp.max(scores, axis=1, keepdims=True))
        weights = jnp.exp2((scores - raised) * SCALE).astype(jnp.bfloat16)
        factor = jnp.exp2((m - raised) * SCALE)
        acc = acc * factor + jnp.dot(weights, values[at, :], preferred_element_type=jnp.float32)
        m = raised
    if not last:
        acc_out[...] = acc
        m_out[...] = jnp.broadcast_to(m, (chunk, HEAD))
        return
    totals = acc[:, HEAD:]
    out[...] = (acc[:, :HEAD] / totals).astype(jnp.bfloat16)
    lse = m * SCALE + jnp.log2(totals)
    for k in range(chunk // ROWS):
        lse_out[step * (chunk // ROWS) + k] = row_of(lse[k * ROWS : (k + 1) * ROWS, :])


def attend(chunk, place, queries, first_rc, pieces, cached, fresh, state=None, offset=0, last=False):
    each = queries[0].shape[0] // chunk
    rows = each * len(queries) * chunk
    total = 2 * ROWS * (len(cached) + len(fresh))
    first_block = offset // chunk

    def query_spec(k):
        return pl.BlockSpec(
            (chunk, HEAD), lambda i, s: (jnp.clip(i - k * each, 0, each - 1), 0)
        )

    row_spec = pl.BlockSpec((chunk, HEAD), lambda i, s: (i, 0))
    in_specs = [query_spec(k) for k in range(len(queries))]
    in_specs += [pl.BlockSpec(p.shape, lambda i, s: (0, 0, 0)) for p in pieces]
    args = [*queries, *pieces]
    if state is not None:
        in_specs += [
            pl.BlockSpec((chunk, 2 * HEAD), lambda i, s: (i + first_block, 0)),
            pl.BlockSpec((chunk, HEAD), lambda i, s: (i + first_block, 0)),
        ]
        args += list(state)
    if last:
        out_specs = [row_spec, pl.BlockSpec((rows // ROWS, 1, ROWS), lambda i, s: (0, 0, 0))]
        out_shape = (
            jax.ShapeDtypeStruct((rows, HEAD), jnp.bfloat16),
            jax.ShapeDtypeStruct((rows // ROWS, 1, ROWS), jnp.float32),
        )
    else:
        out_specs = [pl.BlockSpec((chunk, 2 * HEAD), lambda i, s: (i, 0)), row_spec]
        out_shape = (
            jax.ShapeDtypeStruct((rows, 2 * HEAD), jnp.float32),
            jax.ShapeDtypeStruct((rows, HEAD), jnp.float32),
        )
    return pl.pallas_call(
        functools.partial(
            attend_kernel, chunk, cached, fresh, len(queries), state is None, last, first_rc
        ),
        grid_spec=pltpu.PrefetchScalarGridSpec(
            num_scalar_prefetch=1,
            grid=(rows // chunk,),
            in_specs=in_specs,
            out_specs=out_specs,
            scratch_shapes=[
                pltpu.VMEM((HEAD, total), jnp.bfloat16),
                pltpu.VMEM((total, 2 * HEAD), jnp.bfloat16),
                pltpu.VMEM((chunk, HEAD), jnp.bfloat16),
            ],
        ),
        out_shape=out_shape,
        compiler_params=params(),
        name="attend",
        cost_estimate=pl.CostEstimate(
            flops=4 * rows * total * HEAD,
            bytes_accessed=8 * rows * HEAD + 4 * total * HEAD,
            transcendentals=rows * total,
        ),
    )(place, *args)


def merge_weight(first_lse, second_lse):
    top = jnp.maximum(first_lse, second_lse)
    a, b = jnp.exp2(first_lse - top), jnp.exp2(second_lse - top)
    return a / (a + b), top + jnp.log2(a + b)


def merged(first, second, weight):
    a, b = first.astype(jnp.float32), second.astype(jnp.float32)
    share = column_of(weight)
    return (a * share + b * (1.0 - share)).astype(jnp.bfloat16)


def merge_kernel(own, own_lse, other, other_lse, out, lse_out):
    for k in range(own.shape[0] // ROWS):
        at = slice(k * ROWS, (k + 1) * ROWS)
        weight, lse = merge_weight(own_lse[k], other_lse[k])
        out[at, :] = merged(own[at, :], other[at, :], weight)
        lse_out[k] = lse


def merge_last_kernel(own, own_lse, other, other_lse, out):
    for y in range(2):
        for g in range(GROUP):
            k, j = y * GROUP + g, (1 - y) * GROUP + g
            weight, _ = merge_weight(own_lse[k], other_lse[j])
            out[y, :, g * HEAD : (g + 1) * HEAD] = merged(
                own[k * ROWS : (k + 1) * ROWS, :], other[j * ROWS : (j + 1) * ROWS, :], weight
            )


MERGE_COST = pl.CostEstimate(flops=2_000_000, bytes_accessed=1_600_000, transcendentals=4096)


def merge(own, own_lse, other, other_lse):
    return pl.pallas_call(
        merge_kernel,
        out_shape=(
            jax.ShapeDtypeStruct(own.shape, own.dtype),
            jax.ShapeDtypeStruct(own_lse.shape, own_lse.dtype),
        ),
        compiler_params=params(),
        name="merge",
        cost_estimate=MERGE_COST,
    )(own, own_lse, other, other_lse)


def merge_last(own, own_lse, other, other_lse):
    return pl.pallas_call(
        merge_last_kernel,
        out_shape=jax.ShapeDtypeStruct((2, ROWS, GROUP * HEAD), jnp.bfloat16),
        compiler_params=params(),
        name="merge_last",
        cost_estimate=MERGE_COST,
    )(own, own_lse, other, other_lse)


def project_kernel(place, near, far, *refs):
    weights, top, bottom, out, rows = refs[: Z - 1], *refs[Z - 1 :]
    z, yl, c = place[0], place[1], place[2]
    for ryl in range(2):
        rows[ryl * ROWS : (ryl + 1) * ROWS, :] = near[ryl]
        rows[(2 + ryl) * ROWS : (3 + ryl) * ROWS, :] = far[ryl]
    lhs = rows[...]
    half = GROUP * HEAD // 2
    for i, distance in enumerate(DISTANCES):
        if i < Z - 1:
            product = jnp.dot(lhs, weights[i][...], preferred_element_type=jnp.float32)
        else:
            product = jnp.dot(lhs[:, :half], top[...], preferred_element_type=jnp.float32)
            product += jnp.dot(lhs[:, half:], bottom[...], preferred_element_type=jnp.float32)
        product = product.astype(jnp.bfloat16)
        target = lax.rem(z + distance + Z, Z)
        for k in range(4):
            q = (yl ^ (k % 2)) * 2 + (c ^ (k // 2))
            out[q, target] = product[k * ROWS : (k + 1) * ROWS, :]


def project(place, near, far, weights):
    vmem = pl.BlockSpec(memory_space=pltpu.VMEM)
    depth, columns = weights[0].shape
    return pl.pallas_call(
        project_kernel,
        in_specs=[pl.BlockSpec(memory_space=pltpu.SMEM)] + [vmem] * (3 + Z),
        out_specs=vmem,
        out_shape=jax.ShapeDtypeStruct((4, Z, ROWS, columns), jnp.bfloat16),
        scratch_shapes=[pltpu.VMEM((4 * ROWS, depth), jnp.bfloat16)],
        compiler_params=params(),
        name="project",
        cost_estimate=pl.CostEstimate(
            flops=2 * 4 * ROWS * depth * Z * columns, bytes_accessed=7_000_000, transcendentals=0
        ),
    )(place, near, far, *weights)


PAD = 16


def third_kernel(place, received, hidden, gain, near, far, out, partial, scaled):
    c = place[2]
    columns = received.shape[3]
    squares = jnp.zeros((ROWS, columns), jnp.float32)
    for q in range(4):
        at = slice(q * columns, (q + 1) * columns)
        total = received[q, 0].astype(jnp.float32)
        for h in range(1, Z):
            total = total + received[q, h].astype(jnp.float32)
        result = (hidden[:, at].astype(jnp.float32) + total).astype(jnp.bfloat16)
        out[:, at] = result
        wide = result.astype(jnp.float32)
        squares = squares + wide * wide
        scaled[q // 2, :, (q % 2) * columns : (q % 2 + 1) * columns] = (
            wide * gain[:, at]
        ).astype(jnp.bfloat16)
    squares = jnp.sum(squares, axis=1, keepdims=True)
    row = row_of(jnp.broadcast_to(squares, (ROWS, ROWS)))
    high = row.astype(jnp.bfloat16)
    low = (row - high.astype(jnp.float32)).astype(jnp.bfloat16)
    tail = jnp.broadcast_to(
        jnp.concatenate([high, low], axis=1).astype(jnp.float32), (PAD, 2 * ROWS)
    ).astype(jnp.bfloat16)
    near_rows, far_rows = scaled[c], scaled[1 - c]
    for h in range(Z):
        product = jnp.dot(near_rows, near[h], preferred_element_type=jnp.float32) + jnp.dot(
            far_rows, far[h], preferred_element_type=jnp.float32
        )
        partial[h, :ROWS, :] = product.astype(jnp.bfloat16)
        partial[h, ROWS:, :] = tail


def third_partials(place, received, hidden, gain, near, far):
    vmem = pl.BlockSpec(memory_space=pltpu.VMEM)
    width = hidden.shape[1]
    return pl.pallas_call(
        third_kernel,
        in_specs=[pl.BlockSpec(memory_space=pltpu.SMEM)] + [vmem] * 5,
        out_specs=(vmem, vmem),
        out_shape=(
            jax.ShapeDtypeStruct(hidden.shape, jnp.bfloat16),
            jax.ShapeDtypeStruct((Z, ROWS + PAD, 2 * HEAD), jnp.bfloat16),
        ),
        scratch_shapes=[pltpu.VMEM((2, ROWS, width // 2), jnp.bfloat16)],
        compiler_params=params(),
        name="third",
    )(place, received, hidden, gain, near, far)


def final_kernel(count, partial, bias, cosine, sine, index, out):
    total = partial[0, :ROWS, :].astype(jnp.float32)
    tail = partial[0, ROWS:, :].astype(jnp.float32)
    for h in range(1, Z):
        total = total + partial[h, :ROWS, :].astype(jnp.float32)
        tail = tail + partial[h, ROWS:, :].astype(jnp.float32)
    squares = tail[0:1, :ROWS] + tail[0:1, ROWS:]
    factor = lax.rsqrt(column_of(squares) / MODEL_WIDTH + 1e-06)
    keys = total[:, :HEAD] * factor + bias[:, :HEAD]
    values = total[:, HEAD:] * factor + bias[:, HEAD:]
    keys = rotated(keys, cosine[...], sine[...])
    rows = jnp.concatenate([keys, values], axis=1).astype(jnp.bfloat16)
    slot = lax.broadcasted_iota(jnp.int32, (ROWS, ROWS), 1)
    token = lax.broadcasted_iota(jnp.int32, (ROWS, ROWS), 0)
    chosen = (token == index[...]) & (slot < count[0])
    pick = jnp.where(chosen, 1.0, 0.0).astype(jnp.bfloat16)
    out[...] = lax.dot_general(
        pick, rows, (((0,), (0,)), ((), ())), preferred_element_type=jnp.float32
    ).astype(jnp.bfloat16)


def final(count, partial, bias, cosine, sine, index):
    vmem = pl.BlockSpec(memory_space=pltpu.VMEM)
    return pl.pallas_call(
        final_kernel,
        in_specs=[pl.BlockSpec(memory_space=pltpu.SMEM)] + [vmem] * 5,
        out_specs=vmem,
        out_shape=jax.ShapeDtypeStruct((ROWS, 2 * HEAD), jnp.bfloat16),
        compiler_params=params(),
        name="final",
    )(count, partial, bias, cosine, sine, index)


def swap(x, axis):
    return lax.ppermute(x, axis, [(0, 1), (1, 0)])


def along_z(x, distance):
    return lax.ppermute(x, "z", [(i, (i + distance) % Z) for i in range(Z)])


def after(x, *others):
    return lax.optimization_barrier((x, others))[0]


def step(pair):
    return [along_z(pair[0], 1), along_z(pair[1], -1)]


def local(
    hidden,
    query,
    fresh_key_value,
    cached_key_value,
    positions,
    out_weight,
    norm_gain,
    layer3_key_value_weight,
    layer3_key_value_bias,
    keep_index,
    keep_count,
):
    z, yl, c = lax.axis_index("z"), lax.axis_index("yl"), lax.axis_index("c")
    place = jnp.stack([z, yl, c]).astype(jnp.int32)

    cosine, sine = tables(positions, HEAD)
    rotated_query, kv = prepare(query, fresh_key_value, cached_key_value, cosine, sine)
    third_rows = weight_half(
        place, layer3_key_value_weight.reshape(Z, 2, MODEL_WIDTH // Z // 2, 2 * HEAD)
    )
    rotated_query = rotated_query.reshape(GROUP * ROWS, HEAD)
    across = swap(rotated_query, "yl")
    other_core = swap(rotated_query, "c")
    kv_1, across, third_rows = lax.optimization_barrier((step([kv, kv]), across, third_rows))
    near_query, far_query = [rotated_query, across], [other_core, swap(across, "c")]
    own_weight = after(out_weight, *kv_1)
    weights_1 = step([own_weight, own_weight])
    state = attend(
        1024,
        place,
        near_query + far_query,
        0,
        [kv, *kv_1],
        [(0, 0), (1, 1), (2, 2)],
        [[(0, 0, 0), (1, 1, -1)]],
    )
    kv_2 = list(after(step(kv_1), state))
    kv_3, weights_1, state = lax.optimization_barrier((step(kv_2), weights_1, state))
    third_near = lax.all_to_all(third_rows, HEAD_AXES, 0, 0, tiled=True)
    third_far = swap(third_near, "c")
    weights_2 = step(weights_1)
    kv_4 = along_z(kv_3[0], 1)
    kv_4, state = lax.optimization_barrier((kv_4, state))
    late = [kv_1[1], *kv_2, *kv_3, kv_4]
    late_cached = [(i, i) for i in range(1, 6)]
    late_fresh = [[(0, 0, 1), (1, 1, -2)], [(2, 2, 2), (3, 3, -3)], [(4, 4, 3), (5, 5, 4)]]
    offset = 2 * GROUP * ROWS
    send, send_lse = attend(
        512, place, far_query, 1, late, late_cached, late_fresh, state, offset, True
    )
    got, got_lse = swap(send, "c"), swap(send_lse, "c")
    near_query, _, weights_2 = lax.optimization_barrier((near_query, send_lse, weights_2))
    weights_3 = step(weights_2)
    own, own_lse = attend(
        1024, place, near_query, 0, late, late_cached, late_fresh, state, 0, True
    )
    own, own_lse = merge(own, own_lse, got, got_lse)
    got, got_lse = swap(own, "yl"), swap(own_lse, "yl")
    depth = out_weight.shape[0] // 2
    weights_4 = [along_z(weights_3[0][:depth], 1), along_z(weights_3[1][depth:], -1)]
    got_lse = after(got_lse, third_near, *weights_4)
    near = merge_last(own, own_lse, got, got_lse)
    far = swap(near, "c")
    weights = [out_weight, *weights_1, *weights_2, *weights_3, *weights_4]

    products = project(place, near, far, weights)
    products = products.reshape(4 * Z, *products.shape[2:])
    received = lax.all_to_all(products, ("yl", "c", "x", "yh"), 0, 0, tiled=True)
    received = received.reshape(4, Z, *received.shape[1:])

    layer2_out, partial = third_partials(
        place, received, hidden, norm_gain.reshape(1, -1), third_near, third_far
    )
    partial = lax.all_to_all(partial, HEAD_AXES, 0, 0, tiled=True)
    packed = final(
        keep_count,
        partial,
        layer3_key_value_bias.reshape(1, -1),
        cosine,
        sine,
        keep_index.reshape(1, -1),
    )
    return (layer2_out, packed)


def solution(mesh):
    split = Mesh(mesh.devices.reshape(Z, 2, 2, 4, 2), CTX_AXES + HEAD_AXES)
    placed = (
        P(CTX_AXES, HEAD_AXES),
        P(CTX_AXES, HEAD_AXES),
        P(None, CTX_AXES, HEAD_AXES),
        P(None, CTX_AXES, HEAD_AXES),
        P(None, CTX_AXES),
        P(HEAD_AXES, CTX_AXES),
        P(HEAD_AXES),
        P(None, HEAD_AXES),
        P(HEAD_AXES),
        P(CTX_AXES),
        P(CTX_AXES),
    )
    return jax.shard_map(
        local,
        mesh=split,
        in_specs=placed,
        out_specs=(P(CTX_AXES, HEAD_AXES), P(CTX_AXES, HEAD_AXES)),
        check_vma=False,
    )
```
